32 devices in a mesh: tok: 16 (over z, y, x), rep: 2 (over core).
Axes of the slice: x: 2, y: 2, z: 4, core: 2. Of those that a mesh axis runs over, the one named last changes fastest.
Arguments:
- long_target: bfloat16 [16, 512, 768], P('tok', 'rep'), may hold values from -6 to 6
- short_target: bfloat16 [16, 128, 768], P('tok', 'rep'), may hold values from -6 to 6
- long_memory: bfloat16 [16, 512, 768], P('tok', 'rep'), may hold values from -6 to 6
- short_memory: bfloat16 [16, 128, 768], P('tok', 'rep'), may hold values from -6 to 6
- long_cotangent: bfloat16 [16, 512, 768], P('tok', 'rep'), may hold values from -6 to 6
- short_cotangent: bfloat16 [16, 128, 768], P('tok', 'rep'), may hold values from -6 to 6
- long_target_len: int32 [16], P('tok'), may hold values from 64 to 512, as said below
- short_target_len: int32 [16], P('tok'), may hold values from 16 to 128, as said below
- long_memory_len: int32 [16], P('tok'), may hold values from 64 to 512, as said below
- short_memory_len: int32 [16], P('tok'), may hold values from 16 to 128, as said below
- self_inproj: bfloat16 [768, 2304], replicated, may hold values from -0.21875 to 0.21875
- self_qbias: bfloat16 [768], replicated, may hold values from -3 to 3
- self_vbias: bfloat16 [768], replicated, may hold values from -3 to 3
- self_outproj: bfloat16 [768, 768], replicated, may hold values from -1.75 to 1.75
- self_obias: bfloat16 [768], replicated, may hold values from -2 to 2
- first_gain: bfloat16 [768], replicated, may hold values from 0.5 to 1.5
- first_shift: bfloat16 [768], replicated, may hold values from -2 to 2
- cross_qproj: bfloat16 [768, 768], replicated, may hold values from -0.21875 to 0.21875
- cross_qbias: bfloat16 [768], replicated, may hold values from -3 to 3
- cross_kvproj: bfloat16 [768, 1536], replicated, may hold values from -0.21875 to 0.21875
- cross_vbias: bfloat16 [768], replicated, may hold values from -3 to 3
- cross_outproj: bfloat16 [768, 768], replicated, may hold values from -1.75 to 1.75
- cross_obias: bfloat16 [768], replicated, may hold values from -2 to 2
- second_gain: bfloat16 [768], replicated, may hold values from 0.5 to 1.5
- second_shift: bfloat16 [768], replicated, may hold values from -2 to 2
- expand_weight: bfloat16 [768, 3072], replicated, may hold values from -0.21875 to 0.21875
- expand_bias: bfloat16 [3072], replicated, may hold values from -2 to 2
- reduce_weight: bfloat16 [3072, 768], replicated, may hold values from -0.109375 to 0.109375
- reduce_bias: bfloat16 [768], replicated, may hold values from -2 to 2
- final_gain: bfloat16 [768], replicated, may hold values from 0.5 to 1.5
- final_shift: bfloat16 [768], replicated, may hold values from -2 to 2
Outputs:
- long_output: bfloat16 [16, 512, 768], P('tok', 'rep')
- short_output: bfloat16 [16, 128, 768], P('tok', 'rep')
- long_target_grad: bfloat16 [16, 512, 768], P('tok', 'rep')
- short_target_grad: bfloat16 [16, 128, 768], P('tok', 'rep')
- long_memory_grad: bfloat16 [16, 512, 768], P('tok', 'rep')
- short_memory_grad: bfloat16 [16, 128, 768], P('tok', 'rep')
- grad_self_inproj: float32 [768, 2304], P('tok')
- grad_self_qbias: float32 [768], P('tok')
- grad_self_vbias: float32 [768], P('tok')
- grad_self_outproj: float32 [768, 768], P('tok')
- grad_self_obias: float32 [768], P('tok')
- grad_first_gain: float32 [768], P('tok')
- grad_first_shift: float32 [768], P('tok')
- grad_cross_qproj: float32 [768, 768], P('tok')
- grad_cross_qbias: float32 [768], P('tok')
- grad_cross_kvproj: float32 [768, 1536], P('tok')
- grad_cross_vbias: float32 [768], P('tok')
- grad_cross_outproj: float32 [768, 768], P('tok')
- grad_cross_obias: float32 [768], P('tok')
- grad_second_gain: float32 [768], P('tok')
- grad_second_shift: float32 [768], P('tok')
- grad_expand_weight: float32 [768, 3072], P('tok')
- grad_expand_bias: float32 [3072], P('tok')
- grad_reduce_weight: float32 [3072, 768], P('tok')
- grad_reduce_bias: float32 [768], P('tok')
- grad_final_gain: float32 [768], P('tok')
- grad_final_shift: float32 [768], P('tok')
- statistics: float32 [4], replicated
The draws below stay inside these ranges and needn't reach their ends.
Inputs may be any that keep to these rules, and one draw needn't show every extreme that they name: `long_target_len`: valid target positions of each long row; some row has exactly 512. `short_target_len`: valid target positions of each short row; some row has exactly 128. `long_memory_len`: valid memory positions of each long row; some row has exactly 512. `short_memory_len`: valid memory positions of each short row; some row has exactly 128.
All inputs are finite; a program needn't handle non-finite values.
Results may differ from the reference program's by a relative error of at most 0.025.
Values may be sent and summed in bfloat16 or wider, within the bound.
No kernel may reach another device: no remote copies, remote signals or barrier semaphores. Data moves between devices by JAX's collectives and lax.ppermute only.
A program may use at most 192 MiB of HBM per device.

```python
import math
import jax
import jax.numpy as jnp
from jax import lax

D = 768
HEADS = 12
HEAD_DIM = 64
FF = 3072
LA = 512
LB = 128
ROWS_A = 16
ROWS_B = 16


def draw_lengths(key, row_count, seq_len):
    first_key, second_key = jax.random.split(key)
    drawn = jax.random.randint(first_key, (row_count,), seq_len // 8, seq_len + 1)
    chosen = jax.random.randint(second_key, (), 0, row_count)
    return jnp.where(jnp.arange(row_count) == chosen, seq_len, drawn).astype(jnp.int32)


def draw_long_target_len(key, part):
    return draw_lengths(jax.random.fold_in(key, 11), ROWS_A, LA)


def draw_short_target_len(key, part):
    return draw_lengths(jax.random.fold_in(key, 23), ROWS_B, LB)


def draw_long_memory_len(key, part):
    return draw_lengths(jax.random.fold_in(key, 37), ROWS_A, LA)


def draw_short_memory_len(key, part):
    return draw_lengths(jax.random.fold_in(key, 41), ROWS_B, LB)


def steps_of(rng, dims, shards, least, top_value):
    loudness, own = 1.0, jax.random.fold_in(rng, 6)
    for axis_at, shards_of in shards:
        draws = jnp.exp(jax.random.uniform(jax.random.fold_in(own, axis_at), (shards_of,), jnp.float32, least / len(shards), top_value / len(shards)))
        loudness = loudness * jnp.repeat(draws, dims[axis_at] // shards_of).reshape([-1 if axis == axis_at else 1 for axis in range(len(dims))])
    return loudness


def noise(stream_key, shape, scale, bound, cuts=(), held_as=jnp.bfloat16):
    array = scale * jax.random.normal(stream_key, shape, jnp.float32)
    if cuts:
        array = array * steps_of(stream_key, shape, cuts, -0.22, 0.18)
    return jnp.clip(array, -bound, bound).astype(held_as)


def setup_inputs(seed: int = 0) -> dict:
    arg_keys = jax.random.split(jax.random.key(seed), 32)
    return {
        "long_target": noise(arg_keys[0], (ROWS_A, LA, D), 1.0, 6.0, ((0, 16), (1, 2))),
        "short_target": noise(arg_keys[1], (ROWS_B, LB, D), 1.0, 6.0, ((0, 16), (1, 2))),
        "long_memory": noise(arg_keys[2], (ROWS_A, LA, D), 1.0, 6.0, ((0, 16), (1, 2))),
        "short_memory": noise(arg_keys[3], (ROWS_B, LB, D), 1.0, 6.0, ((0, 16), (1, 2))),
        "long_cotangent": noise(arg_keys[4], (ROWS_A, LA, D), 1.0, 6.0, ((0, 16), (1, 2))),
        "short_cotangent": noise(arg_keys[5], (ROWS_B, LB, D), 1.0, 6.0, ((0, 16), (1, 2))),
        "long_target_len": draw_long_target_len(jax.random.fold_in(arg_keys[31], 71), 0),
        "short_target_len": draw_short_target_len(jax.random.fold_in(arg_keys[31], 71), 0),
        "long_memory_len": draw_long_memory_len(jax.random.fold_in(arg_keys[31], 71), 0),
        "short_memory_len": draw_short_memory_len(jax.random.fold_in(arg_keys[31], 71), 0),
        "self_inproj": noise(arg_keys[10], (D, 3 * D), D ** -0.5, 0.21875),
        "self_qbias": noise(arg_keys[11], (D,), 0.5, 3.0),
        "self_vbias": noise(arg_keys[12], (D,), 0.5, 3.0),
        "self_outproj": noise(arg_keys[13], (D, D), (D // 64) ** -0.5, 1.75),
        "self_obias": noise(arg_keys[14], (D,), 0.3, 2.0),
        "first_gain": jnp.clip(1.0 + 0.1 * jax.random.normal(arg_keys[15], (D,), jnp.float32), 0.5, 1.5).astype(jnp.bfloat16),
        "first_shift": noise(arg_keys[16], (D,), 0.3, 2.0),
        "cross_qproj": noise(arg_keys[17], (D, D), D ** -0.5, 0.21875),
        "cross_qbias": noise(arg_keys[18], (D,), 0.5, 3.0),
        "cross_kvproj": noise(arg_keys[19], (D, 2 * D), D ** -0.5, 0.21875),
        "cross_vbias": noise(arg_keys[20], (D,), 0.5, 3.0),
        "cross_outproj": noise(arg_keys[21], (D, D), (D // 64) ** -0.5, 1.75),
        "cross_obias": noise(arg_keys[22], (D,), 0.3, 2.0),
        "second_gain": jnp.clip(1.0 + 0.1 * jax.random.normal(arg_keys[23], (D,), jnp.float32), 0.5, 1.5).astype(jnp.bfloat16),
        "second_shift": noise(arg_keys[24], (D,), 0.3, 2.0),
        "expand_weight": noise(arg_keys[25], (D, FF), D ** -0.5, 0.21875),
        "expand_bias": noise(arg_keys[26], (FF,), 0.3, 2.0),
        "reduce_weight": noise(arg_keys[27], (FF, D), FF ** -0.5, 0.109375),
        "reduce_bias": noise(arg_keys[28], (D,), 0.3, 2.0),
        "final_gain": jnp.clip(1.0 + 0.1 * jax.random.normal(arg_keys[29], (D,), jnp.float32), 0.5, 1.5).astype(jnp.bfloat16),
        "final_shift": noise(arg_keys[30], (D,), 0.3, 2.0),
    }


@jax.custom_vjp
def low(v):
    return lax.optimization_barrier(v.astype(jnp.bfloat16)).astype(jnp.float32)

@jax.custom_vjp
def low_back(v):
    return v

def low_keep(v):
    return (low(v), None)

def low_pass(kept, grad):
    return (grad,)

def back_keep(v):
    return (v, None)

def back_low(kept, grad):
    return (low(grad),)
low.defvjp(low_keep, low_pass)
low_back.defvjp(back_keep, back_low)
epsilon = 1e-05
highest = lax.Precision.HIGHEST
masked = -1e+30

def product(equation, operand, another):
    return jnp.einsum(equation, operand, another, precision=highest, preferred_element_type=jnp.float32)

def normalize(tensor, gain_vec, shift_vec):
    centre = tensor - lax.optimization_barrier(jnp.mean(tensor, axis=-1, keepdims=True))
    spread = lax.optimization_barrier(jnp.mean(centre * centre, axis=-1, keepdims=True))
    return centre * lax.rsqrt(spread + epsilon) * gain_vec + shift_vec

def split_heads(tensor):
    row_count, seq_len, _ = tensor.shape
    return tensor.reshape(row_count, seq_len, HEADS, HEAD_DIM).transpose(0, 2, 1, 3)

def merge_heads(tensor):
    row_count, head_count, seq_len, _ = tensor.shape
    return tensor.transpose(0, 2, 1, 3).reshape(row_count, seq_len, head_count * HEAD_DIM)

def attention(queries, key_vecs, values, query_len, key_len, causal):
    seq_len = queries.shape[2]
    positions = jnp.arange(seq_len)
    scaling = 1.0 / math.sqrt(HEAD_DIM)
    scores = low_back(product('rhqd,rhkd->rhqk', queries, key_vecs) * scaling)
    allowed = positions[None, None, None, :] < key_len[:, None, None, None]
    if causal:
        allowed = allowed & (positions[None, :] <= positions[:, None])[None, None]
    weights = jax.nn.softmax(jnp.where(allowed, scores, masked), axis=-1)
    context = product('rhqk,rhkd->rhqd', low(weights), values)
    live_rows = positions[None, None, :, None] < query_len[:, None, None, None]
    return jnp.where(live_rows, context, 0.0)

def forward(params, target, memory, target_len, memory_len):
    self_inproj, self_qbias, self_vbias, self_outproj, self_obias, first_gain, first_shift, cross_qproj, cross_qbias, cross_kvproj, cross_vbias, cross_outproj, cross_obias, second_gain, second_shift, expand_weight, expand_bias, reduce_weight, reduce_bias, final_gain, final_shift = params
    features = target.shape[-1]
    projected = product('rsd,de->rse', low(target), self_inproj)
    queries = low(low_back(projected[..., :features] + self_qbias))
    key_vecs = low(low_back(projected[..., features:2 * features]))
    values = low(low_back(projected[..., 2 * features:] + self_vbias))
    context = attention(split_heads(queries), split_heads(key_vecs), split_heads(values), target_len, target_len, True)
    context = low(low_back(merge_heads(context)))
    self_branch = low_back(product('rsd,de->rse', context, self_outproj) + self_obias)
    after_self = normalize(target + self_branch, first_gain, first_shift)
    cross_queries = low(low_back(product('rsd,de->rse', low(after_self), cross_qproj) + cross_qbias))
    memory_proj = product('rsd,de->rse', low(memory), cross_kvproj)
    cross_keys = low(low_back(memory_proj[..., :features]))
    cross_values = low(low_back(memory_proj[..., features:] + cross_vbias))
    mixed = attention(split_heads(cross_queries), split_heads(cross_keys), split_heads(cross_values), target_len, memory_len, False)
    mixed = low(low_back(merge_heads(mixed)))
    cross_branch = low_back(product('rsd,de->rse', mixed, cross_outproj) + cross_obias)
    after_cross = normalize(after_self + cross_branch, second_gain, second_shift)
    inner_act = low_back(product('rsd,df->rsf', low(after_cross), expand_weight) + expand_bias)
    hidden = low(jax.nn.gelu(inner_act, approximate=False))
    ffn_branch = low_back(product('rsf,fd->rsd', hidden, reduce_weight) + reduce_bias)
    final = normalize(after_cross + ffn_branch, final_gain, final_shift)
    return (final, (self_branch, cross_branch, ffn_branch))

def add_arrays(first_arr, second_arr):
    return first_arr + second_arr

def run_bucket(params, target, memory, cotangent, target_len, memory_len):
    row_count, seq_len, features = target.shape
    group_rows = math.gcd(row_count, max(1, 4096 // seq_len))
    step_count = row_count // group_rows

    def regroup(tensor):
        return tensor.reshape((step_count, group_rows) + tensor.shape[1:])

    def scan_step(carried, inputs):
        gradients, square_sums = carried
        tgt_rows, mem_rows, cot_rows, tgt_len, mem_len = inputs
        live_mask = (jnp.arange(seq_len)[None, :] < tgt_len[:, None]).astype(jnp.float32)[..., None]

        def forward_of(param_set, tgt_value, mem_value):
            return forward(param_set, tgt_value, mem_value, tgt_len, mem_len)
        output, pullback, branches = jax.vjp(forward_of, params, tgt_rows.astype(jnp.float32), mem_rows.astype(jnp.float32), has_aux=True)
        grad_params, grad_target, grad_memory = pullback(cot_rows.astype(jnp.float32) * live_mask)
        gradients = jax.tree.map(add_arrays, gradients, grad_params)
        squares = jnp.stack([jnp.sum(live_mask * output * output), jnp.sum(live_mask * branches[0] * branches[0]), jnp.sum(live_mask * branches[1] * branches[1]), jnp.sum(live_mask * branches[2] * branches[2])])
        return ((gradients, square_sums + squares), (output.astype(jnp.bfloat16), grad_target.astype(jnp.bfloat16), grad_memory.astype(jnp.bfloat16)))
    initial = (jax.tree.map(jnp.zeros_like, params), jnp.zeros((4,), jnp.float32))
    (gradients, square_sums), (outputs, target_grads, memory_grads) = lax.scan(scan_step, initial, (regroup(target), regroup(memory), regroup(cotangent), regroup(target_len), regroup(memory_len)))
    shape_full = (row_count, seq_len, features)
    return (outputs.reshape(shape_full), target_grads.reshape(shape_full), memory_grads.reshape(shape_full), gradients, square_sums)

def reference(long_target, short_target, long_memory, short_memory, long_cotangent, short_cotangent, long_target_len, short_target_len, long_memory_len, short_memory_len, self_inproj, self_qbias, self_vbias, self_outproj, self_obias, first_gain, first_shift, cross_qproj, cross_qbias, cross_kvproj, cross_vbias, cross_outproj, cross_obias, second_gain, second_shift, expand_weight, expand_bias, reduce_weight, reduce_bias, final_gain, final_shift):
    params = tuple((weight.astype(jnp.float32) for weight in (self_inproj, self_qbias, self_vbias, self_outproj, self_obias, first_gain, first_shift, cross_qproj, cross_qbias, cross_kvproj, cross_vbias, cross_outproj, cross_obias, second_gain, second_shift, expand_weight, expand_bias, reduce_weight, reduce_bias, final_gain, final_shift)))
    long_res = run_bucket(params, long_target, long_memory, long_cotangent, long_target_len, long_memory_len)
    short_res = run_bucket(params, short_target, short_memory, short_cotangent, short_target_len, short_memory_len)
    gradients = jax.tree.map(add_arrays, long_res[3], short_res[3])
    token_count = (jnp.sum(long_target_len) + jnp.sum(short_target_len)).astype(jnp.float32) * D
    statistics = jnp.sqrt((long_res[4] + short_res[4]) / token_count)
    return (long_res[0], short_res[0], long_res[1], short_res[1], long_res[2], short_res[2], gradients[0], gradients[1], gradients[2], gradients[3], gradients[4], gradients[5], gradients[6], gradients[7], gradients[8], gradients[9], gradients[10], gradients[11], gradients[12], gradients[13], gradients[14], gradients[15], gradients[16], gradients[17], gradients[18], gradients[19], gradients[20], statistics)
```

```python
import math

import jax
import jax.numpy as jnp
from jax import lax
from jax.experimental import pallas as pl
from jax.experimental.pallas import tpu as pltpu
from jax.sharding import PartitionSpec as P

HEADS = 12
HEAD_DIM = 64
LANES = 128
EPS = 1e-05
MASKED = -1e30
LIMIT = 62 * 1024 * 1024

f32 = jnp.float32
bf16 = jnp.bfloat16

ANY = pl.BlockSpec(memory_space=pl.ANY)
VMEM = pl.BlockSpec(memory_space=pltpu.VMEM)
SMEM = pl.BlockSpec(memory_space=pltpu.SMEM)


def dot(a, b):
    return lax.dot_general(a, b, (((1,), (0,)), ((), ())), preferred_element_type=f32)


def dot_nt(a, b):
    return lax.dot_general(a, b, (((1,), (1,)), ((), ())), preferred_element_type=f32)


def dot_tn(a, b):
    return lax.dot_general(a, b, (((0,), (0,)), ((), ())), preferred_element_type=f32)


def shape(dims, dtype):
    return jax.ShapeDtypeStruct(dims, dtype)


def whole(ref):
    return ref


def columns(start, count):
    return lambda ref: ref.at[:, pl.ds(start, count)]


def rows(start, count):
    return lambda ref: ref.at[pl.ds(start, count)]


def first(ref):
    return ref.at[0]


def load(array):
    return Load(array.shape, array.dtype, [(array, whole, 0)])


class Load:
    def __init__(self, dims, dtype, pieces):
        self.dims = dims
        self.dtype = dtype
        self.pieces = pieces


class Stage:
    def __init__(self, sems):
        self.sems = sems
        self.count = 0
        self.refs = {}
        self.loads = {}
        self.targets = {}
        self.sent = []

    def start(self, source, target):
        copy = pltpu.make_async_copy(source, target, self.sems.at[self.count])
        self.count += 1
        copy.start()
        return copy

    def __getitem__(self, name):
        for copy in self.loads.pop(name, ()):
            copy.wait()
        return self.refs[name]

    def __setitem__(self, name, value):
        self.refs[name][...] = value
        self.put(name)

    def put(self, name):
        if name in self.targets:
            self.sent.append(self.start(self.refs[name], self.targets.pop(name)))

    def finish(self):
        for name in list(self.targets):
            self.put(name)
        for name in list(self.loads):
            self[name]
        for copy in self.sent:
            copy.wait()


TIMES = {
    "forward": 27,
    "expand_grad": 7,
    "reduce_grad": 8,
    "cross_back": 16,
    "self_back": 8,
    "cross_grads": 10,
    "self_grads": 9,
    "add_step": 3,
}
SCALE = 0.25


def cost(name):
    return pl.CostEstimate(flops=int(TIMES[name] * SCALE * 1.15e9), bytes_accessed=1024, transcendentals=0)


def staged(name, body, loads, direct, outs, scratch):
    arrays = [piece[0] for value in loads.values() for piece in value.pieces]
    arrays += [value for value, unused in direct.values()]
    specs = [ANY] * sum(len(value.pieces) for value in loads.values())
    specs += [space for unused, space in direct.values()]
    buffers = {key: pltpu.VMEM(value.dims, value.dtype) for key, value in loads.items()}
    buffers.update({key: pltpu.VMEM(value.shape, value.dtype) for key, value in outs.items()})
    buffers.update({key: pltpu.VMEM(value.shape, value.dtype) for key, value in scratch.items()})
    copies = sum(len(value.pieces) for value in loads.values()) + len(outs)

    def kernel(*refs):
        refs = list(refs)
        stage = Stage(refs[-1])
        sources = {key: [refs.pop(0) for unused in value.pieces] for key, value in loads.items()}
        for key in direct:
            stage.refs[key] = refs.pop(0)
        for key in outs:
            stage.targets[key] = refs.pop(0)
        for key in buffers:
            stage.refs[key] = refs.pop(0)
        for key, value in loads.items():
            stage.loads[key] = []
            for ref, (unused, pick, start) in zip(sources[key], value.pieces):
                source = pick(ref)
                target = stage.refs[key]
                if source.shape != target.shape:
                    target = target.at[pl.ds(start, source.shape[0])]
                stage.loads[key].append(stage.start(source, target))
        body(stage)
        stage.finish()

    results = pl.pallas_call(
        kernel,
        name=name,
        out_shape=list(outs.values()),
        in_specs=specs,
        out_specs=[ANY] * len(outs),
        scratch_shapes=[*buffers.values(), pltpu.SemaphoreType.DMA((copies,))],
        compiler_params=pltpu.CompilerParams(vmem_limit_bytes=LIMIT),
        cost_estimate=cost(name),
    )(*arrays)
    return dict(zip(outs, results))


def row(ref):
    return ref[...].astype(f32).reshape(1, ref.shape[0])


def lane_heads():
    lane = lax.broadcasted_iota(jnp.int32, (1, LANES), 1)
    return (lane < HEAD_DIM, lane >= HEAD_DIM)


def only(mask, value):
    return jnp.where(mask, value, jnp.zeros_like(value))


def both_heads(heads, value):
    return jnp.concatenate([only(heads[0], value), only(heads[1], value)], axis=0)


def rejoin(heads, value):
    rows = value.shape[0] // 2
    return jnp.where(heads[0], value[:rows], value[rows:])


class Sizes:
    def __init__(self, long_local, short_local, width):
        self.a = long_local
        self.b = short_local
        self.own = long_local + short_local
        self.full = 2 * self.own
        self.width = width
        self.pairs = width // LANES
        self.buckets = ((0, self.a, 0), (self.a, self.b, 2 * self.a))

    def own_pieces(self, long_part, short_part, other_long=None, other_short=None):
        pieces = [(long_part, first, 0), (short_part, first, self.a)]
        if other_long is not None:
            pieces += [(other_long, first, self.own), (other_short, first, self.own + self.a)]
        return pieces

    def full_pieces(self, long_part, short_part, other_long, other_short):
        return [
            (long_part, first, 0),
            (other_long, first, self.a),
            (short_part, first, 2 * self.a),
            (other_short, first, 2 * self.a + self.b),
        ]


def key_positions(rows, core):
    at = lax.broadcasted_iota(jnp.int32, (2 * rows, 1), 0)
    return jnp.where(at < rows, core * rows + at, (1 - core) * rows + at - rows)


def query_positions(rows, core):
    at = lax.broadcasted_iota(jnp.int32, (1, 2 * rows), 1)
    return core * rows + jnp.where(at < rows, at, at - rows)


def softmax_columns(scores):
    raised = jnp.exp(scores - jnp.max(scores, axis=0, keepdims=True))
    return (raised * (1.0 / jnp.sum(raised, axis=0, keepdims=True))).astype(bf16)


def attend(size, q, k, v, bias, probs, out, live):
    heads = lane_heads()
    for start, rows, kstart in size.buckets:
        which = 0 if start == 0 else 1
        weights = []
        for pair in range(size.pairs):
            lanes = slice(pair * LANES, (pair + 1) * LANES)
            queries = both_heads(heads, q[start : start + rows, lanes])
            scores = dot_nt(k[kstart : kstart + 2 * rows, lanes], queries) + bias[which][...]
            weights.append(softmax_columns(scores))
            if rows >= LANES:
                finish_pair(size, v, probs, out, live, which, pair, weights.pop(), heads)
        for pair, value in enumerate(weights):
            finish_pair(size, v, probs, out, live, which, pair, value, heads)


def finish_pair(size, v, probs, out, live, which, pair, weights, heads):
    start, rows, kstart = size.buckets[which]
    lanes = slice(pair * LANES, (pair + 1) * LANES)
    probs[which][pair] = weights
    values = v[kstart : kstart + 2 * rows, lanes]
    context = by_query(heads, weights, values)
    out[start : start + rows, lanes] = jnp.where(live[which], context, 0.0).astype(bf16)


def by_query(heads, across, keyed):
    rows = across.shape[1] // 2
    if rows < LANES:
        return rejoin(heads, dot_tn(across, keyed))
    feature = lax.broadcasted_iota(jnp.int32, (LANES, 1), 0)
    turned = dot(keyed.T, across)
    return jnp.where(feature < HEAD_DIM, turned[:, :rows], turned[:, rows:]).T


def head_sums(product):
    rows = product.shape[0]
    if rows < LANES:
        turned = jnp.concatenate([product, product], axis=0).T
        lane = lax.broadcasted_iota(jnp.int32, (1, LANES), 1)
        low = jnp.sum(turned[:HEAD_DIM], axis=0, keepdims=True)
        high = jnp.sum(turned[HEAD_DIM:], axis=0, keepdims=True)
        return jnp.where(lane < rows, low, high)
    turned = product.T
    low = jnp.sum(turned[:HEAD_DIM], axis=0, keepdims=True)
    high = jnp.sum(turned[HEAD_DIM:], axis=0, keepdims=True)
    return jnp.concatenate([low, high], axis=1)


def attend_back(size, q, k, v, probs, context, grad, dq, dk, dv, scaling):
    heads = lane_heads()
    for which, (start, rows, kstart) in enumerate(size.buckets):
        held = []

        def finish(pair, weights, grads, dscores):
            lanes = slice(pair * LANES, (pair + 1) * LANES)
            at = slice(start, start + rows)
            keys = slice(kstart, kstart + 2 * rows)
            dk[keys, lanes] = dot(dscores, both_heads(heads, q[at, lanes])).astype(bf16)
            dv[keys, lanes] = dot(weights, grads).astype(bf16)
            dq[at, lanes] = (by_query(heads, dscores, k[keys, lanes]) * scaling).astype(bf16)

        for pair in range(size.pairs):
            lanes = slice(pair * LANES, (pair + 1) * LANES)
            at = slice(start, start + rows)
            weights = probs[which][pair]
            grads = grad[at, lanes]
            centred = head_sums(grads.astype(f32) * context[at, lanes].astype(f32))
            grads = both_heads(heads, grads)
            dprobs = dot_nt(v[kstart : kstart + 2 * rows, lanes], grads)
            dscores = (weights.astype(f32) * (dprobs - centred)).astype(bf16)
            if rows >= LANES:
                finish(pair, weights, grads, dscores)
            else:
                held.append((pair, weights, grads, dscores))
        for item in held:
            finish(*item)


def norm_parts(tensor):
    centre = tensor - jnp.mean(tensor, axis=-1, keepdims=True)
    rstd = lax.rsqrt(jnp.mean(centre * centre, axis=-1, keepdims=True) + EPS)
    return centre * rstd, rstd


def norm_back(normed, rstd, gain, gradient):
    scaled = gradient * gain
    inner = scaled - jnp.mean(scaled, axis=-1, keepdims=True)
    inner = inner - normed * jnp.mean(scaled * normed, axis=-1, keepdims=True)
    return inner * rstd


def column_sum(tensor):
    return jnp.sum(tensor.astype(f32), axis=0, keepdims=True)


def live_column(rows, core, length):
    return core * rows + lax.broadcasted_iota(jnp.int32, (rows, 1), 0) < length


def forward_body(size, hidden_width, scaling, g):
    core = lax.axis_index("rep")
    a, b, own, width = size.a, size.b, size.own, size.width
    target_len = (g["target_len_a"][0], g["target_len_b"][0])
    memory_len = (g["memory_len_a"][0], g["memory_len_b"][0])
    live = (live_column(a, core, target_len[0]), live_column(b, core, target_len[1]))
    live_all = jnp.concatenate(live, axis=0)
    bias = (g["bias_a"], g["bias_b"])
    context, mixed, low1 = (columns_of(g["ship3"], at * width, width) for at in range(3))
    low2, inner_send = columns_of(g["ship1"], 0, width), columns_of(g["ship1"], width, hidden_width // 2)
    hidden, ffn_send = columns_of(g["ship2"], 0, hidden_width), columns_of(g["ship2"], hidden_width, width // 2)
    for which, rows in enumerate((a, b)):
        at = key_positions(rows, core)
        allowed = (at < target_len[which]) & (at <= query_positions(rows, core))
        bias[which][...] = jnp.where(allowed, 0.0, MASKED)
    xo = g["xo"]
    g["q"] = ((dot(xo[...], g["w_q"][...]) + row(g["qbias"])).astype(bf16) * scaling).astype(bf16)
    xf = g["xf"]
    g["k"] = dot(xf[...], g["w_k"][...]).astype(bf16)
    g["v"] = (dot(xf[...], g["w_v"][...]) + row(g["vbias"])).astype(bf16)
    attend(size, g["q"], g["k"], g["v"], bias, (g["ps_a"], g["ps_b"]), context, live)
    for name in ("ps_a", "ps_b"):
        g.put(name)
    mf, w_ckv = g["mf"], g["w_ckv"]
    g["ck"] = dot(mf[...], w_ckv[:, :width]).astype(bf16)
    g["cv"] = (dot(mf[...], w_ckv[:, width:]) + row(g["cvbias"])).astype(bf16)

    def squares(tensor):
        kept = jnp.where(live_all, tensor * tensor, 0.0)
        return jnp.sum(jnp.sum(kept, axis=0, keepdims=True), axis=1, keepdims=True)

    branch = g["branch"]
    self_branch = dot(context[...], g["w_out"][...]) + row(g["obias"])
    square_self = squares(self_branch)
    normed, rstd = norm_parts(xo[...].astype(f32) + self_branch)
    g["n1"] = normed
    g["r1"] = rstd
    after_self = normed * row(g["gain1"]) + row(g["shift1"])
    low1[...] = after_self.astype(bf16)
    branch[...] = after_self
    query = dot(low1[...], g["w_cq"][...]) + row(g["cqbias"])
    g["cq"] = (query.astype(bf16) * scaling).astype(bf16)
    for which, rows in enumerate((a, b)):
        allowed = key_positions(rows, core) < memory_len[which]
        bias[which][...] = jnp.broadcast_to(jnp.where(allowed, 0.0, MASKED), bias[which].shape)
    attend(size, g["cq"], g["ck"], g["cv"], bias, (g["pc_a"], g["pc_b"]), mixed, live)
    for name in ("pc_a", "pc_b", "ship3"):
        g.put(name)
    cross_branch = dot(mixed[...], g["w_cout"][...]) + row(g["cobias"])
    square_cross = squares(cross_branch)
    normed, rstd = norm_parts(branch[...] + cross_branch)
    g["n2"] = normed
    g["r2"] = rstd
    after_cross = normed * row(g["gain2"]) + row(g["shift2"])
    low2[...] = after_cross.astype(bf16)
    branch[...] = after_cross
    third, slope = g["third"], g["slope"]
    w_exp, w_red = g["w_exp"], g["w_red"]
    eb = row(g["ebias"])
    total = None
    for step in range(hidden_width // width):
        cols = slice(step * width, (step + 1) * width)
        act = dot(low2[...], w_exp[:, cols]) + eb[:, cols]
        phi = 0.5 * (1.0 + lax.erf(act * (1.0 / math.sqrt(2.0))))
        hidden[:, cols] = (act * phi).astype(bf16)
        density = jnp.exp(-0.5 * act * act) * (1.0 / math.sqrt(2.0 * math.pi))
        slope[:, cols] = (phi + act * density).astype(bf16)
        part = dot(hidden[:, cols], w_red[cols, :])
        if step == 0:
            third[...] = part
        else:
            third[...] += part
    ffn_branch = third[...] + row(g["rbias"])
    square_ffn = squares(ffn_branch)
    normed, rstd = norm_parts(branch[...] + ffn_branch)
    gain = row(g["gain3"])
    final = normed * gain + row(g["shift3"])
    square_final = squares(final)
    low = final.astype(bf16)
    g["out_a"] = low[:a][None]
    g["out_b"] = low[a:][None]
    gradient = jnp.where(live_all, g["cot"][...].astype(f32), 0.0)
    d_third = norm_back(normed, rstd, gain, gradient)
    g["third"] = d_third
    d_ffn = d_third.astype(bf16)
    dffn = g["dffn"]
    dffn[...] = d_ffn
    half = width // 2
    g["ffn_keep"] = dffn[:, half_of(core, half)]
    ffn_send[...] = dffn[:, half_of(1 - core, half)]
    g.put("ship2")
    sums = g["sums"]
    sums[0:1] = column_sum(gradient * normed)
    sums[1:2] = column_sum(gradient)
    sums[2:3] = column_sum(d_ffn)
    count = jnp.sum(jnp.where(live_all, 1.0, 0.0), axis=0, keepdims=True)
    for at, value in enumerate((square_final, square_self, square_cross, square_ffn, count)):
        sums[3 + at : 4 + at] = jnp.broadcast_to(value, (1, width))
    g.put("sums")
    inner = g["inner"]
    half = hidden_width // 2
    for side, target in ((1 - core, inner_send), (core, g["inner_keep"])):
        for start in range(0, half, width):
            cols = pl.ds(pl.multiple_of(side * half + start, LANES), width)
            grad = dot_nt(dffn[...], w_red[cols, :]) * slope[:, cols].astype(f32)
            low = grad.astype(bf16)
            inner[:, cols] = low
            target[:, pl.ds(start, width)] = low
            g["inner_sum"][:, cols] = column_sum(low)
        g.put("ship1")
    g.put("inner")


def columns_of(ref, start, count):
    return ref.at[:, pl.ds(start, count)]


def half_of(core, half):
    return pl.ds(pl.multiple_of(core * half, LANES), half)


def run_forward(size, hidden_width, scaling, lengths, own, other, cots, weights, vectors):
    a, b, n, t, w, h = size.a, size.b, size.own, size.full, size.width, hidden_width
    w_in, w_out, w_cq, w_ckv, w_cout, w_exp, w_red = weights
    loads = {
        "xo": Load((n, w), bf16, size.own_pieces(own[0], own[1])),
        "w_q": Load((w, w), bf16, [(w_in, columns(0, w), 0)]),
        "xf": Load((t, w), bf16, size.full_pieces(own[0], own[1], other[0], other[1])),
        "w_k": Load((w, w), bf16, [(w_in, columns(w, w), 0)]),
        "w_v": Load((w, w), bf16, [(w_in, columns(2 * w, w), 0)]),
        "mf": Load((t, w), bf16, size.full_pieces(own[2], own[3], other[2], other[3])),
        "w_ckv": load(w_ckv),
        "w_out": load(w_out),
        "w_cq": load(w_cq),
        "w_cout": load(w_cout),
        "w_exp": load(w_exp),
        "w_red": load(w_red),
        "cot": Load((n, w), bf16, size.own_pieces(cots[0], cots[1])),
    }
    names = ("qbias", "vbias", "obias", "gain1", "shift1", "cqbias", "cvbias", "cobias", "gain2", "shift2")
    names += ("ebias", "rbias", "gain3", "shift3")
    direct = dict(zip(("target_len_a", "target_len_b", "memory_len_a", "memory_len_b"), ((v, SMEM) for v in lengths)))
    direct.update(zip(names, ((v, VMEM) for v in vectors)))
    square = shape((n, w), bf16)
    keys = shape((t, w), bf16)
    outs = {
        "out_a": shape((1, a, w), bf16),
        "out_b": shape((1, b, w), bf16),
        "q": square,
        "k": keys,
        "v": keys,
        "cq": square,
        "ck": keys,
        "cv": keys,
        "ps_a": shape((size.pairs, 2 * a, 2 * a), bf16),
        "ps_b": shape((size.pairs, 2 * b, 2 * b), bf16),
        "pc_a": shape((size.pairs, 2 * a, 2 * a), bf16),
        "pc_b": shape((size.pairs, 2 * b, 2 * b), bf16),
        "ship1": shape((n, w + h // 2), bf16),
        "ship2": shape((n, h + w // 2), bf16),
        "ship3": shape((n, 3 * w), bf16),
        "n1": shape((n, w), f32),
        "r1": shape((n, 1), f32),
        "n2": shape((n, w), f32),
        "r2": shape((n, 1), f32),
        "third": shape((n, w), f32),
        "ffn_keep": shape((n, w // 2), bf16),
        "sums": shape((8, w), f32),
        "inner": shape((n, h), bf16),
        "inner_keep": shape((n, h // 2), bf16),
        "inner_sum": shape((1, h), f32),
    }
    scratch = {
        "bias_a": shape((2 * a, 2 * a), f32),
        "bias_b": shape((2 * b, 2 * b), f32),
        "branch": shape((n, w), f32),
        "slope": shape((n, h), bf16),
        "dffn": square,
    }
    return staged(
        "forward",
        lambda g: forward_body(size, hidden_width, scaling, g),
        loads,
        direct,
        outs,
        scratch,
    )


def split_partial(size, core, dk, dv, keep, send):
    a, b = size.a, size.b
    moves = ((0, a, a), (a, 0, a), (2 * a, 2 * a + b, b), (2 * a + b, 2 * a, b))
    for here, (stay, leave) in ((0, (dk, dv)), (1, (dv, dk))):

        @pl.when(core == here)
        def unused(stay=stay, leave=leave):
            keep[...] = stay[...]
            for target, source, rows in moves:
                send[pl.ds(target, rows)] = leave[pl.ds(source, rows)]


def through_norm(size, g, gradient, normed, rstd, gain, w_out, sums, back):
    normed = g[normed][...]
    d_sum = norm_back(normed, g[rstd][...], row(g[gain]), gradient)
    sums[0:1] = column_sum(gradient * normed)
    sums[1:2] = column_sum(gradient)
    low = d_sum.astype(bf16)
    sums[2:3] = column_sum(low)
    g["branch"][...] = low
    back[...] = dot_nt(low, g[w_out][...]).astype(bf16)
    return d_sum


def send_halves(core, value, keep, send, at, half):
    keep[:, at * half : (at + 1) * half] = value[:, half_of(core, half)]
    send[:, at * half : (at + 1) * half] = value[:, half_of(1 - core, half)]


def cross_body(size, scaling, g):
    core = lax.axis_index("rep")
    half = size.width // 2
    keep = g["half_keep"]
    send, part_send = g["ship_half"], g["ship_part"]
    sums, sums2 = g["sums"].at[pl.ds(0, 8)], g["sums"].at[pl.ds(8, 8)]
    g["sums"][...] = jnp.zeros_like(g["sums"])
    gradient = g["third"][...] + dot_nt(g["inner"][...], g["w_exp"][...])
    g["mid"][...] = through_norm(size, g, gradient, "n2", "r2", "gain2", "w_cout", sums, g["back"])
    send_halves(core, g["branch"], keep, send, 0, half)
    attend_back(
        size, g["cq"], g["ck"], g["cv"], (g["pc_a"], g["pc_b"]), g["mixed"], g["back"], g["dq"], g["dk"], g["dv"], scaling
    )
    send_halves(core, g["dq"], keep, send, 1, half)
    split_partial(size, core, g["dk"], g["dv"], g["part_keep"], part_send)
    g.put("ship_part")
    g.put("part_keep")
    gradient = g["mid"][...] + dot_nt(g["dq"][...], g["w_cq"][...])
    g["low"] = through_norm(size, g, gradient, "n1", "r1", "gain1", "w_out", sums2, g["dcontext"])
    g.put("dcontext")
    send_halves(core, g["branch"], keep, send, 2, half)
    g.put("ship_half")
    g.put("half_keep")
    sums[3:4] = column_sum(g["dq"][...])
    sums[4:5] = column_sum(g["dv"][...])


def run_cross(size, scaling, f, ship3, third, weights, gains):
    n, t, w = size.own, size.full, size.width
    w_exp, w_cout, w_cq, w_out = weights
    loads = {
        "inner": load(f["inner"]),
        "w_exp": load(w_exp),
        "third": load(third),
        "n2": load(f["n2"]),
        "r2": load(f["r2"]),
        "w_cout": load(w_cout),
        "mixed": Load((n, w), bf16, [(ship3, columns(w, w), 0)]),
        "cv": load(f["cv"]),
        "pc_a": load(f["pc_a"]),
        "cq": load(f["cq"]),
        "ck": load(f["ck"]),
        "pc_b": load(f["pc_b"]),
        "w_cq": load(w_cq),
        "n1": load(f["n1"]),
        "r1": load(f["r1"]),
        "w_out": load(w_out),
    }
    square = shape((n, w), bf16)
    keys = shape((t, w), bf16)
    return staged(
        "cross_back",
        lambda g: cross_body(size, scaling, g),
        loads,
        {"gain2": (gains[0], VMEM), "gain1": (gains[1], VMEM)},
        {
            "low": shape((n, w), f32),
            "dcontext": square,
            "half_keep": shape((n, 3 * (w // 2)), bf16),
            "ship_half": shape((n, 3 * (w // 2)), bf16),
            "part_keep": keys,
            "ship_part": keys,
            "sums": shape((16, w), f32),
        },
        {"branch": square, "back": square, "dq": square, "dk": keys, "dv": keys, "mid": shape((n, w), f32)},
    )


def self_body(size, scaling, g):
    core = lax.axis_index("rep")
    half = size.width // 2
    send, part_send = g["ship_half"], g["ship_part"]
    sums = g["sums"]
    sums[...] = jnp.zeros_like(sums)
    attend_back(
        size, g["q"], g["k"], g["v"], (g["ps_a"], g["ps_b"]), g["context"], g["dcontext"], g["dq"], g["dk"], g["dv"], scaling
    )
    g.put("dq")
    split_partial(size, core, g["dk"], g["dv"], g["part_keep"], part_send)
    g.put("ship_part")
    send_halves(core, g["dq"], g["half_keep"], send, 0, half)
    g.put("ship_half")
    g.put("part_keep")
    g.put("half_keep")
    sums[0:1] = column_sum(g["dq"][...])
    sums[1:2] = column_sum(g["dv"][...])


def run_self(size, scaling, f, ship3, dcontext):
    n, t, w = size.own, size.full, size.width
    loads = {
        "dcontext": load(dcontext),
        "context": Load((n, w), bf16, [(ship3, columns(0, w), 0)]),
        "v": load(f["v"]),
        "ps_a": load(f["ps_a"]),
        "q": load(f["q"]),
        "k": load(f["k"]),
        "ps_b": load(f["ps_b"]),
    }
    square = shape((n, w), bf16)
    keys = shape((t, w), bf16)
    return staged(
        "self_back",
        lambda g: self_body(size, scaling, g),
        loads,
        {},
        {
            "dq": square,
            "half_keep": shape((n, w // 2), bf16),
            "ship_half": shape((n, w // 2), bf16),
            "part_keep": keys,
            "ship_part": keys,
            "sums": shape((8, w), f32),
        },
        {"dk": keys, "dv": keys},
    )


BLOCKS = 16
STAGES = 4
ORDER_X = (0, 1, 2, 3)
ORDER_Y = (1, 0, 2, 3)


class Scatter:
    def __init__(self, order, me, keep, send, rows):
        self.order = order
        self.me = me
        self.keep = keep
        self.send = send
        self.rows = rows

    def store(self, block, value, start, count):
        distance = self.me ^ block
        place = 0
        for stage, bit in enumerate(self.order):
            place = place + (((distance >> bit) & 1) << (STAGES - 1 - stage))
        low = place < BLOCKS // 2
        at = pl.multiple_of(jnp.where(low, place, place - BLOCKS // 2) * self.rows, 16)
        rows = pl.ds(at, self.rows)
        cols = slice(start, start + count)

        @pl.when(low)
        def unused():
            self.keep[rows, cols] = value.astype(bf16)

        @pl.when(jnp.logical_not(low))
        def unused_too():
            self.send[rows, cols] = value.astype(bf16)

    def store_all(self, product, start):
        for block in range(BLOCKS):
            self.store(block, product[block * self.rows : (block + 1) * self.rows], start, product.shape[1])


def my_block(group):
    return lax.axis_index("tok") // group


def chunk_outs(size, columns, names):
    rows = size.width // 2
    return {name: shape((rows, columns), bf16) for name in names}


def expand_body(size, group, g):
    scatter = Scatter(ORDER_Y, my_block(group), g["keep"], g["send"], size.width // BLOCKS)
    for start in range(0, g["d"].shape[1], size.width):
        scatter.store_all(dot_tn(g["low"][...], g["d"][:, start : start + size.width]), start)


def run_expand_grad(size, group, ship, ship_other, keep):
    n, t, w = size.own, size.full, size.width
    half = keep.shape[1]
    return staged(
        "expand_grad",
        lambda g: expand_body(size, group, g),
        {
            "low": Load((t, w), bf16, [(ship, columns(0, w), 0), (ship_other, columns(0, w), n)]),
            "d": Load((t, half), bf16, [(keep, whole, 0), (ship_other, columns(w, half), n)]),
        },
        {},
        chunk_outs(size, half, ("keep", "send")),
        {},
    )


def reduce_body(size, group, g):
    rows = size.width // BLOCKS
    scatter = Scatter(ORDER_X, my_block(group), g["keep"], g["send"], rows)
    half = size.width // 2
    parts = g["hidden"].shape[1] // size.width
    for step in range(parts):
        product = dot_tn(g["hidden"][:, step * size.width : (step + 1) * size.width], g["d"][...])
        for at in range(BLOCKS):
            index = step * BLOCKS + at
            value = product[at * rows : (at + 1) * rows]
            scatter.store(index // parts, value, (index % parts) * half, half)


def run_reduce_grad(size, group, ship, ship_other, keep):
    n, t, w = size.own, size.full, size.width
    half = keep.shape[1]
    h = ship.shape[1] - half
    return staged(
        "reduce_grad",
        lambda g: reduce_body(size, group, g),
        {
            "d": Load((t, half), bf16, [(keep, whole, 0), (ship_other, columns(h, half), n)]),
            "hidden": Load((t, h), bf16, [(ship, columns(0, h), 0), (ship_other, columns(0, h), n)]),
        },
        {},
        chunk_outs(size, h // 2, ("keep", "send")),
        {},
    )


def projection_share(size, g, scatter):
    a, b = size.a, size.b
    total = g["total"]
    total[...] = (g["part_keep"][...].astype(f32) + g["part_recv"][...].astype(f32)).astype(bf16)
    scatter.store_all(dot_tn(g["source"][...], total[...]), 0)
    g.put("send_p")
    share = dot_nt(total[...], g["weight"][...])
    g["grad_send"][pl.ds(0, a)] = share[a : 2 * a].astype(bf16)
    g["grad_send"][pl.ds(a, b)] = share[2 * a + b :].astype(bf16)
    g["grad_own"][pl.ds(0, a)] = share[:a]
    g["grad_own"][pl.ds(a, b)] = share[2 * a : 2 * a + b]


def cross_grad_body(size, group, g):
    half = size.width // 2
    me = my_block(group)
    count = size.width // BLOCKS
    scatter_w = Scatter(ORDER_Y, me, g["keep_w"], g["send_w"], count)
    for at, name in enumerate(("mixed", "low1", "context")):
        cols = slice(at * half, (at + 1) * half)
        scatter_w.store_all(dot_tn(g[name][...], g["halves"][:, cols]), at * half)
    g.put("send_w")
    projection_share(size, g, Scatter(ORDER_X, me, g["keep_p"], g["send_p"], count))
    g.put("keep_w")
    g.put("keep_p")
    g.put("grad_send")


def my_columns(weight, width):
    skip = weight.shape[1] - 2 * width

    def pick(ref):
        return ref.at[:, pl.ds(pl.multiple_of(skip + lax.axis_index("rep") * width, LANES), width)]

    return Load((width, width), bf16, [(weight, pick, 0)])


def run_cross_grads(size, group, ship3, ship3_other, half_keep, half_recv, part_keep, part_recv, sources, weight):
    n, t, w = size.own, size.full, size.width

    def both(at):
        return Load((t, w), bf16, [(ship3, columns(at * w, w), 0), (ship3_other, columns(at * w, w), n)])

    half = w // 2
    outs = chunk_outs(size, 3 * half, ("keep_w", "send_w"))
    outs.update(chunk_outs(size, w, ("keep_p", "send_p")))
    outs["grad_own"] = shape((n, w), f32)
    outs["grad_send"] = shape((n, w), bf16)
    return staged(
        "cross_grads",
        lambda g: cross_grad_body(size, group, g),
        {
            "mixed": both(1),
            "halves": Load((t, 3 * half), bf16, [(half_keep, whole, 0), (half_recv, whole, n)]),
            "low1": both(2),
            "context": both(0),
            "part_keep": load(part_keep),
            "part_recv": load(part_recv),
            "source": Load((t, w), bf16, size.full_pieces(*sources)),
            "weight": my_columns(weight, w),
        },
        {},
        outs,
        {"total": shape((t, w), bf16)},
    )


def self_grad_body(size, group, sums, g):
    width = size.width
    half = width // 2
    me = my_block(group)
    count = width // BLOCKS
    scatter_w = Scatter(ORDER_Y, me, g["keep_w"], g["send_w"], count)
    held = g["rows"]
    held[...] = jnp.zeros_like(held)
    at = 0
    for name in sums:
        held[pl.ds(at, g[name].shape[0])] = g[name][...]
        at += g[name].shape[0]
    scatter_w.store_all(jnp.transpose(held[...]), half)
    projection_share(size, g, Scatter(ORDER_X, me, g["keep_p"], g["send_p"], count))
    scatter_w.store_all(dot_tn(g["lhs"][...], g["halves"][...]), 0)
    g.put("send_w")
    g.put("keep_p")
    g.put("keep_w")
    g.put("grad_send")
    g["grad_own"][...] += g["low"][...] + dot_nt(g["dq"][...], g["w_q"][...])


def run_self_grads(size, group, half_keep, half_recv, part_keep, part_recv, sources, weight, low, dq, sums):
    n, t, w = size.own, size.full, size.width
    half = w // 2
    loads = {key: load(value) for key, value in sums.items()}
    loads.update(
        part_keep=load(part_keep),
        part_recv=load(part_recv),
        source=Load((t, w), bf16, size.full_pieces(*sources)),
        weight=my_columns(weight, w),
        lhs=Load((t, w), bf16, size.own_pieces(*sources)),
        halves=Load((t, half), bf16, [(half_keep, whole, 0), (half_recv, whole, n)]),
        dq=load(dq),
        w_q=Load((w, w), bf16, [(weight, columns(0, w), 0)]),
        low=load(low),
    )
    outs = chunk_outs(size, half + LANES, ("keep_w", "send_w"))
    outs.update(chunk_outs(size, w, ("keep_p", "send_p")))
    outs["grad_own"] = shape((n, w), f32)
    outs["grad_send"] = shape((n, w), bf16)
    return staged(
        "self_grads",
        lambda g: self_grad_body(size, group, tuple(sums), g),
        loads,
        {},
        outs,
        {"total": shape((t, w), bf16), "rows": shape((LANES, w), f32)},
    )


def swap(value):
    return lax.ppermute(value, "rep", [(0, 1), (1, 0)])


class Line:
    def __init__(self):
        self.last = None

    def wait(self, *values):
        if self.last is None:
            return values
        return lax.optimization_barrier((*values, self.last))[:-1]

    def record(self, value):
        self.last = value


def add_step(pairs):
    rows = pairs[0][0].shape[0] // 2
    columns = sum(keep.shape[1] for keep, unused in pairs)

    def kernel(*refs):
        keep_out, send_out = refs[-2:]
        at = 0
        for index in range(len(pairs)):
            keep, received = refs[2 * index], refs[2 * index + 1]
            cols = slice(at, at + keep.shape[1])
            at += keep.shape[1]
            total = (keep[...].astype(f32) + received[...].astype(f32)).astype(bf16)
            keep_out[:, cols] = total[:rows]
            send_out[:, cols] = total[rows:]

    flat = [value for pair in pairs for value in pair]
    return pl.pallas_call(
        kernel,
        name="add_step",
        out_shape=[shape((rows, columns), bf16)] * 2,
        in_specs=[VMEM] * len(flat),
        out_specs=[VMEM] * 2,
        compiler_params=pltpu.CompilerParams(vmem_limit_bytes=LIMIT),
        cost_estimate=cost("add_step"),
    )(*flat)


class Chunk:
    def __init__(self, keep, send, order, group, stage=0):
        self.keep = keep
        self.order = order
        self.group = group
        self.stage = stage
        self.begin(send)

    def begin(self, send):
        devices = lax.axis_size("tok")
        bit = self.group << self.order[self.stage]
        self.received = lax.ppermute(send, "tok", [(i, i ^ bit) for i in range(devices)])

    def step(self, line):
        keep, received = line.wait(self.keep, self.received)
        self.stage += 1
        if self.stage == STAGES:
            self.total = (keep.astype(f32) + received.astype(f32)).astype(bf16)
            line.record(self.total)
            return
        half = keep.shape[0] // 2
        send = (keep[half:].astype(f32) + received[half:].astype(f32)).astype(bf16)
        self.keep = (keep[:half].astype(f32) + received[:half].astype(f32)).astype(bf16)
        line.record(self.keep)
        self.begin(send)


def spread(total, group):
    if group == 1:
        return total
    devices = lax.axis_size("tok")
    sets = [[start + i for i in range(group)] for start in range(0, devices, group)]
    total = lax.psum_scatter(total.astype(f32), "tok", scatter_dimension=0, tiled=True, axis_index_groups=sets)
    return total.astype(bf16)


def spread_ffn(total, group, columns, parts):
    if group == 1:
        return total
    wide = columns // parts
    rows = jnp.concatenate([total[:, at * wide : (at + 1) * wide] for at in range(parts)], axis=0)
    rows = spread(rows, group)
    count = rows.shape[0] // parts
    rows = jnp.concatenate([rows[at * count : (at + 1) * count] for at in range(parts)], axis=1)
    return jnp.concatenate([rows, spread(total[:, columns:], group)], axis=1)


def merge(line, *chunks):
    values = line.wait(*[value for chunk in chunks for value in (chunk.keep, chunk.received)])
    keep, send = add_step(list(zip(values[::2], values[1::2])))
    line.record(keep)
    return Chunk(keep, send, chunks[0].order, chunks[0].group, chunks[0].stage + 1)


def per_device(*args):
    (
        long_target,
        short_target,
        long_memory,
        short_memory,
        long_cot,
        short_cot,
        long_target_len,
        short_target_len,
        long_memory_len,
        short_memory_len,
        self_inproj,
        self_qbias,
        self_vbias,
        self_outproj,
        self_obias,
        first_gain,
        first_shift,
        cross_qproj,
        cross_qbias,
        cross_kvproj,
        cross_vbias,
        cross_outproj,
        cross_obias,
        second_gain,
        second_shift,
        expand_weight,
        expand_bias,
        reduce_weight,
        reduce_bias,
        final_gain,
        final_shift,
    ) = args
    core = lax.axis_index("rep")
    devices = lax.axis_size("tok")
    group = devices // BLOCKS
    width = long_target.shape[2]
    hidden_width = expand_weight.shape[1]
    size = Sizes(long_target.shape[1], short_target.shape[1], width)
    n = size.own
    scaling = 1.0 / math.sqrt(HEAD_DIM)
    own = (long_target, short_target, long_memory, short_memory)
    other = tuple(swap(value) for value in own)
    f = run_forward(
        size,
        hidden_width,
        scaling,
        (long_target_len, short_target_len, long_memory_len, short_memory_len),
        own,
        other,
        (long_cot, short_cot),
        (self_inproj, self_outproj, cross_qproj, cross_kvproj, cross_outproj, expand_weight, reduce_weight),
        (
            self_qbias,
            self_vbias,
            self_obias,
            first_gain,
            first_shift,
            cross_qbias,
            cross_vbias,
            cross_obias,
            second_gain,
            second_shift,
            expand_bias,
            reduce_bias,
            final_gain,
            final_shift,
        ),
    )
    line = Line()
    ship1_other = swap(f["ship1"])
    line.record(ship1_other)
    (ship2,) = line.wait(f["ship2"])
    ship2_other = swap(ship2)
    e = run_expand_grad(size, group, f["ship1"], ship1_other, f["inner_keep"])
    c2 = Chunk(e["keep"], e["send"], ORDER_Y, group)
    line.record(e["keep"])
    (ffn_keep,) = line.wait(f["ffn_keep"])
    r = run_reduce_grad(size, group, ship2, ship2_other, ffn_keep)
    c1 = Chunk(r["keep"], r["send"], ORDER_X, group)
    line.record(r["keep"])
    ship3, third = line.wait(f["ship3"], f["third"])
    ship3_other = swap(ship3)
    c = run_cross(
        size, scaling, f, ship3, third, (expand_weight, cross_outproj, cross_qproj, self_outproj), (second_gain, first_gain)
    )
    line.record(c["low"])
    chalf_other = swap(c["ship_half"])
    cpart_other = swap(c["ship_part"])
    b = run_self(size, scaling, f, ship3, c["dcontext"])
    line.record(b["dq"])
    shalf_other = swap(b["ship_half"])
    spart_other = swap(b["ship_part"])
    c2.step(line)
    c1.step(line)
    (chalf_keep,) = line.wait(c["half_keep"])
    m = run_cross_grads(
        size,
        group,
        ship3,
        ship3_other,
        chalf_keep,
        chalf_other,
        c["part_keep"],
        cpart_other,
        (long_memory, short_memory, other[2], other[3]),
        cross_kvproj,
    )
    line.record(m["keep_w"])
    c4 = Chunk(m["keep_w"], m["send_w"], ORDER_Y, group)
    c3 = Chunk(m["keep_p"], m["send_p"], ORDER_X, group)
    memory_other = swap(m["grad_send"])
    expand_rows = f["inner_sum"].reshape(devices, 4, width // devices).transpose(1, 0, 2).reshape(4, width)
    d1 = merge(line, c1, c2)
    (shalf_keep,) = line.wait(b["half_keep"])
    t = run_self_grads(
        size,
        group,
        shalf_keep,
        shalf_other,
        b["part_keep"],
        spart_other,
        (long_target, short_target, other[0], other[1]),
        self_inproj,
        c["low"],
        b["dq"],
        {"sums0": f["sums"], "sums1": c["sums"], "sums2": b["sums"], "sums3": expand_rows},
    )
    line.record(t["keep_w"])
    c6 = Chunk(t["keep_w"], t["send_w"], ORDER_Y, group)
    c5 = Chunk(t["keep_p"], t["send_p"], ORDER_X, group)
    target_other = swap(t["grad_send"])
    c3.step(line)
    c4.step(line)
    d1.step(line)
    c5.step(line)
    c6.step(line)
    d2 = merge(line, c3, c4)
    d1.step(line)
    ffn_mine = spread_ffn(d1.total, group, hidden_width // 2, hidden_width // width)
    ffn_theirs = swap(ffn_mine)
    d3 = merge(line, c5, c6)
    memory_own, memory_recv = line.wait(m["grad_own"], memory_other)
    memory_grad = (memory_own + memory_recv.astype(f32)).astype(bf16)
    target_own, target_recv = line.wait(t["grad_own"], target_other)
    target_grad = (target_own + target_recv.astype(f32)).astype(bf16)
    d2.step(line)
    d3.step(line)
    d2.step(line)
    cross_mine = spread(d2.total, group)
    cross_theirs = swap(cross_mine)
    d3.step(line)
    self_mine = spread(d3.total, group)
    self_theirs = swap(self_mine)

    def by_core(mine, theirs):
        return jnp.where(core == 0, mine, theirs).astype(f32), jnp.where(core == 0, theirs, mine).astype(f32)

    half = width // 2
    half_h = hidden_width // 2
    zero, one = by_core(ffn_mine, ffn_theirs)
    grad_reduce = jnp.concatenate(
        [
            jnp.concatenate([value[:, at * half : (at + 1) * half] for value in (zero, one)], axis=1)
            for at in range(hidden_width // width)
        ],
        axis=0,
    )
    grad_expand = jnp.concatenate([zero[:, half_h:], one[:, half_h:]], axis=1)
    zero, one = by_core(cross_mine, cross_theirs)

    def both(start, count):
        return jnp.concatenate([zero[:, start : start + count], one[:, start : start + count]], axis=1)

    grad_cross_kv = both(0, width)
    grad_cross_out = both(width, half)
    grad_cross_q = both(width + half, half)
    grad_self_out = both(2 * width, half)
    zero, one = by_core(self_mine, self_theirs)
    grad_self_in = jnp.concatenate(
        [zero[:, width : width + half], one[:, width : width + half], zero[:, :width], one[:, :width]], axis=1
    )
    small = (zero[:, width + half :] + one[:, width + half :]).T
    statistics = jnp.sqrt(small[3:7, 0] / (small[7, 0] * width))
    grad_expand_bias = small[32:36].reshape(-1)

    def tokens(flat):
        return flat[: size.a][None], flat[size.a :][None]

    return (
        f["out_a"],
        f["out_b"],
        *tokens(target_grad),
        *tokens(memory_grad),
        grad_self_in,
        small[24],
        small[25],
        grad_self_out,
        small[18],
        small[16],
        small[17],
        grad_cross_q,
        small[11],
        grad_cross_kv,
        small[12],
        grad_cross_out,
        small[10],
        small[8],
        small[9],
        grad_expand,
        grad_expand_bias,
        grad_reduce,
        small[2],
        small[0],
        small[1],
        statistics,
    )


def solution(mesh):
    split = P("tok", "rep", None)
    in_specs = (split,) * 6 + (P("tok"),) * 4 + (P(),) * 21
    out_specs = (split,) * 6 + (
        P("tok", None),
        P("tok"),
        P("tok"),
        P("tok", None),
        P("tok"),
        P("tok"),
        P("tok"),
        P("tok", None),
        P("tok"),
        P("tok", None),
        P("tok"),
        P("tok", None),
        P("tok"),
        P("tok"),
        P("tok"),
        P("tok", None),
        P("tok"),
        P("tok", None),
        P("tok"),
        P("tok"),
        P("tok"),
        P(),
    )
    return jax.shard_map(per_device, mesh=mesh, in_specs=in_specs, out_specs=out_specs, check_vma=False)
```

```python
import math

import jax
import jax.numpy as jnp
from jax import lax
from jax.experimental import pallas as pl
from jax.experimental.pallas import tpu as pltpu
from jax.sharding import PartitionSpec as P

HEADS = 12
HEAD_DIM = 64
LANES = 128
EPS = 1e-05
MASKED = -1e30
LIMIT = 62 * 1024 * 1024
ADD_LIMIT = 24 * 1024 * 1024

f32 = jnp.float32
bf16 = jnp.bfloat16

ANY = pl.BlockSpec(memory_space=pl.ANY)
VMEM = pl.BlockSpec(memory_space=pltpu.VMEM)
SMEM = pl.BlockSpec(memory_space=pltpu.SMEM)


def dot(a, b):
    return lax.dot_general(a, b, (((1,), (0,)), ((), ())), preferred_element_type=f32)


def dot_nt(a, b):
    return lax.dot_general(a, b, (((1,), (1,)), ((), ())), preferred_element_type=f32)


def dot_tn(a, b):
    return lax.dot_general(a, b, (((0,), (0,)), ((), ())), preferred_element_type=f32)


def shape(dims, dtype):
    return jax.ShapeDtypeStruct(dims, dtype)


def whole(ref):
    return ref


def columns(start, count):
    return lambda ref: ref.at[:, pl.ds(start, count)]


def rows(start, count):
    return lambda ref: ref.at[pl.ds(start, count)]


def first(ref):
    return ref.at[0]


def load(array):
    return Load(array.shape, array.dtype, [(array, whole, 0)])


class Load:
    def __init__(self, dims, dtype, pieces):
        self.dims = dims
        self.dtype = dtype
        self.pieces = pieces


class Split:
    def __init__(self, dims, dtype, count):
        self.shape = dims
        self.dtype = jnp.dtype(dtype)
        self.count = count

    def parts(self):
        return [shape((self.shape[0] // self.count, *self.shape[1:]), self.dtype)] * self.count


def parts_of(value):
    return value.parts() if isinstance(value, Split) else [value]


class Stage:
    def __init__(self, sems):
        self.sems = sems
        self.count = 0
        self.refs = {}
        self.loads = {}
        self.targets = {}
        self.sent = []

    def start(self, source, target):
        copy = pltpu.make_async_copy(source, target, self.sems.at[self.count])
        self.count += 1
        copy.start()
        return copy

    def __getitem__(self, name):
        for copy in self.loads.pop(name, ()):
            copy.wait()
        return self.refs[name]

    def __setitem__(self, name, value):
        self.refs[name][...] = value
        self.put(name)

    def put(self, name):
        targets = self.targets.pop(name, ())
        for index, target in enumerate(targets):
            source = self.refs[name]
            if len(targets) > 1:
                source = source.at[pl.ds(index * target.shape[0], target.shape[0])]
            self.sent.append(self.start(source, target))

    def finish(self):
        for name in list(self.targets):
            self.put(name)
        for name in list(self.loads):
            self[name]
        for copy in self.sent:
            copy.wait()


TIMES = {
    "forward": 27,
    "expand_grad": 7,
    "reduce_grad": 8,
    "cross_back": 16,
    "self_back": 8,
    "cross_grads": 10,
    "self_grads": 9,
    "add_step": 20,
}
SCALE = 0.02


def cost(name, weight=1.0):
    return pl.CostEstimate(flops=int(TIMES[name] * weight * SCALE * 1.15e9), bytes_accessed=1024, transcendentals=0)


def staged(name, body, loads, direct, outs, scratch):
    arrays = [piece[0] for value in loads.values() for piece in value.pieces]
    arrays += [value for value, unused in direct.values()]
    specs = [ANY] * sum(len(value.pieces) for value in loads.values())
    specs += [space for unused, space in direct.values()]
    buffers = {key: pltpu.VMEM(value.dims, value.dtype) for key, value in loads.items()}
    buffers.update({key: pltpu.VMEM(value.shape, value.dtype) for key, value in outs.items()})
    buffers.update({key: pltpu.VMEM(value.shape, value.dtype) for key, value in scratch.items()})
    results = [part for value in outs.values() for part in parts_of(value)]
    copies = sum(len(value.pieces) for value in loads.values()) + len(results)

    def kernel(*refs):
        refs = list(refs)
        stage = Stage(refs[-1])
        sources = {key: [refs.pop(0) for unused in value.pieces] for key, value in loads.items()}
        for key in direct:
            stage.refs[key] = refs.pop(0)
        for key, value in outs.items():
            stage.targets[key] = [refs.pop(0) for unused in parts_of(value)]
        for key in buffers:
            stage.refs[key] = refs.pop(0)
        for key, value in loads.items():
            stage.loads[key] = []
            for ref, (unused, pick, start) in zip(sources[key], value.pieces):
                source = pick(ref)
                target = stage.refs[key]
                if source.shape != target.shape:
                    target = target.at[pl.ds(start, source.shape[0])]
                stage.loads[key].append(stage.start(source, target))
        body(stage)
        stage.finish()

    values = pl.pallas_call(
        kernel,
        name=name,
        out_shape=results,
        in_specs=specs,
        out_specs=[ANY] * len(results),
        scratch_shapes=[*buffers.values(), pltpu.SemaphoreType.DMA((copies,))],
        compiler_params=pltpu.CompilerParams(vmem_limit_bytes=LIMIT),
        cost_estimate=cost(name),
    )(*arrays)
    values = list(values)
    return {
        key: [values.pop(0) for unused in parts_of(value)] if isinstance(value, Split) else values.pop(0)
        for key, value in outs.items()
    }


def row(ref):
    return ref[...].astype(f32).reshape(1, ref.shape[0])


def lane_heads():
    lane = lax.broadcasted_iota(jnp.int32, (1, LANES), 1)
    return (lane < HEAD_DIM, lane >= HEAD_DIM)


def only(mask, value):
    return jnp.where(mask, value, jnp.zeros_like(value))


def both_heads(heads, value):
    return jnp.concatenate([only(heads[0], value), only(heads[1], value)], axis=0)


def rejoin(heads, value):
    rows = value.shape[0] // 2
    return jnp.where(heads[0], value[:rows], value[rows:])


class Sizes:
    def __init__(self, long_local, short_local, width):
        self.a = long_local
        self.b = short_local
        self.own = long_local + short_local
        self.full = 2 * self.own
        self.width = width
        self.pairs = width // LANES
        self.buckets = ((0, self.a, 0), (self.a, self.b, 2 * self.a))

    def own_pieces(self, long_part, short_part, other_long=None, other_short=None):
        pieces = [(long_part, first, 0), (short_part, first, self.a)]
        if other_long is not None:
            pieces += [(other_long, first, self.own), (other_short, first, self.own + self.a)]
        return pieces

    def full_pieces(self, long_part, short_part, other_long, other_short):
        return [
            (long_part, first, 0),
            (other_long, first, self.a),
            (short_part, first, 2 * self.a),
            (other_short, first, 2 * self.a + self.b),
        ]


def key_positions(rows, core):
    at = lax.broadcasted_iota(jnp.int32, (2 * rows, 1), 0)
    return jnp.where(at < rows, core * rows + at, (1 - core) * rows + at - rows)


def query_positions(rows, core):
    at = lax.broadcasted_iota(jnp.int32, (1, 2 * rows), 1)
    return core * rows + jnp.where(at < rows, at, at - rows)


def softmax_columns(scores):
    raised = jnp.exp(scores - jnp.max(scores, axis=0, keepdims=True))
    return (raised * (1.0 / jnp.sum(raised, axis=0, keepdims=True))).astype(bf16)


def attend(size, q, k, v, bias, probs, out, live):
    heads = lane_heads()
    for start, rows, kstart in size.buckets:
        which = 0 if start == 0 else 1
        weights = []
        for pair in range(size.pairs):
            lanes = slice(pair * LANES, (pair + 1) * LANES)
            queries = both_heads(heads, q[start : start + rows, lanes])
            scores = dot_nt(k[kstart : kstart + 2 * rows, lanes], queries) + bias[which][...]
            weights.append(softmax_columns(scores))
            if rows >= LANES:
                finish_pair(size, v, probs, out, live, which, pair, weights.pop(), heads)
        for pair, value in enumerate(weights):
            finish_pair(size, v, probs, out, live, which, pair, value, heads)


def finish_pair(size, v, probs, out, live, which, pair, weights, heads):
    start, rows, kstart = size.buckets[which]
    lanes = slice(pair * LANES, (pair + 1) * LANES)
    probs[which][pair] = weights
    values = v[kstart : kstart + 2 * rows, lanes]
    context = by_query(heads, weights, values)
    out[start : start + rows, lanes] = jnp.where(live[which], context, 0.0).astype(bf16)


def by_query(heads, across, keyed):
    rows = across.shape[1] // 2
    if rows < LANES:
        return rejoin(heads, dot_tn(across, keyed))
    feature = lax.broadcasted_iota(jnp.int32, (LANES, 1), 0)
    turned = dot(keyed.T, across)
    return jnp.where(feature < HEAD_DIM, turned[:, :rows], turned[:, rows:]).T


def head_sums(product):
    rows = product.shape[0]
    if rows < LANES:
        turned = jnp.concatenate([product, product], axis=0).T
        lane = lax.broadcasted_iota(jnp.int32, (1, LANES), 1)
        low = jnp.sum(turned[:HEAD_DIM], axis=0, keepdims=True)
        high = jnp.sum(turned[HEAD_DIM:], axis=0, keepdims=True)
        return jnp.where(lane < rows, low, high)
    turned = product.T
    low = jnp.sum(turned[:HEAD_DIM], axis=0, keepdims=True)
    high = jnp.sum(turned[HEAD_DIM:], axis=0, keepdims=True)
    return jnp.concatenate([low, high], axis=1)


def attend_back(size, q, k, v, probs, context, grad, dq, dk, dv, scaling):
    heads = lane_heads()
    for which, (start, rows, kstart) in enumerate(size.buckets):
        held = []

        def finish(pair, weights, grads, dscores):
            lanes = slice(pair * LANES, (pair + 1) * LANES)
            at = slice(start, start + rows)
            keys = slice(kstart, kstart + 2 * rows)
            dk[keys, lanes] = dot(dscores, both_heads(heads, q[at, lanes])).astype(bf16)
            dv[keys, lanes] = dot(weights, grads).astype(bf16)
            dq[at, lanes] = (by_query(heads, dscores, k[keys, lanes]) * scaling).astype(bf16)

        for pair in range(size.pairs):
            lanes = slice(pair * LANES, (pair + 1) * LANES)
            at = slice(start, start + rows)
            weights = probs[which][pair]
            grads = grad[at, lanes]
            centred = head_sums(grads.astype(f32) * context[at, lanes].astype(f32))
            grads = both_heads(heads, grads)
            dprobs = dot_nt(v[kstart : kstart + 2 * rows, lanes], grads)
            dscores = (weights.astype(f32) * (dprobs - centred)).astype(bf16)
            if rows >= LANES:
                finish(pair, weights, grads, dscores)
            else:
                held.append((pair, weights, grads, dscores))
        for item in held:
            finish(*item)


def norm_parts(tensor):
    centre = tensor - jnp.mean(tensor, axis=-1, keepdims=True)
    rstd = lax.rsqrt(jnp.mean(centre * centre, axis=-1, keepdims=True) + EPS)
    return centre * rstd, rstd


def norm_back(normed, rstd, gain, gradient):
    scaled = gradient * gain
    inner = scaled - jnp.mean(scaled, axis=-1, keepdims=True)
    inner = inner - normed * jnp.mean(scaled * normed, axis=-1, keepdims=True)
    return inner * rstd


def column_sum(tensor):
    return jnp.sum(tensor.astype(f32), axis=0, keepdims=True)


def live_column(rows, core, length):
    return core * rows + lax.broadcasted_iota(jnp.int32, (rows, 1), 0) < length


def forward_body(size, hidden_width, scaling, g):
    core = lax.axis_index("rep")
    a, b, own, width = size.a, size.b, size.own, size.width
    target_len = (g["target_len_a"][0], g["target_len_b"][0])
    memory_len = (g["memory_len_a"][0], g["memory_len_b"][0])
    live = (live_column(a, core, target_len[0]), live_column(b, core, target_len[1]))
    live_all = jnp.concatenate(live, axis=0)
    bias = (g["bias_a"], g["bias_b"])
    context, mixed, low1 = (columns_of(g["ship3"], at * width, width) for at in range(3))
    low2, inner_send = columns_of(g["ship1"], 0, width), columns_of(g["ship1"], width, hidden_width // 2)
    hidden, ffn_send = columns_of(g["ship2"], 0, hidden_width), columns_of(g["ship2"], hidden_width, width // 2)
    for which, rows in enumerate((a, b)):
        at = key_positions(rows, core)
        allowed = (at < target_len[which]) & (at <= query_positions(rows, core))
        bias[which][...] = jnp.where(allowed, 0.0, MASKED)
    xo = g["xo"]
    g["q"] = ((dot(xo[...], g["w_q"][...]) + row(g["qbias"])).astype(bf16) * scaling).astype(bf16)
    xf = g["xf"]
    g["k"] = dot(xf[...], g["w_k"][...]).astype(bf16)
    g["v"] = (dot(xf[...], g["w_v"][...]) + row(g["vbias"])).astype(bf16)
    attend(size, g["q"], g["k"], g["v"], bias, (g["ps_a"], g["ps_b"]), context, live)
    for name in ("ps_a", "ps_b"):
        g.put(name)
    mf, w_ckv = g["mf"], g["w_ckv"]
    g["ck"] = dot(mf[...], w_ckv[:, :width]).astype(bf16)
    g["cv"] = (dot(mf[...], w_ckv[:, width:]) + row(g["cvbias"])).astype(bf16)

    def squares(tensor):
        kept = jnp.where(live_all, tensor * tensor, 0.0)
        return jnp.sum(jnp.sum(kept, axis=0, keepdims=True), axis=1, keepdims=True)

    branch = g["branch"]
    self_branch = dot(context[...], g["w_out"][...]) + row(g["obias"])
    square_self = squares(self_branch)
    normed, rstd = norm_parts(xo[...].astype(f32) + self_branch)
    g["n1"] = normed
    g["r1"] = rstd
    after_self = normed * row(g["gain1"]) + row(g["shift1"])
    low1[...] = after_self.astype(bf16)
    branch[...] = after_self
    query = dot(low1[...], g["w_cq"][...]) + row(g["cqbias"])
    g["cq"] = (query.astype(bf16) * scaling).astype(bf16)
    for which, rows in enumerate((a, b)):
        allowed = key_positions(rows, core) < memory_len[which]
        bias[which][...] = jnp.broadcast_to(jnp.where(allowed, 0.0, MASKED), bias[which].shape)
    attend(size, g["cq"], g["ck"], g["cv"], bias, (g["pc_a"], g["pc_b"]), mixed, live)
    for name in ("pc_a", "pc_b", "ship3"):
        g.put(name)
    cross_branch = dot(mixed[...], g["w_cout"][...]) + row(g["cobias"])
    square_cross = squares(cross_branch)
    normed, rstd = norm_parts(branch[...] + cross_branch)
    g["n2"] = normed
    g["r2"] = rstd
    after_cross = normed * row(g["gain2"]) + row(g["shift2"])
    low2[...] = after_cross.astype(bf16)
    branch[...] = after_cross
    third, slope = g["third"], g["slope"]
    w_exp, w_red = g["w_exp"], g["w_red"]
    eb = row(g["ebias"])
    total = None
    for step in range(hidden_width // width):
        cols = slice(step * width, (step + 1) * width)
        act = dot(low2[...], w_exp[:, cols]) + eb[:, cols]
        phi = 0.5 * (1.0 + lax.erf(act * (1.0 / math.sqrt(2.0))))
        hidden[:, cols] = (act * phi).astype(bf16)
        density = jnp.exp(-0.5 * act * act) * (1.0 / math.sqrt(2.0 * math.pi))
        slope[:, cols] = (phi + act * density).astype(bf16)
        part = dot(hidden[:, cols], w_red[cols, :])
        if step == 0:
            third[...] = part
        else:
            third[...] += part
    ffn_branch = third[...] + row(g["rbias"])
    square_ffn = squares(ffn_branch)
    normed, rstd = norm_parts(branch[...] + ffn_branch)
    gain = row(g["gain3"])
    final = normed * gain + row(g["shift3"])
    square_final = squares(final)
    low = final.astype(bf16)
    g["out_a"] = low[:a][None]
    g["out_b"] = low[a:][None]
    gradient = jnp.where(live_all, g["cot"][...].astype(f32), 0.0)
    d_third = norm_back(normed, rstd, gain, gradient)
    g["third"] = d_third
    d_ffn = d_third.astype(bf16)
    dffn = g["dffn"]
    dffn[...] = d_ffn
    half = width // 2
    g["ffn_keep"] = dffn[:, half_of(core, half)]
    ffn_send[...] = dffn[:, half_of(1 - core, half)]
    g.put("ship2")
    sums = g["sums"]
    sums[0:1] = column_sum(gradient * normed)
    sums[1:2] = column_sum(gradient)
    sums[2:3] = column_sum(d_ffn)
    count = jnp.sum(jnp.where(live_all, 1.0, 0.0), axis=0, keepdims=True)
    for at, value in enumerate((square_final, square_self, square_cross, square_ffn, count)):
        sums[3 + at : 4 + at] = jnp.broadcast_to(value, (1, width))
    g.put("sums")
    half = hidden_width // 2
    for side in (1 - core, core):
        for at, start in enumerate(range(0, half, width)):
            cols = pl.ds(pl.multiple_of(side * half + start, LANES), width)
            grad = dot_nt(dffn[...], w_red[cols, :]) * slope[:, cols].astype(f32)
            low = grad.astype(bf16)
            g["inner_sum"][:, cols] = column_sum(low)
            if side is core:
                g["inner_keep%d" % at] = low
            else:
                inner_send[:, pl.ds(start, width)] = low
        g.put("ship1")


def columns_of(ref, start, count):
    return ref.at[:, pl.ds(start, count)]


def half_of(core, half):
    return pl.ds(pl.multiple_of(core * half, LANES), half)


def run_forward(size, hidden_width, scaling, lengths, own, other, cots, weights, vectors):
    a, b, n, t, w, h = size.a, size.b, size.own, size.full, size.width, hidden_width
    w_in, w_out, w_cq, w_ckv, w_cout, w_exp, w_red = weights
    loads = {
        "xo": Load((n, w), bf16, size.own_pieces(own[0], own[1])),
        "w_q": Load((w, w), bf16, [(w_in, columns(0, w), 0)]),
        "xf": Load((t, w), bf16, size.full_pieces(own[0], own[1], other[0], other[1])),
        "w_k": Load((w, w), bf16, [(w_in, columns(w, w), 0)]),
        "w_v": Load((w, w), bf16, [(w_in, columns(2 * w, w), 0)]),
        "mf": Load((t, w), bf16, size.full_pieces(own[2], own[3], other[2], other[3])),
        "w_ckv": load(w_ckv),
        "w_out": load(w_out),
        "w_cq": load(w_cq),
        "w_cout": load(w_cout),
        "w_exp": load(w_exp),
        "w_red": load(w_red),
        "cot": Load((n, w), bf16, size.own_pieces(cots[0], cots[1])),
    }
    names = ("qbias", "vbias", "obias", "gain1", "shift1", "cqbias", "cvbias", "cobias", "gain2", "shift2")
    names += ("ebias", "rbias", "gain3", "shift3")
    direct = dict(zip(("target_len_a", "target_len_b", "memory_len_a", "memory_len_b"), ((v, SMEM) for v in lengths)))
    direct.update(zip(names, ((v, VMEM) for v in vectors)))
    square = shape((n, w), bf16)
    keys = shape((t, w), bf16)
    outs = {
        "out_a": shape((1, a, w), bf16),
        "out_b": shape((1, b, w), bf16),
        "q": square,
        "k": keys,
        "v": keys,
        "cq": square,
        "ck": keys,
        "cv": keys,
        "ps_a": shape((size.pairs, 2 * a, 2 * a), bf16),
        "ps_b": shape((size.pairs, 2 * b, 2 * b), bf16),
        "pc_a": shape((size.pairs, 2 * a, 2 * a), bf16),
        "pc_b": shape((size.pairs, 2 * b, 2 * b), bf16),
        "ship1": shape((n, w + h // 2), bf16),
        "ship2": shape((n, h + w // 2), bf16),
        "ship3": shape((n, 3 * w), bf16),
        "n1": shape((n, w), f32),
        "r1": shape((n, 1), f32),
        "n2": shape((n, w), f32),
        "r2": shape((n, 1), f32),
        "third": shape((n, w), f32),
        "ffn_keep": shape((n, w // 2), bf16),
        "sums": shape((8, w), f32),
        "inner_keep0": square,
        "inner_keep1": square,
        "inner_sum": shape((1, h), f32),
    }
    scratch = {
        "bias_a": shape((2 * a, 2 * a), f32),
        "bias_b": shape((2 * b, 2 * b), f32),
        "branch": shape((n, w), f32),
        "slope": shape((n, h), bf16),
        "dffn": square,
    }
    return staged(
        "forward",
        lambda g: forward_body(size, hidden_width, scaling, g),
        loads,
        direct,
        outs,
        scratch,
    )


def split_partial(size, core, dk, dv, keep, send):
    a, b = size.a, size.b
    moves = ((0, a, a), (a, 0, a), (2 * a, 2 * a + b, b), (2 * a + b, 2 * a, b))
    for here, (stay, leave) in ((0, (dk, dv)), (1, (dv, dk))):

        @pl.when(core == here)
        def unused(stay=stay, leave=leave):
            keep[...] = stay[...]
            for target, source, rows in moves:
                send[pl.ds(target, rows)] = leave[pl.ds(source, rows)]


def through_norm(size, g, gradient, normed, rstd, gain, w_out, sums, back):
    normed = g[normed][...]
    d_sum = norm_back(normed, g[rstd][...], row(g[gain]), gradient)
    sums[0:1] = column_sum(gradient * normed)
    sums[1:2] = column_sum(gradient)
    low = d_sum.astype(bf16)
    sums[2:3] = column_sum(low)
    g["branch"][...] = low
    back[...] = dot_nt(low, g[w_out][...]).astype(bf16)
    return d_sum


def send_halves(core, value, keep, send, at, half):
    keep[:, at * half : (at + 1) * half] = value[:, half_of(core, half)]
    send[:, at * half : (at + 1) * half] = value[:, half_of(1 - core, half)]


def cross_body(size, scaling, parts, g):
    core = lax.axis_index("rep")
    half = size.width // 2
    keep = g["half_keep"]
    send, part_send = g["ship_half"], g["ship_part"]
    sums, sums2 = g["sums"].at[pl.ds(0, 8)], g["sums"].at[pl.ds(8, 8)]
    g["sums"][...] = jnp.zeros_like(g["sums"])
    gradient = g["third"][...]
    for index in range(parts):
        gradient = gradient + dot_nt(g["inner%d" % index][...], g["w_exp%d" % index][...])
    g["mid"][...] = through_norm(size, g, gradient, "n2", "r2", "gain2", "w_cout", sums, g["back"])
    send_halves(core, g["branch"], keep, send, 0, half)
    attend_back(
        size, g["cq"], g["ck"], g["cv"], (g["pc_a"], g["pc_b"]), g["mixed"], g["back"], g["dq"], g["dk"], g["dv"], scaling
    )
    send_halves(core, g["dq"], keep, send, 1, half)
    g.put("ship_half")
    split_partial(size, core, g["dk"], g["dv"], g["part_keep"], part_send)
    g.put("ship_part")
    g.put("part_keep")
    gradient = g["mid"][...] + dot_nt(g["dq"][...], g["w_cq"][...])
    g["low"] = through_norm(size, g, gradient, "n1", "r1", "gain1", "w_out", sums2, g["dcontext"])
    g.put("dcontext")
    keep[:, 2 * half :] = g["branch"][:, half_of(core, half)]
    g["ship_self"] = g["branch"][:, half_of(1 - core, half)]
    g.put("half_keep")
    sums[3:4] = column_sum(g["dq"][...])
    sums[4:5] = column_sum(g["dv"][...])


def run_cross(size, scaling, f, ship3, third, weights, gains):
    n, t, w = size.own, size.full, size.width
    w_exp, w_cout, w_cq, w_out = weights
    loads = {
        "third": load(third),
    }
    parts = w_exp.shape[1] // w

    def column_part(index):
        def pick(ref):
            core = lax.axis_index("rep")
            side = core if index < 2 else 1 - core
            return ref.at[:, pl.ds(pl.multiple_of((2 * side + index % 2) * w, LANES), w)]

        return Load((w, w), bf16, [(w_exp, pick, 0)])

    for index in range(parts):
        source = (f["inner_keep%d" % index], whole, 0) if index < 2 else (f["ship1"], columns((index - 1) * w, w), 0)
        loads["inner%d" % index] = Load((n, w), bf16, [source])
        loads["w_exp%d" % index] = column_part(index)
    loads |= {
        "n2": load(f["n2"]),
        "r2": load(f["r2"]),
        "w_cout": load(w_cout),
        "mixed": Load((n, w), bf16, [(ship3, columns(w, w), 0)]),
        "cv": load(f["cv"]),
        "pc_a": load(f["pc_a"]),
        "cq": load(f["cq"]),
        "ck": load(f["ck"]),
        "pc_b": load(f["pc_b"]),
        "w_cq": load(w_cq),
        "n1": load(f["n1"]),
        "r1": load(f["r1"]),
        "w_out": load(w_out),
    }
    square = shape((n, w), bf16)
    keys = shape((t, w), bf16)
    return staged(
        "cross_back",
        lambda g: cross_body(size, scaling, parts, g),
        loads,
        {"gain2": (gains[0], VMEM), "gain1": (gains[1], VMEM)},
        {
            "low": shape((n, w), f32),
            "dcontext": square,
            "half_keep": shape((n, 3 * (w // 2)), bf16),
            "ship_half": square,
            "ship_self": shape((n, w // 2), bf16),
            "part_keep": keys,
            "ship_part": Split((t, w), bf16, PIECES),
            "sums": shape((16, w), f32),
        },
        {"branch": square, "back": square, "dq": square, "dk": keys, "dv": keys, "mid": shape((n, w), f32)},
    )


def self_body(size, scaling, g):
    core = lax.axis_index("rep")
    half = size.width // 2
    send, part_send = g["ship_half"], g["ship_part"]
    sums = g["sums"]
    sums[...] = jnp.zeros_like(sums)
    attend_back(
        size, g["q"], g["k"], g["v"], (g["ps_a"], g["ps_b"]), g["context"], g["dcontext"], g["dq"], g["dk"], g["dv"], scaling
    )
    g.put("dq")
    split_partial(size, core, g["dk"], g["dv"], g["part_keep"], part_send)
    g.put("ship_part")
    send_halves(core, g["dq"], g["half_keep"], send, 0, half)
    g.put("ship_half")
    g.put("part_keep")
    g.put("half_keep")
    sums[0:1] = column_sum(g["dq"][...])
    sums[1:2] = column_sum(g["dv"][...])


def run_self(size, scaling, f, ship3, dcontext):
    n, t, w = size.own, size.full, size.width
    loads = {
        "dcontext": load(dcontext),
        "context": Load((n, w), bf16, [(ship3, columns(0, w), 0)]),
        "v": load(f["v"]),
        "ps_a": load(f["ps_a"]),
        "q": load(f["q"]),
        "k": load(f["k"]),
        "ps_b": load(f["ps_b"]),
    }
    square = shape((n, w), bf16)
    keys = shape((t, w), bf16)
    return staged(
        "self_back",
        lambda g: self_body(size, scaling, g),
        loads,
        {},
        {
            "dq": square,
            "half_keep": shape((n, w // 2), bf16),
            "ship_half": Split((n, w // 2), bf16, 1),
            "part_keep": keys,
            "ship_part": Split((t, w), bf16, PIECES),
            "sums": shape((8, w), f32),
        },
        {"dk": keys, "dv": keys},
    )


PIECES = 2
BLOCKS = 16
STAGES = 4
ORDER_XZY = (0, 2, 3, 1)
ORDER_YXZ = (1, 0, 2, 3)
ORDER_ZXY = (2, 3, 0, 1)


class Scatter:
    def __init__(self, order, me, keep, send, rows):
        self.order = order
        self.me = me
        self.keep = keep
        self.send = send
        self.rows = rows

    def store(self, block, value, start, count):
        distance = self.me ^ block
        place = 0
        for stage, bit in enumerate(self.order):
            place = place + (((distance >> bit) & 1) << (STAGES - 1 - stage))
        low = place < BLOCKS // 2
        at = pl.multiple_of(jnp.where(low, place, place - BLOCKS // 2) * self.rows, 16)
        rows = pl.ds(at, self.rows)
        cols = slice(start, start + count)

        @pl.when(low)
        def unused():
            self.keep[rows, cols] = value.astype(bf16)

        @pl.when(jnp.logical_not(low))
        def unused_too():
            self.send[rows, cols] = value.astype(bf16)

    def store_all(self, product, start):
        for block in range(BLOCKS):
            self.store(block, product[block * self.rows : (block + 1) * self.rows], start, product.shape[1])


def my_block(group):
    return lax.axis_index("tok") // group


def chunk_outs(size, columns, names):
    rows = size.width // 2
    return {name: shape((rows, columns), bf16) for name in names}


def expand_body(size, group, g):
    scatter = Scatter(ORDER_XZY, my_block(group), g["keep"], g["send"], size.width // BLOCKS)
    for at in range(2):
        scatter.store_all(dot_tn(g["low"][...], g["d%d" % at][...]), at * size.width)
    g.put("send")


def run_expand_grad(size, group, ship, ship_other, keeps):
    n, t, w = size.own, size.full, size.width
    loads = {"low": Load((t, w), bf16, [(ship, columns(0, w), 0), (ship_other, columns(0, w), n)])}
    for at, keep in enumerate(keeps):
        loads["d%d" % at] = Load((t, w), bf16, [(keep, whole, 0), (ship_other, columns(w + at * w, w), n)])
    return staged(
        "expand_grad",
        lambda g: expand_body(size, group, g),
        loads,
        {},
        chunk_outs(size, 2 * w, ("keep", "send")),
        {},
    )


def reduce_chunk(group, index):
    return (my_block(group) >> 2) ^ (1, 3, 0, 2)[index]


def reduce_body(size, group, g):
    count = size.width // BLOCKS
    half = size.width // 2
    parts = BLOCKS // 4
    mine = my_block(group) & 3
    for index in range(4):
        target = g["send"] if index < 2 else g["keep"]
        product = dot_tn(g["hidden%d" % index][...], g["d"][...])
        for block in range(4):
            distance = mine ^ block
            place = (index % 2) * 4 + ((distance & 1) << 1) + (distance >> 1)
            at = pl.ds(pl.multiple_of(place * count, 16), count)
            for part in range(parts):
                start = (block * parts + part) * count
                target[at, part * half : (part + 1) * half] = product[start : start + count].astype(bf16)
        if index % 2 == 1:
            g.put("send" if index < 2 else "keep")


def run_reduce_grad(size, group, ship, ship_other, keep):
    n, t, w = size.own, size.full, size.width
    half = keep.shape[1]
    h = ship.shape[1] - half
    quarter = h // 4

    def chunk(index):
        def pick(ref):
            return ref.at[:, pl.ds(pl.multiple_of(reduce_chunk(group, index) * quarter, LANES), quarter)]

        return Load((t, quarter), bf16, [(ship, pick, 0), (ship_other, pick, n)])

    loads = {"d": Load((t, half), bf16, [(keep, whole, 0), (ship_other, columns(h, half), n)])}
    loads.update({"hidden%d" % index: chunk(index) for index in range(4)})
    return staged(
        "reduce_grad",
        lambda g: reduce_body(size, group, g),
        loads,
        {},
        chunk_outs(size, h // 2, ("send", "keep")),
        {},
    )


def projection_share(size, g, scatter):
    a, b = size.a, size.b
    total = g["total"]
    total[...] = (g["part_keep"][...].astype(f32) + g["part_recv"][...].astype(f32)).astype(bf16)
    scatter.store_all(dot_tn(g["source"][...], total[...]), 0)
    g.put("send")
    share = dot_nt(total[...], g["weight"][...])
    g["grad_send"][pl.ds(0, a)] = share[a : 2 * a].astype(bf16)
    g["grad_send"][pl.ds(a, b)] = share[2 * a + b :].astype(bf16)
    g["grad_own"][pl.ds(0, a)] = share[:a]
    g["grad_own"][pl.ds(a, b)] = share[2 * a : 2 * a + b]


def cross_grad_body(size, group, g):
    width = size.width
    half = width // 2
    scatter = Scatter(ORDER_YXZ, my_block(group), g["keep"], g["send"], width // BLOCKS)
    for at, name in enumerate(("mixed", "low1")):
        cols = slice(at * half, (at + 1) * half)
        scatter.store_all(dot_tn(g[name][...], g["halves"][:, cols]), width + at * half)
    scatter.store_all(dot_tn(g["context"][...], g["halves_self"][...]), 2 * width)
    projection_share(size, g, scatter)
    g.put("keep")
    g.put("grad_send")


def stacked(arrays, start):
    return [(array, whole, start + index * array.shape[0]) for index, array in enumerate(arrays)]


def my_columns(weight, width):
    skip = weight.shape[1] - 2 * width

    def pick(ref):
        return ref.at[:, pl.ds(pl.multiple_of(skip + lax.axis_index("rep") * width, LANES), width)]

    return Load((width, width), bf16, [(weight, pick, 0)])


def run_cross_grads(size, group, ship3, ship3_other, half_keep, half_recv, part_keep, part_recv, sources, weight):
    n, t, w = size.own, size.full, size.width

    def both(at):
        return Load((t, w), bf16, [(ship3, columns(at * w, w), 0), (ship3_other, columns(at * w, w), n)])

    half = w // 2
    outs = chunk_outs(size, w + 3 * half, ("keep", "send"))
    outs["grad_own"] = shape((n, w), f32)
    outs["grad_send"] = shape((n, w), bf16)
    return staged(
        "cross_grads",
        lambda g: cross_grad_body(size, group, g),
        {
            "mixed": both(1),
            "halves": Load((t, 2 * half), bf16, [(half_keep, columns(0, 2 * half), 0), (half_recv[0], whole, n)]),
            "low1": both(2),
            "context": both(0),
            "halves_self": Load((t, half), bf16, [(half_keep, columns(2 * half, half), 0), (half_recv[1], whole, n)]),
            "part_keep": load(part_keep),
            "part_recv": Load((t, w), bf16, stacked(part_recv, 0)),
            "source": Load((t, w), bf16, size.full_pieces(*sources)),
            "weight": my_columns(weight, w),
        },
        {},
        outs,
        {"total": shape((t, w), bf16)},
    )


def regroup(value, width, count):
    parts = value.shape[1] // width
    lane = lax.broadcasted_iota(jnp.int32, (1, width), 1)
    rows_out = [jnp.zeros((1, width), f32)] * parts
    for step in range(parts):
        piece = value[:, step * width : (step + 1) * width]
        for at in range(width // count):
            device, part = divmod(step * (width // count) + at, parts)
            moved = pltpu.roll(piece, ((device - at) * count) % width, 1)
            mine = (lane >= device * count) & (lane < (device + 1) * count)
            rows_out[part] = jnp.where(mine, moved, rows_out[part])
    return jnp.concatenate(rows_out, axis=0)


def self_grad_body(size, group, sums, g):
    width = size.width
    half = width // 2
    count = width // BLOCKS
    scatter = Scatter(ORDER_YXZ, my_block(group), g["keep"], g["send"], count)
    held = g["rows"]
    held[...] = jnp.zeros_like(held)
    at = 0
    for name in sums:
        value = g[name][...]
        if value.shape[1] > width:
            value = regroup(value, width, count)
        held[pl.ds(at, value.shape[0])] = value
        at += value.shape[0]
    scatter.store_all(jnp.transpose(held[...]), width + half)
    scatter.store_all(dot_tn(g["lhs"][...], g["halves"][...]), width)
    projection_share(size, g, scatter)
    g.put("keep")
    g.put("grad_send")
    g["grad_own"][...] += g["low"][...] + dot_nt(g["dq"][...], g["w_q"][...])


def run_self_grads(size, group, half_keep, half_recv, part_keep, part_recv, sources, weight, low, dq, sums):
    n, t, w = size.own, size.full, size.width
    half = w // 2
    loads = {key: load(value) for key, value in sums.items()}
    loads.update(
        part_keep=load(part_keep),
        part_recv=Load((t, w), bf16, stacked(part_recv, 0)),
        source=Load((t, w), bf16, size.full_pieces(*sources)),
        weight=my_columns(weight, w),
        lhs=Load((t, w), bf16, size.own_pieces(*sources)),
        halves=Load((t, half), bf16, [(half_keep, whole, 0), *stacked(half_recv, n)]),
        dq=load(dq),
        w_q=Load((w, w), bf16, [(weight, columns(0, w), 0)]),
        low=load(low),
    )
    outs = chunk_outs(size, w + half + LANES, ("keep", "send"))
    outs["grad_own"] = shape((n, w), f32)
    outs["grad_send"] = shape((n, w), bf16)
    return staged(
        "self_grads",
        lambda g: self_grad_body(size, group, tuple(sums), g),
        loads,
        {},
        outs,
        {"total": shape((t, w), bf16), "rows": shape((LANES, w), f32)},
    )


def swap(value):
    return lax.ppermute(value, "rep", [(0, 1), (1, 0)])


class Line:
    def __init__(self):
        self.last = None

    def wait(self, *values):
        if self.last is None:
            return values
        return lax.optimization_barrier((*values, self.last))[:-1]

    def record(self, value):
        self.last = value


def add_step(pairs, weight=1.0):
    rows = pairs[0][0].shape[0] // 2
    columns = sum(keep.shape[1] for keep, unused in pairs)

    def kernel(*refs):
        keep_out, send_out = refs[-2:]
        at = 0
        for index in range(len(pairs)):
            keep, received = refs[2 * index], refs[2 * index + 1]
            cols = slice(at, at + keep.shape[1])
            at += keep.shape[1]
            total = (keep[...].astype(f32) + received[...].astype(f32)).astype(bf16)
            keep_out[:, cols] = total[:rows]
            send_out[:, cols] = total[rows:]

    flat = [value for pair in pairs for value in pair]
    return pl.pallas_call(
        kernel,
        name="add_step",
        out_shape=[shape((rows, columns), bf16)] * 2,
        in_specs=[VMEM] * len(flat),
        out_specs=[VMEM] * 2,
        compiler_params=pltpu.CompilerParams(vmem_limit_bytes=ADD_LIMIT),
        cost_estimate=cost("add_step", weight),
    )(*flat)


def add_last(keep, received):
    def kernel(keep, received, out):
        out[...] = (keep[...].astype(f32) + received[...].astype(f32)).astype(bf16)

    return pl.pallas_call(
        kernel,
        name="add_last",
        out_shape=shape(keep.shape, bf16),
        in_specs=[VMEM] * 2,
        out_specs=VMEM,
        compiler_params=pltpu.CompilerParams(vmem_limit_bytes=ADD_LIMIT),
        cost_estimate=cost("add_step"),
    )(keep, received)


class Chunk:
    def __init__(self, keep, send, order, group, stage=0):
        self.keep = keep
        self.order = order
        self.group = group
        self.stage = stage
        self.begin(send)

    def begin(self, send):
        devices = lax.axis_size("tok")
        bit = self.group << self.order[self.stage]
        self.received = lax.ppermute(send, "tok", [(i, i ^ bit) for i in range(devices)])

    def launch(self, line):
        (send,) = line.wait(self.send)
        self.begin(send)

    def step(self, line, weight=1.0):
        self.absorb(line, weight)
        if self.stage < STAGES:
            self.begin(self.send)

    def absorb(self, line, weight=1.0):
        keep, received = line.wait(self.keep, self.received)
        self.stage += 1
        if self.stage == STAGES:
            self.total = add_last(keep, received)
            line.record(self.total)
            return
        self.keep, self.send = add_step([(keep, received)], weight)
        line.record(self.keep)


def spread(total, group):
    if group == 1:
        return total
    devices = lax.axis_size("tok")
    sets = [[start + i for i in range(group)] for start in range(0, devices, group)]
    total = lax.psum_scatter(total.astype(f32), "tok", scatter_dimension=0, tiled=True, axis_index_groups=sets)
    return total.astype(bf16)


def spread_blocks(total, group, parts):
    if group == 1:
        return total
    wide = total.shape[1] // parts
    rows_in = jnp.concatenate([total[:, at * wide : (at + 1) * wide] for at in range(parts)], axis=0)
    rows_in = spread(rows_in, group)
    count = rows_in.shape[0] // parts
    return jnp.concatenate([rows_in[at * count : (at + 1) * count] for at in range(parts)], axis=1)


def merge(line, *chunks):
    values = line.wait(*[value for chunk in chunks for value in (chunk.keep, chunk.received)])
    keep, send = add_step(list(zip(values[::2], values[1::2])))
    line.record(keep)
    return Chunk(keep, send, chunks[0].order, chunks[0].group, chunks[0].stage + 1)


def add_tokens(size, *values):
    a, b, w = size.a, size.b, size.width

    def kernel(*refs):
        for at in range(2):
            own, received = refs[2 * at : 2 * at + 2]
            long_out, short_out = refs[4 + 2 * at : 6 + 2 * at]
            long_out[0] = (own[:a] + received[:a].astype(f32)).astype(bf16)
            short_out[0] = (own[a:] + received[a:].astype(f32)).astype(bf16)

    outs = pl.pallas_call(
        kernel,
        name="add_tokens",
        out_shape=[shape((1, a, w), bf16), shape((1, b, w), bf16)] * 2,
        in_specs=[VMEM] * 4,
        out_specs=[VMEM] * 4,
        compiler_params=pltpu.CompilerParams(vmem_limit_bytes=ADD_LIMIT),
        cost_estimate=cost("add_step", 0.0),
    )(*values)
    return outs[:2], outs[2:]


def finish(pairs, dims, moves):
    outs = [shape(value, f32) for value in dims]

    def kernel(*refs):
        core = lax.axis_index("rep")
        for pair, out, start, count, row_at, column in moves:
            mine, theirs = refs[2 * pair], refs[2 * pair + 1]
            target = refs[len(pairs) + out]
            at = slice(row_at, row_at + mine.shape[0])
            cols = slice(start, start + count)
            if column is None:
                target[at, :] = mine[:, cols].astype(f32) + theirs[:, cols].astype(f32)
                continue
            for ref, side in ((mine, core), (theirs, 1 - core)):
                target[at, pl.ds(pl.multiple_of(column + side * count, LANES), count)] = ref[:, cols].astype(f32)

    return pl.pallas_call(
        kernel,
        name="finish",
        out_shape=outs,
        in_specs=[VMEM] * len(pairs),
        out_specs=[VMEM] * len(outs),
        compiler_params=pltpu.CompilerParams(vmem_limit_bytes=ADD_LIMIT),
        cost_estimate=cost("add_step"),
    )(*pairs)


def per_device(*args):
    (
        long_target,
        short_target,
        long_memory,
        short_memory,
        long_cot,
        short_cot,
        long_target_len,
        short_target_len,
        long_memory_len,
        short_memory_len,
        self_inproj,
        self_qbias,
        self_vbias,
        self_outproj,
        self_obias,
        first_gain,
        first_shift,
        cross_qproj,
        cross_qbias,
        cross_kvproj,
        cross_vbias,
        cross_outproj,
        cross_obias,
        second_gain,
        second_shift,
        expand_weight,
        expand_bias,
        reduce_weight,
        reduce_bias,
        final_gain,
        final_shift,
    ) = args
    core = lax.axis_index("rep")
    devices = lax.axis_size("tok")
    group = devices // BLOCKS
    width = long_target.shape[2]
    hidden_width = expand_weight.shape[1]
    size = Sizes(long_target.shape[1], short_target.shape[1], width)
    n = size.own
    scaling = 1.0 / math.sqrt(HEAD_DIM)
    own = (long_target, short_target, long_memory, short_memory)
    other = tuple(swap(value) for value in own)
    f = run_forward(
        size,
        hidden_width,
        scaling,
        (long_target_len, short_target_len, long_memory_len, short_memory_len),
        own,
        other,
        (long_cot, short_cot),
        (self_inproj, self_outproj, cross_qproj, cross_kvproj, cross_outproj, expand_weight, reduce_weight),
        (
            self_qbias,
            self_vbias,
            self_obias,
            first_gain,
            first_shift,
            cross_qbias,
            cross_vbias,
            cross_obias,
            second_gain,
            second_shift,
            expand_bias,
            reduce_bias,
            final_gain,
            final_shift,
        ),
    )
    line = Line()
    ship1_other = swap(f["ship1"])
    ship2_other = swap(f["ship2"])
    ship3 = f["ship3"]
    ship3_other = swap(ship3)
    c = run_cross(
        size,
        scaling,
        f,
        ship3,
        f["third"],
        (expand_weight, cross_outproj, cross_qproj, self_outproj),
        (second_gain, first_gain),
    )
    line.record(c["low"])
    chalf_other = (swap(c["ship_half"]), swap(c["ship_self"]))
    cpart_other = [swap(value) for value in c["ship_part"]]
    (ffn_keep,) = line.wait(f["ffn_keep"])
    r = run_reduce_grad(size, group, f["ship2"], ship2_other, ffn_keep)
    c1 = Chunk(r["keep"], r["send"], ORDER_ZXY, group)
    line.record(r["keep"])
    (chalf_keep,) = line.wait(c["half_keep"])
    m = run_cross_grads(
        size,
        group,
        ship3,
        ship3_other,
        chalf_keep,
        chalf_other,
        c["part_keep"],
        cpart_other,
        (long_memory, short_memory, other[2], other[3]),
        cross_kvproj,
    )
    c3 = Chunk(m["keep"], m["send"], ORDER_YXZ, group)
    line.record(m["keep"])
    (inner_keep0,) = line.wait(f["inner_keep0"])
    e = run_expand_grad(size, group, f["ship1"], ship1_other, (inner_keep0, f["inner_keep1"]))
    c2 = Chunk(e["keep"], e["send"], ORDER_XZY, group)
    line.record(e["keep"])
    (dcontext,) = line.wait(c["dcontext"])
    b = run_self(size, scaling, f, ship3, dcontext)
    line.record(b["dq"])
    shalf_other = [swap(value) for value in b["ship_half"]]
    spart_other = [swap(value) for value in b["ship_part"]]
    c1.step(line, 0.0)
    (shalf_keep,) = line.wait(b["half_keep"])
    if group == 1:
        expand_rows = f["inner_sum"]
    else:
        expand_rows = f["inner_sum"].reshape(devices, 4, width // devices).transpose(1, 0, 2).reshape(4, width)
    t = run_self_grads(
        size,
        group,
        shalf_keep,
        shalf_other,
        b["part_keep"],
        spart_other,
        (long_target, short_target, other[0], other[1]),
        self_inproj,
        c["low"],
        b["dq"],
        {"sums0": f["sums"], "sums1": c["sums"], "sums2": b["sums"], "sums3": expand_rows},
    )
    c5 = Chunk(t["keep"], t["send"], ORDER_YXZ, group)
    line.record(t["keep"])
    c3.step(line, 0.0)
    c2.step(line, 0.0)
    c1.step(line, 12.0)
    memory_recv, target_recv = (swap(value) for value in line.wait(m["grad_send"], t["grad_send"]))
    for chunk in (c5, c3, c2):
        chunk.step(line)
    memory_grads, target_grads = add_tokens(
        size, *line.wait(m["grad_own"], memory_recv, t["grad_own"], target_recv)
    )
    line.record(target_grads[0])
    for chunk in (c1, c5, c3, c2, c1):
        chunk.step(line)
    reduce_mine = spread_blocks(c1.total, group, hidden_width // width)
    reduce_theirs = swap(reduce_mine)
    c5.step(line)
    c3.step(line)
    cross_mine = spread(c3.total, group)
    cross_theirs = swap(cross_mine)
    c2.step(line)
    expand_mine = spread(c2.total, group)
    expand_theirs = swap(expand_mine)
    c5.step(line)
    self_mine = spread(c5.total, group)
    self_theirs = swap(self_mine)
    half = width // 2
    half_h = hidden_width // 2
    parts = hidden_width // width
    reduce_theirs, expand_theirs, cross_theirs = line.wait(reduce_theirs, expand_theirs, cross_theirs)
    rows_out = reduce_mine.shape[0]
    grad_reduce, grad_expand = finish(
        (reduce_mine, reduce_theirs, expand_mine, expand_theirs),
        ((parts * rows_out, width), (rows_out, hidden_width)),
        [(0, 0, at * half, half, at * rows_out, 0) for at in range(parts)] + [(1, 1, 0, half_h, 0, 0)],
    )
    grad_cross_kv, grad_cross_out, grad_cross_q, grad_self_out = finish(
        (cross_mine, cross_theirs),
        ((rows_out, 2 * width), (rows_out, width), (rows_out, width), (rows_out, width)),
        [
            (0, 0, 0, width, 0, 0),
            (0, 1, width, half, 0, 0),
            (0, 2, width + half, half, 0, 0),
            (0, 3, 2 * width, half, 0, 0),
        ],
    )
    grad_self_in, small = finish(
        (self_mine, self_theirs),
        ((rows_out, 3 * width), (rows_out, LANES)),
        [(0, 0, width, half, 0, 0), (0, 0, 0, width, 0, width), (0, 1, width + half, LANES, 0, None)],
    )
    small = small.T
    statistics = jnp.sqrt(small[3:7, 0] / (small[7, 0] * width))
    grad_expand_bias = small[32:36].reshape(-1)

    return (
        f["out_a"],
        f["out_b"],
        *target_grads,
        *memory_grads,
        grad_self_in,
        small[24],
        small[25],
        grad_self_out,
        small[18],
        small[16],
        small[17],
        grad_cross_q,
        small[11],
        grad_cross_kv,
        small[12],
        grad_cross_out,
        small[10],
        small[8],
        small[9],
        grad_expand,
        grad_expand_bias,
        grad_reduce,
        small[2],
        small[0],
        small[1],
        statistics,
    )


def solution(mesh):
    split = P("tok", "rep", None)
    in_specs = (split,) * 6 + (P("tok"),) * 4 + (P(),) * 21
    out_specs = (split,) * 6 + (
        P("tok", None),
        P("tok"),
        P("tok"),
        P("tok", None),
        P("tok"),
        P("tok"),
        P("tok"),
        P("tok", None),
        P("tok"),
        P("tok", None),
        P("tok"),
        P("tok", None),
        P("tok"),
        P("tok"),
        P("tok"),
        P("tok", None),
        P("tok"),
        P("tok", None),
        P("tok"),
        P("tok"),
        P("tok"),
        P(),
    )
    return jax.shard_map(per_device, mesh=mesh, in_specs=in_specs, out_specs=out_specs, check_vma=False)
```

```python
import math

import jax
import jax.numpy as jnp
from jax import lax
from jax.experimental import pallas as pl
from jax.experimental.pallas import tpu as pltpu
from jax.sharding import PartitionSpec as P

HEADS = 12
HEAD_DIM = 64
LANES = 128
EPS = 1e-05
MASKED = -1e30
LIMIT = 62 * 1024 * 1024
ADD_LIMIT = 24 * 1024 * 1024

f32 = jnp.float32
bf16 = jnp.bfloat16

ANY = pl.BlockSpec(memory_space=pl.ANY)
VMEM = pl.BlockSpec(memory_space=pltpu.VMEM)
SMEM = pl.BlockSpec(memory_space=pltpu.SMEM)


def dot(a, b):
    return lax.dot_general(a, b, (((1,), (0,)), ((), ())), preferred_element_type=f32)


def dot_nt(a, b):
    return lax.dot_general(a, b, (((1,), (1,)), ((), ())), preferred_element_type=f32)


def dot_tn(a, b):
    return lax.dot_general(a, b, (((0,), (0,)), ((), ())), preferred_element_type=f32)


def shape(dims, dtype):
    return jax.ShapeDtypeStruct(dims, dtype)


def whole(ref):
    return ref


def columns(start, count):
    return lambda ref: ref.at[:, pl.ds(start, count)]


def rows(start, count):
    return lambda ref: ref.at[pl.ds(start, count)]


def first(ref):
    return ref.at[0]


def load(array):
    return Load(array.shape, array.dtype, [(array, whole, 0)])


class Load:
    def __init__(self, dims, dtype, pieces):
        self.dims = dims
        self.dtype = dtype
        self.pieces = pieces


class Split:
    def __init__(self, dims, dtype, count):
        self.shape = dims
        self.dtype = jnp.dtype(dtype)
        self.count = count

    def parts(self):
        return [shape((self.shape[0] // self.count, *self.shape[1:]), self.dtype)] * self.count


def parts_of(value):
    return value.parts() if isinstance(value, Split) else [value]


class Stage:
    def __init__(self, sems):
        self.sems = sems
        self.count = 0
        self.refs = {}
        self.loads = {}
        self.targets = {}
        self.sent = []

    def start(self, source, target):
        copy = pltpu.make_async_copy(source, target, self.sems.at[self.count])
        self.count += 1
        copy.start()
        return copy

    def __getitem__(self, name):
        for copy in self.loads.pop(name, ()):
            copy.wait()
        return self.refs[name]

    def __setitem__(self, name, value):
        self.refs[name][...] = value
        self.put(name)

    def put(self, name):
        targets = self.targets.pop(name, ())
        for index, target in enumerate(targets):
            source = self.refs[name]
            if len(targets) > 1:
                source = source.at[pl.ds(index * target.shape[0], target.shape[0])]
            self.sent.append(self.start(source, target))

    def finish(self):
        for name in list(self.targets):
            self.put(name)
        for name in list(self.loads):
            self[name]
        for copy in self.sent:
            copy.wait()


TIMES = {
    "forward": 27,
    "expand_grad": 7,
    "reduce_grad": 8,
    "cross_back": 16,
    "self_back": 8,
    "cross_grads": 100,
    "self_grads": 9,
    "add_step": 20,
}
SCALE = 0.02


def cost(name, weight=1.0):
    return pl.CostEstimate(flops=int(TIMES[name] * weight * SCALE * 1.15e9), bytes_accessed=1024, transcendentals=0)


def staged(name, body, loads, direct, outs, scratch):
    arrays = [piece[0] for value in loads.values() for piece in value.pieces]
    arrays += [value for value, unused in direct.values()]
    specs = [ANY] * sum(len(value.pieces) for value in loads.values())
    specs += [space for unused, space in direct.values()]
    buffers = {key: pltpu.VMEM(value.dims, value.dtype) for key, value in loads.items()}
    buffers.update({key: pltpu.VMEM(value.shape, value.dtype) for key, value in outs.items()})
    buffers.update({key: pltpu.VMEM(value.shape, value.dtype) for key, value in scratch.items()})
    results = [part for value in outs.values() for part in parts_of(value)]
    copies = sum(len(value.pieces) for value in loads.values()) + len(results)

    def kernel(*refs):
        refs = list(refs)
        stage = Stage(refs[-1])
        sources = {key: [refs.pop(0) for unused in value.pieces] for key, value in loads.items()}
        for key in direct:
            stage.refs[key] = refs.pop(0)
        for key, value in outs.items():
            stage.targets[key] = [refs.pop(0) for unused in parts_of(value)]
        for key in buffers:
            stage.refs[key] = refs.pop(0)
        for key, value in loads.items():
            stage.loads[key] = []
            for ref, (unused, pick, start) in zip(sources[key], value.pieces):
                source = pick(ref)
                target = stage.refs[key]
                if source.shape != target.shape:
                    target = target.at[pl.ds(start, source.shape[0])]
                stage.loads[key].append(stage.start(source, target))
        body(stage)
        stage.finish()

    values = pl.pallas_call(
        kernel,
        name=name,
        out_shape=results,
        in_specs=specs,
        out_specs=[ANY] * len(results),
        scratch_shapes=[*buffers.values(), pltpu.SemaphoreType.DMA((copies,))],
        compiler_params=pltpu.CompilerParams(vmem_limit_bytes=LIMIT),
        cost_estimate=cost(name),
    )(*arrays)
    values = list(values)
    return {
        key: [values.pop(0) for unused in parts_of(value)] if isinstance(value, Split) else values.pop(0)
        for key, value in outs.items()
    }


def row(ref):
    return ref[...].astype(f32).reshape(1, ref.shape[0])


def lane_heads():
    lane = lax.broadcasted_iota(jnp.int32, (1, LANES), 1)
    return (lane < HEAD_DIM, lane >= HEAD_DIM)


def only(mask, value):
    return jnp.where(mask, value, jnp.zeros_like(value))


def both_heads(heads, value):
    return jnp.concatenate([only(heads[0], value), only(heads[1], value)], axis=0)


def rejoin(heads, value):
    rows = value.shape[0] // 2
    return jnp.where(heads[0], value[:rows], value[rows:])


class Sizes:
    def __init__(self, long_local, short_local, width):
        self.a = long_local
        self.b = short_local
        self.own = long_local + short_local
        self.full = 2 * self.own
        self.width = width
        self.pairs = width // LANES
        self.buckets = ((0, self.a, 0), (self.a, self.b, 2 * self.a))

    def own_pieces(self, long_part, short_part, other_long=None, other_short=None):
        pieces = [(long_part, first, 0), (short_part, first, self.a)]
        if other_long is not None:
            pieces += [(other_long, first, self.own), (other_short, first, self.own + self.a)]
        return pieces

    def full_pieces(self, long_part, short_part, other_long, other_short):
        return [
            (long_part, first, 0),
            (other_long, first, self.a),
            (short_part, first, 2 * self.a),
            (other_short, first, 2 * self.a + self.b),
        ]


def key_positions(rows, core):
    at = lax.broadcasted_iota(jnp.int32, (2 * rows, 1), 0)
    return jnp.where(at < rows, core * rows + at, (1 - core) * rows + at - rows)


def query_positions(rows, core):
    at = lax.broadcasted_iota(jnp.int32, (1, 2 * rows), 1)
    return core * rows + jnp.where(at < rows, at, at - rows)


def softmax_columns(scores):
    raised = jnp.exp(scores - jnp.max(scores, axis=0, keepdims=True))
    return (raised * (1.0 / jnp.sum(raised, axis=0, keepdims=True))).astype(bf16)


def attend(size, q, k, v, bias, probs, out, live):
    heads = lane_heads()
    for start, rows, kstart in size.buckets:
        which = 0 if start == 0 else 1
        weights = []
        for pair in range(size.pairs):
            lanes = slice(pair * LANES, (pair + 1) * LANES)
            queries = both_heads(heads, q[start : start + rows, lanes])
            scores = dot_nt(k[kstart : kstart + 2 * rows, lanes], queries) + bias[which][...]
            weights.append(softmax_columns(scores))
            if rows >= LANES:
                finish_pair(size, v, probs, out, live, which, pair, weights.pop(), heads)
        for pair, value in enumerate(weights):
            finish_pair(size, v, probs, out, live, which, pair, value, heads)


def finish_pair(size, v, probs, out, live, which, pair, weights, heads):
    start, rows, kstart = size.buckets[which]
    lanes = slice(pair * LANES, (pair + 1) * LANES)
    probs[which][pair] = weights
    values = v[kstart : kstart + 2 * rows, lanes]
    context = by_query(heads, weights, values)
    out[start : start + rows, lanes] = jnp.where(live[which], context, 0.0).astype(bf16)


def by_query(heads, across, keyed):
    rows = across.shape[1] // 2
    if rows < LANES:
        return rejoin(heads, dot_tn(across, keyed))
    feature = lax.broadcasted_iota(jnp.int32, (LANES, 1), 0)
    turned = dot(keyed.T, across)
    return jnp.where(feature < HEAD_DIM, turned[:, :rows], turned[:, rows:]).T


def head_sums(product):
    rows = product.shape[0]
    if rows < LANES:
        turned = jnp.concatenate([product, product], axis=0).T
        lane = lax.broadcasted_iota(jnp.int32, (1, LANES), 1)
        low = jnp.sum(turned[:HEAD_DIM], axis=0, keepdims=True)
        high = jnp.sum(turned[HEAD_DIM:], axis=0, keepdims=True)
        return jnp.where(lane < rows, low, high)
    turned = product.T
    low = jnp.sum(turned[:HEAD_DIM], axis=0, keepdims=True)
    high = jnp.sum(turned[HEAD_DIM:], axis=0, keepdims=True)
    return jnp.concatenate([low, high], axis=1)


def attend_back(size, q, k, v, probs, context, grad, dq, dk, dv, scaling):
    heads = lane_heads()
    for which, (start, rows, kstart) in enumerate(size.buckets):
        held = []

        def finish(pair, weights, grads, dscores):
            lanes = slice(pair * LANES, (pair + 1) * LANES)
            at = slice(start, start + rows)
            keys = slice(kstart, kstart + 2 * rows)
            dk[keys, lanes] = dot(dscores, both_heads(heads, q[at, lanes])).astype(bf16)
            dv[keys, lanes] = dot(weights, grads).astype(bf16)
            dq[at, lanes] = (by_query(heads, dscores, k[keys, lanes]) * scaling).astype(bf16)

        for pair in range(size.pairs):
            lanes = slice(pair * LANES, (pair + 1) * LANES)
            at = slice(start, start + rows)
            weights = probs[which][pair]
            grads = grad[at, lanes]
            centred = head_sums(grads.astype(f32) * context[at, lanes].astype(f32))
            grads = both_heads(heads, grads)
            dprobs = dot_nt(v[kstart : kstart + 2 * rows, lanes], grads)
            dscores = (weights.astype(f32) * (dprobs - centred)).astype(bf16)
            if rows >= LANES:
                finish(pair, weights, grads, dscores)
            else:
                held.append((pair, weights, grads, dscores))
        for item in held:
            finish(*item)


def norm_parts(tensor):
    centre = tensor - jnp.mean(tensor, axis=-1, keepdims=True)
    rstd = lax.rsqrt(jnp.mean(centre * centre, axis=-1, keepdims=True) + EPS)
    return centre * rstd, rstd


def norm_back(normed, rstd, gain, gradient):
    scaled = gradient * gain
    inner = scaled - jnp.mean(scaled, axis=-1, keepdims=True)
    inner = inner - normed * jnp.mean(scaled * normed, axis=-1, keepdims=True)
    return inner * rstd


def column_sum(tensor):
    return jnp.sum(tensor.astype(f32), axis=0, keepdims=True)


def live_column(rows, core, length):
    return core * rows + lax.broadcasted_iota(jnp.int32, (rows, 1), 0) < length


def forward_body(size, hidden_width, scaling, g):
    core = lax.axis_index("rep")
    a, b, own, width = size.a, size.b, size.own, size.width
    target_len = (g["target_len_a"][0], g["target_len_b"][0])
    memory_len = (g["memory_len_a"][0], g["memory_len_b"][0])
    live = (live_column(a, core, target_len[0]), live_column(b, core, target_len[1]))
    live_all = jnp.concatenate(live, axis=0)
    bias = (g["bias_a"], g["bias_b"])
    context, mixed, low1 = (columns_of(g["ship3"], at * width, width) for at in range(3))
    low2, inner_send = columns_of(g["ship1"], 0, width), columns_of(g["ship1"], width, hidden_width // 2)
    hidden, ffn_send = columns_of(g["ship2"], 0, hidden_width), columns_of(g["ship2"], hidden_width, width // 2)
    for which, rows in enumerate((a, b)):
        at = key_positions(rows, core)
        allowed = (at < target_len[which]) & (at <= query_positions(rows, core))
        bias[which][...] = jnp.where(allowed, 0.0, MASKED)
    xo = g["xo"]
    g["q"] = ((dot(xo[...], g["w_q"][...]) + row(g["qbias"])).astype(bf16) * scaling).astype(bf16)
    xf = g["xf"]
    g["k"] = dot(xf[...], g["w_k"][...]).astype(bf16)
    g["v"] = (dot(xf[...], g["w_v"][...]) + row(g["vbias"])).astype(bf16)
    attend(size, g["q"], g["k"], g["v"], bias, (g["ps_a"], g["ps_b"]), context, live)
    for name in ("ps_a", "ps_b"):
        g.put(name)
    mf, w_ckv = g["mf"], g["w_ckv"]
    g["ck"] = dot(mf[...], w_ckv[:, :width]).astype(bf16)
    g["cv"] = (dot(mf[...], w_ckv[:, width:]) + row(g["cvbias"])).astype(bf16)

    def squares(tensor):
        kept = jnp.where(live_all, tensor * tensor, 0.0)
        return jnp.sum(jnp.sum(kept, axis=0, keepdims=True), axis=1, keepdims=True)

    branch = g["branch"]
    self_branch = dot(context[...], g["w_out"][...]) + row(g["obias"])
    square_self = squares(self_branch)
    normed, rstd = norm_parts(xo[...].astype(f32) + self_branch)
    g["n1"] = normed
    g["r1"] = rstd
    after_self = normed * row(g["gain1"]) + row(g["shift1"])
    low1[...] = after_self.astype(bf16)
    branch[...] = after_self
    query = dot(low1[...], g["w_cq"][...]) + row(g["cqbias"])
    g["cq"] = (query.astype(bf16) * scaling).astype(bf16)
    for which, rows in enumerate((a, b)):
        allowed = key_positions(rows, core) < memory_len[which]
        bias[which][...] = jnp.broadcast_to(jnp.where(allowed, 0.0, MASKED), bias[which].shape)
    attend(size, g["cq"], g["ck"], g["cv"], bias, (g["pc_a"], g["pc_b"]), mixed, live)
    for name in ("pc_a", "pc_b", "ship3"):
        g.put(name)
    cross_branch = dot(mixed[...], g["w_cout"][...]) + row(g["cobias"])
    square_cross = squares(cross_branch)
    normed, rstd = norm_parts(branch[...] + cross_branch)
    g["n2"] = normed
    g["r2"] = rstd
    after_cross = normed * row(g["gain2"]) + row(g["shift2"])
    low2[...] = after_cross.astype(bf16)
    branch[...] = after_cross
    third, slope = g["third"], g["slope"]
    w_exp, w_red = g["w_exp"], g["w_red"]
    eb = row(g["ebias"])
    total = None
    for step in range(hidden_width // width):
        cols = slice(step * width, (step + 1) * width)
        act = dot(low2[...], w_exp[:, cols]) + eb[:, cols]
        phi = 0.5 * (1.0 + lax.erf(act * (1.0 / math.sqrt(2.0))))
        hidden[:, cols] = (act * phi).astype(bf16)
        density = jnp.exp(-0.5 * act * act) * (1.0 / math.sqrt(2.0 * math.pi))
        slope[:, cols] = (phi + act * density).astype(bf16)
        part = dot(hidden[:, cols], w_red[cols, :])
        if step == 0:
            third[...] = part
        else:
            third[...] += part
    ffn_branch = third[...] + row(g["rbias"])
    square_ffn = squares(ffn_branch)
    normed, rstd = norm_parts(branch[...] + ffn_branch)
    gain = row(g["gain3"])
    final = normed * gain + row(g["shift3"])
    square_final = squares(final)
    low = final.astype(bf16)
    g["out_a"] = low[:a][None]
    g["out_b"] = low[a:][None]
    gradient = jnp.where(live_all, g["cot"][...].astype(f32), 0.0)
    d_third = norm_back(normed, rstd, gain, gradient)
    g["third"] = d_third
    d_ffn = d_third.astype(bf16)
    dffn = g["dffn"]
    dffn[...] = d_ffn
    half = width // 2
    g["ffn_keep"] = dffn[:, half_of(core, half)]
    ffn_send[...] = dffn[:, half_of(1 - core, half)]
    g.put("ship2")
    sums = g["sums"]
    sums[0:1] = column_sum(gradient * normed)
    sums[1:2] = column_sum(gradient)
    sums[2:3] = column_sum(d_ffn)
    count = jnp.sum(jnp.where(live_all, 1.0, 0.0), axis=0, keepdims=True)
    for at, value in enumerate((square_final, square_self, square_cross, square_ffn, count)):
        sums[3 + at : 4 + at] = jnp.broadcast_to(value, (1, width))
    g.put("sums")
    half = hidden_width // 2
    for side in (1 - core, core):
        for at, start in enumerate(range(0, half, width)):
            cols = pl.ds(pl.multiple_of(side * half + start, LANES), width)
            grad = dot_nt(dffn[...], w_red[cols, :]) * slope[:, cols].astype(f32)
            low = grad.astype(bf16)
            g["inner_sum"][:, cols] = column_sum(low)
            if side is core:
                g["inner_keep%d" % at] = low
            else:
                inner_send[:, pl.ds(start, width)] = low
        g.put("ship1")


def columns_of(ref, start, count):
    return ref.at[:, pl.ds(start, count)]


def half_of(core, half):
    return pl.ds(pl.multiple_of(core * half, LANES), half)


def run_forward(size, hidden_width, scaling, lengths, own, other, cots, weights, vectors):
    a, b, n, t, w, h = size.a, size.b, size.own, size.full, size.width, hidden_width
    w_in, w_out, w_cq, w_ckv, w_cout, w_exp, w_red = weights
    loads = {
        "xo": Load((n, w), bf16, size.own_pieces(own[0], own[1])),
        "w_q": Load((w, w), bf16, [(w_in, columns(0, w), 0)]),
        "xf": Load((t, w), bf16, size.full_pieces(own[0], own[1], other[0], other[1])),
        "w_k": Load((w, w), bf16, [(w_in, columns(w, w), 0)]),
        "w_v": Load((w, w), bf16, [(w_in, columns(2 * w, w), 0)]),
        "mf": Load((t, w), bf16, size.full_pieces(own[2], own[3], other[2], other[3])),
        "w_ckv": load(w_ckv),
        "w_out": load(w_out),
        "w_cq": load(w_cq),
        "w_cout": load(w_cout),
        "w_exp": load(w_exp),
        "w_red": load(w_red),
        "cot": Load((n, w), bf16, size.own_pieces(cots[0], cots[1])),
    }
    names = ("qbias", "vbias", "obias", "gain1", "shift1", "cqbias", "cvbias", "cobias", "gain2", "shift2")
    names += ("ebias", "rbias", "gain3", "shift3")
    direct = dict(zip(("target_len_a", "target_len_b", "memory_len_a", "memory_len_b"), ((v, SMEM) for v in lengths)))
    direct.update(zip(names, ((v, VMEM) for v in vectors)))
    square = shape((n, w), bf16)
    keys = shape((t, w), bf16)
    outs = {
        "out_a": shape((1, a, w), bf16),
        "out_b": shape((1, b, w), bf16),
        "q": square,
        "k": keys,
        "v": keys,
        "cq": square,
        "ck": keys,
        "cv": keys,
        "ps_a": shape((size.pairs, 2 * a, 2 * a), bf16),
        "ps_b": shape((size.pairs, 2 * b, 2 * b), bf16),
        "pc_a": shape((size.pairs, 2 * a, 2 * a), bf16),
        "pc_b": shape((size.pairs, 2 * b, 2 * b), bf16),
        "ship1": shape((n, w + h // 2), bf16),
        "ship2": shape((n, h + w // 2), bf16),
        "ship3": shape((n, 3 * w), bf16),
        "n1": shape((n, w), f32),
        "r1": shape((n, 1), f32),
        "n2": shape((n, w), f32),
        "r2": shape((n, 1), f32),
        "third": shape((n, w), f32),
        "ffn_keep": shape((n, w // 2), bf16),
        "sums": shape((8, w), f32),
        "inner_keep0": square,
        "inner_keep1": square,
        "inner_sum": shape((1, h), f32),
    }
    scratch = {
        "bias_a": shape((2 * a, 2 * a), f32),
        "bias_b": shape((2 * b, 2 * b), f32),
        "branch": shape((n, w), f32),
        "slope": shape((n, h), bf16),
        "dffn": square,
    }
    return staged(
        "forward",
        lambda g: forward_body(size, hidden_width, scaling, g),
        loads,
        direct,
        outs,
        scratch,
    )


def split_partial(size, core, dk, dv, keep, send):
    a, b = size.a, size.b
    moves = ((0, a, a), (a, 0, a), (2 * a, 2 * a + b, b), (2 * a + b, 2 * a, b))
    for here, (stay, leave) in ((0, (dk, dv)), (1, (dv, dk))):

        @pl.when(core == here)
        def unused(stay=stay, leave=leave):
            keep[...] = stay[...]
            for target, source, rows in moves:
                send[pl.ds(target, rows)] = leave[pl.ds(source, rows)]


def through_norm(size, g, gradient, normed, rstd, gain, w_out, sums, back):
    normed = g[normed][...]
    d_sum = norm_back(normed, g[rstd][...], row(g[gain]), gradient)
    sums[0:1] = column_sum(gradient * normed)
    sums[1:2] = column_sum(gradient)
    low = d_sum.astype(bf16)
    sums[2:3] = column_sum(low)
    g["branch"][...] = low
    back[...] = dot_nt(low, g[w_out][...]).astype(bf16)
    return d_sum


def send_halves(core, value, keep, send, at, half):
    keep[:, at * half : (at + 1) * half] = value[:, half_of(core, half)]
    send[:, at * half : (at + 1) * half] = value[:, half_of(1 - core, half)]


def cross_body(size, scaling, parts, g):
    core = lax.axis_index("rep")
    half = size.width // 2
    keep = g["half_keep"]
    send, part_send = g["ship_half"], g["ship_part"]
    sums, sums2 = g["sums"].at[pl.ds(0, 8)], g["sums"].at[pl.ds(8, 8)]
    g["sums"][...] = jnp.zeros_like(g["sums"])
    gradient = g["third"][...]
    for index in range(parts):
        gradient = gradient + dot_nt(g["inner%d" % index][...], g["w_exp%d" % index][...])
    g["mid"][...] = through_norm(size, g, gradient, "n2", "r2", "gain2", "w_cout", sums, g["back"])
    send_halves(core, g["branch"], keep, send, 0, half)
    attend_back(
        size, g["cq"], g["ck"], g["cv"], (g["pc_a"], g["pc_b"]), g["mixed"], g["back"], g["dq"], g["dk"], g["dv"], scaling
    )
    send_halves(core, g["dq"], keep, send, 1, half)
    g.put("ship_half")
    split_partial(size, core, g["dk"], g["dv"], g["part_keep"], part_send)
    g.put("ship_part")
    g.put("part_keep")
    gradient = g["mid"][...] + dot_nt(g["dq"][...], g["w_cq"][...])
    g["low"] = through_norm(size, g, gradient, "n1", "r1", "gain1", "w_out", sums2, g["dcontext"])
    g.put("dcontext")
    keep[:, 2 * half :] = g["branch"][:, half_of(core, half)]
    g["ship_self"] = g["branch"][:, half_of(1 - core, half)]
    g.put("half_keep")
    sums[3:4] = column_sum(g["dq"][...])
    sums[4:5] = column_sum(g["dv"][...])


def run_cross(size, scaling, f, ship3, third, weights, gains):
    n, t, w = size.own, size.full, size.width
    w_exp, w_cout, w_cq, w_out = weights
    loads = {
        "third": load(third),
    }
    parts = w_exp.shape[1] // w

    def column_part(index):
        def pick(ref):
            core = lax.axis_index("rep")
            side = core if index < 2 else 1 - core
            return ref.at[:, pl.ds(pl.multiple_of((2 * side + index % 2) * w, LANES), w)]

        return Load((w, w), bf16, [(w_exp, pick, 0)])

    for index in range(parts):
        source = (f["inner_keep%d" % index], whole, 0) if index < 2 else (f["ship1"], columns((index - 1) * w, w), 0)
        loads["inner%d" % index] = Load((n, w), bf16, [source])
        loads["w_exp%d" % index] = column_part(index)
    loads |= {
        "n2": load(f["n2"]),
        "r2": load(f["r2"]),
        "w_cout": load(w_cout),
        "mixed": Load((n, w), bf16, [(ship3, columns(w, w), 0)]),
        "cv": load(f["cv"]),
        "pc_a": load(f["pc_a"]),
        "cq": load(f["cq"]),
        "ck": load(f["ck"]),
        "pc_b": load(f["pc_b"]),
        "w_cq": load(w_cq),
        "n1": load(f["n1"]),
        "r1": load(f["r1"]),
        "w_out": load(w_out),
    }
    square = shape((n, w), bf16)
    keys = shape((t, w), bf16)
    return staged(
        "cross_back",
        lambda g: cross_body(size, scaling, parts, g),
        loads,
        {"gain2": (gains[0], VMEM), "gain1": (gains[1], VMEM)},
        {
            "low": shape((n, w), f32),
            "dcontext": square,
            "half_keep": shape((n, 3 * (w // 2)), bf16),
            "ship_half": square,
            "ship_self": shape((n, w // 2), bf16),
            "part_keep": keys,
            "ship_part": Split((t, w), bf16, PIECES),
            "sums": shape((16, w), f32),
        },
        {"branch": square, "back": square, "dq": square, "dk": keys, "dv": keys, "mid": shape((n, w), f32)},
    )


def self_body(size, scaling, g):
    core = lax.axis_index("rep")
    half = size.width // 2
    send, part_send = g["ship_half"], g["ship_part"]
    sums = g["sums"]
    sums[...] = jnp.zeros_like(sums)
    attend_back(
        size, g["q"], g["k"], g["v"], (g["ps_a"], g["ps_b"]), g["context"], g["dcontext"], g["dq"], g["dk"], g["dv"], scaling
    )
    g.put("dq")
    split_partial(size, core, g["dk"], g["dv"], g["part_keep"], part_send)
    g.put("ship_part")
    send_halves(core, g["dq"], g["half_keep"], send, 0, half)
    g.put("ship_half")
    g.put("part_keep")
    g.put("half_keep")
    sums[0:1] = column_sum(g["dq"][...])
    sums[1:2] = column_sum(g["dv"][...])


def run_self(size, scaling, f, ship3, dcontext):
    n, t, w = size.own, size.full, size.width
    loads = {
        "dcontext": load(dcontext),
        "context": Load((n, w), bf16, [(ship3, columns(0, w), 0)]),
        "v": load(f["v"]),
        "ps_a": load(f["ps_a"]),
        "q": load(f["q"]),
        "k": load(f["k"]),
        "ps_b": load(f["ps_b"]),
    }
    square = shape((n, w), bf16)
    keys = shape((t, w), bf16)
    return staged(
        "self_back",
        lambda g: self_body(size, scaling, g),
        loads,
        {},
        {
            "dq": square,
            "half_keep": shape((n, w // 2), bf16),
            "ship_half": Split((n, w // 2), bf16, 1),
            "part_keep": keys,
            "ship_part": Split((t, w), bf16, PIECES),
            "sums": shape((8, w), f32),
        },
        {"dk": keys, "dv": keys},
    )


PIECES = 2
BLOCKS = 16
STAGES = 4
ORDER_XZY = (0, 2, 3, 1)
ORDER_YXZ = (1, 0, 2, 3)
ORDER_ZXY = (2, 3, 0, 1)


class Scatter:
    def __init__(self, order, me, keep, send, rows):
        self.order = order
        self.me = me
        self.keep = keep
        self.send = send
        self.rows = rows

    def store(self, block, value, start, count):
        distance = self.me ^ block
        place = 0
        for stage, bit in enumerate(self.order):
            place = place + (((distance >> bit) & 1) << (STAGES - 1 - stage))
        low = place < BLOCKS // 2
        at = pl.multiple_of(jnp.where(low, place, place - BLOCKS // 2) * self.rows, 16)
        rows = pl.ds(at, self.rows)
        cols = slice(start, start + count)

        @pl.when(low)
        def unused():
            self.keep[rows, cols] = value.astype(bf16)

        @pl.when(jnp.logical_not(low))
        def unused_too():
            self.send[rows, cols] = value.astype(bf16)

    def store_all(self, product, start):
        for block in range(BLOCKS):
            self.store(block, product[block * self.rows : (block + 1) * self.rows], start, product.shape[1])


def my_block(group):
    return lax.axis_index("tok") // group


def chunk_outs(size, columns, names):
    rows = size.width // 2
    return {name: shape((rows, columns), bf16) for name in names}


def expand_body(size, group, g):
    scatter = Scatter(ORDER_XZY, my_block(group), g["keep"], g["send"], size.width // BLOCKS)
    for at in range(2):
        scatter.store_all(dot_tn(g["low"][...], g["d%d" % at][...]), at * size.width)
    g.put("send")


def run_expand_grad(size, group, ship, ship_other, keeps):
    n, t, w = size.own, size.full, size.width
    loads = {"low": Load((t, w), bf16, [(ship, columns(0, w), 0), (ship_other, columns(0, w), n)])}
    for at, keep in enumerate(keeps):
        loads["d%d" % at] = Load((t, w), bf16, [(keep, whole, 0), (ship_other, columns(w + at * w, w), n)])
    return staged(
        "expand_grad",
        lambda g: expand_body(size, group, g),
        loads,
        {},
        chunk_outs(size, 2 * w, ("keep", "send")),
        {},
    )


def reduce_chunk(group, index):
    return (my_block(group) >> 2) ^ (1, 3, 0, 2)[index]


def reduce_body(size, group, g):
    count = size.width // BLOCKS
    half = size.width // 2
    parts = BLOCKS // 4
    mine = my_block(group) & 3
    for index in range(4):
        target = g["send"] if index < 2 else g["keep"]
        product = dot_tn(g["hidden%d" % index][...], g["d"][...])
        for block in range(4):
            distance = mine ^ block
            place = (index % 2) * 4 + ((distance & 1) << 1) + (distance >> 1)
            at = pl.ds(pl.multiple_of(place * count, 16), count)
            for part in range(parts):
                start = (block * parts + part) * count
                target[at, part * half : (part + 1) * half] = product[start : start + count].astype(bf16)
        if index % 2 == 1:
            g.put("send" if index < 2 else "keep")


def run_reduce_grad(size, group, ship, ship_other, keep):
    n, t, w = size.own, size.full, size.width
    half = keep.shape[1]
    h = ship.shape[1] - half
    quarter = h // 4

    def chunk(index):
        def pick(ref):
            return ref.at[:, pl.ds(pl.multiple_of(reduce_chunk(group, index) * quarter, LANES), quarter)]

        return Load((t, quarter), bf16, [(ship, pick, 0), (ship_other, pick, n)])

    loads = {"d": Load((t, half), bf16, [(keep, whole, 0), (ship_other, columns(h, half), n)])}
    loads.update({"hidden%d" % index: chunk(index) for index in range(4)})
    return staged(
        "reduce_grad",
        lambda g: reduce_body(size, group, g),
        loads,
        {},
        chunk_outs(size, h // 2, ("send", "keep")),
        {},
    )


def projection_share(size, g, scatter):
    a, b = size.a, size.b
    total = g["total"]
    total[...] = (g["part_keep"][...].astype(f32) + g["part_recv"][...].astype(f32)).astype(bf16)
    scatter.store_all(dot_tn(g["source"][...], total[...]), 0)
    g.put("send")
    share = dot_nt(total[...], g["weight"][...])
    g["grad_send"][pl.ds(0, a)] = share[a : 2 * a].astype(bf16)
    g["grad_send"][pl.ds(a, b)] = share[2 * a + b :].astype(bf16)
    g["grad_own"][pl.ds(0, a)] = share[:a]
    g["grad_own"][pl.ds(a, b)] = share[2 * a : 2 * a + b]


def cross_grad_body(size, group, g):
    width = size.width
    half = width // 2
    scatter = Scatter(ORDER_YXZ, my_block(group), g["keep"], g["send"], width // BLOCKS)
    for at, name in enumerate(("mixed", "low1")):
        cols = slice(at * half, (at + 1) * half)
        scatter.store_all(dot_tn(g[name][...], g["halves"][:, cols]), width + at * half)
    scatter.store_all(dot_tn(g["context"][...], g["halves_self"][...]), 2 * width)
    projection_share(size, g, scatter)
    g.put("keep")
    g.put("grad_send")


def stacked(arrays, start):
    return [(array, whole, start + index * array.shape[0]) for index, array in enumerate(arrays)]


def my_columns(weight, width):
    skip = weight.shape[1] - 2 * width

    def pick(ref):
        return ref.at[:, pl.ds(pl.multiple_of(skip + lax.axis_index("rep") * width, LANES), width)]

    return Load((width, width), bf16, [(weight, pick, 0)])


def run_cross_grads(size, group, ship3, ship3_other, half_keep, half_recv, part_keep, part_recv, sources, weight):
    n, t, w = size.own, size.full, size.width

    def both(at):
        return Load((t, w), bf16, [(ship3, columns(at * w, w), 0), (ship3_other, columns(at * w, w), n)])

    half = w // 2
    outs = chunk_outs(size, w + 3 * half, ("keep", "send"))
    outs["grad_own"] = shape((n, w), f32)
    outs["grad_send"] = shape((n, w), bf16)
    return staged(
        "cross_grads",
        lambda g: cross_grad_body(size, group, g),
        {
            "mixed": both(1),
            "halves": Load((t, 2 * half), bf16, [(half_keep, columns(0, 2 * half), 0), (half_recv[0], whole, n)]),
            "low1": both(2),
            "context": both(0),
            "halves_self": Load((t, half), bf16, [(half_keep, columns(2 * half, half), 0), (half_recv[1], whole, n)]),
            "part_keep": load(part_keep),
            "part_recv": Load((t, w), bf16, stacked(part_recv, 0)),
            "source": Load((t, w), bf16, size.full_pieces(*sources)),
            "weight": my_columns(weight, w),
        },
        {},
        outs,
        {"total": shape((t, w), bf16)},
    )


def regroup(value, width, count):
    parts = value.shape[1] // width
    lane = lax.broadcasted_iota(jnp.int32, (1, width), 1)
    rows_out = [jnp.zeros((1, width), f32)] * parts
    for step in range(parts):
        piece = value[:, step * width : (step + 1) * width]
        for at in range(width // count):
            device, part = divmod(step * (width // count) + at, parts)
            moved = pltpu.roll(piece, ((device - at) * count) % width, 1)
            mine = (lane >= device * count) & (lane < (device + 1) * count)
            rows_out[part] = jnp.where(mine, moved, rows_out[part])
    return jnp.concatenate(rows_out, axis=0)


def self_grad_body(size, group, sums, g):
    width = size.width
    half = width // 2
    count = width // BLOCKS
    scatter = Scatter(ORDER_YXZ, my_block(group), g["keep"], g["send"], count)
    held = g["rows"]
    held[...] = jnp.zeros_like(held)
    at = 0
    for name in sums:
        value = g[name][...]
        if value.shape[1] > width:
            value = regroup(value, width, count)
        held[pl.ds(at, value.shape[0])] = value
        at += value.shape[0]
    scatter.store_all(jnp.transpose(held[...]), width + half)
    scatter.store_all(dot_tn(g["lhs"][...], g["halves"][...]), width)
    projection_share(size, g, scatter)
    g.put("keep")
    g.put("grad_send")
    g["grad_own"][...] += g["low"][...] + dot_nt(g["dq"][...], g["w_q"][...])


def run_self_grads(size, group, half_keep, half_recv, part_keep, part_recv, sources, weight, low, dq, sums):
    n, t, w = size.own, size.full, size.width
    half = w // 2
    loads = {key: load(value) for key, value in sums.items()}
    loads.update(
        part_keep=load(part_keep),
        part_recv=Load((t, w), bf16, stacked(part_recv, 0)),
        source=Load((t, w), bf16, size.full_pieces(*sources)),
        weight=my_columns(weight, w),
        lhs=Load((t, w), bf16, size.own_pieces(*sources)),
        halves=Load((t, half), bf16, [(half_keep, whole, 0), *stacked(half_recv, n)]),
        dq=load(dq),
        w_q=Load((w, w), bf16, [(weight, columns(0, w), 0)]),
        low=load(low),
    )
    outs = chunk_outs(size, w + half + LANES, ("keep", "send"))
    outs["grad_own"] = shape((n, w), f32)
    outs["grad_send"] = shape((n, w), bf16)
    return staged(
        "self_grads",
        lambda g: self_grad_body(size, group, tuple(sums), g),
        loads,
        {},
        outs,
        {"total": shape((t, w), bf16), "rows": shape((LANES, w), f32)},
    )


def swap(value):
    return lax.ppermute(value, "rep", [(0, 1), (1, 0)])


class Line:
    def __init__(self):
        self.last = None

    def wait(self, *values):
        if self.last is None:
            return values
        return lax.optimization_barrier((*values, self.last))[:-1]

    def record(self, value):
        self.last = value


def add_step(pairs, weight=1.0):
    rows = pairs[0][0].shape[0] // 2
    columns = sum(keep.shape[1] for keep, unused in pairs)

    def kernel(*refs):
        keep_out, send_out = refs[-2:]
        at = 0
        for index in range(len(pairs)):
            keep, received = refs[2 * index], refs[2 * index + 1]
            cols = slice(at, at + keep.shape[1])
            at += keep.shape[1]
            total = (keep[...].astype(f32) + received[...].astype(f32)).astype(bf16)
            keep_out[:, cols] = total[:rows]
            send_out[:, cols] = total[rows:]

    flat = [value for pair in pairs for value in pair]
    return pl.pallas_call(
        kernel,
        name="add_step",
        out_shape=[shape((rows, columns), bf16)] * 2,
        in_specs=[VMEM] * len(flat),
        out_specs=[VMEM] * 2,
        compiler_params=pltpu.CompilerParams(vmem_limit_bytes=ADD_LIMIT),
        cost_estimate=cost("add_step", weight),
    )(*flat)


def add_last(keep, received, weight=1.0):
    def kernel(keep, received, out):
        out[...] = (keep[...].astype(f32) + received[...].astype(f32)).astype(bf16)

    return pl.pallas_call(
        kernel,
        name="add_last",
        out_shape=shape(keep.shape, bf16),
        in_specs=[VMEM] * 2,
        out_specs=VMEM,
        compiler_params=pltpu.CompilerParams(vmem_limit_bytes=ADD_LIMIT),
        cost_estimate=cost("add_step", weight),
    )(keep, received)


class Chunk:
    def __init__(self, keep, send, order, group, stage=0):
        self.keep = keep
        self.order = order
        self.group = group
        self.stage = stage
        self.begin(send)

    def begin(self, send):
        devices = lax.axis_size("tok")
        bit = self.group << self.order[self.stage]
        self.received = lax.ppermute(send, "tok", [(i, i ^ bit) for i in range(devices)])

    def launch(self, line):
        (send,) = line.wait(self.send)
        self.begin(send)

    def step(self, line, weight=1.0):
        self.absorb(line, weight)
        if self.stage < STAGES:
            self.begin(self.send)

    def absorb(self, line, weight=1.0):
        keep, received = line.wait(self.keep, self.received)
        self.stage += 1
        if self.stage == STAGES:
            self.total = add_last(keep, received, weight)
            line.record(self.total)
            return
        self.keep, self.send = add_step([(keep, received)], weight)
        line.record(self.keep)


def spread(total, group):
    if group == 1:
        return total
    devices = lax.axis_size("tok")
    sets = [[start + i for i in range(group)] for start in range(0, devices, group)]
    total = lax.psum_scatter(total.astype(f32), "tok", scatter_dimension=0, tiled=True, axis_index_groups=sets)
    return total.astype(bf16)


def spread_blocks(total, group, parts):
    if group == 1:
        return total
    wide = total.shape[1] // parts
    rows_in = jnp.concatenate([total[:, at * wide : (at + 1) * wide] for at in range(parts)], axis=0)
    rows_in = spread(rows_in, group)
    count = rows_in.shape[0] // parts
    return jnp.concatenate([rows_in[at * count : (at + 1) * count] for at in range(parts)], axis=1)


def merge(line, *chunks):
    values = line.wait(*[value for chunk in chunks for value in (chunk.keep, chunk.received)])
    keep, send = add_step(list(zip(values[::2], values[1::2])))
    line.record(keep)
    return Chunk(keep, send, chunks[0].order, chunks[0].group, chunks[0].stage + 1)


def add_tokens(size, *values):
    a, b, w = size.a, size.b, size.width

    def kernel(*refs):
        for at in range(2):
            own, received = refs[2 * at : 2 * at + 2]
            long_out, short_out = refs[4 + 2 * at : 6 + 2 * at]
            long_out[0] = (own[:a] + received[:a].astype(f32)).astype(bf16)
            short_out[0] = (own[a:] + received[a:].astype(f32)).astype(bf16)

    outs = pl.pallas_call(
        kernel,
        name="add_tokens",
        out_shape=[shape((1, a, w), bf16), shape((1, b, w), bf16)] * 2,
        in_specs=[VMEM] * 4,
        out_specs=[VMEM] * 4,
        compiler_params=pltpu.CompilerParams(vmem_limit_bytes=ADD_LIMIT),
        cost_estimate=cost("add_step", 0.0),
    )(*values)
    return outs[:2], outs[2:]


SMALL_ROWS = (24, 25, 18, 16, 17, 11, 12, 10, 8, 9, 2, 0, 1)


def finish_small(mine, theirs, width, start):
    rows_out = mine.shape[0]
    outs = [shape((rows_out,), f32)] * len(SMALL_ROWS) + [shape((4 * rows_out,), f32), shape((4,), f32)]

    def kernel(mine, theirs, *refs):
        cols = slice(start, start + LANES)
        total = mine[:, cols].astype(f32) + theirs[:, cols].astype(f32)
        turned = total.T
        for ref, at in zip(refs, SMALL_ROWS):
            ref[...] = turned[at : at + 1].reshape(rows_out)
        refs[-2][...] = jnp.concatenate([turned[at : at + 1] for at in range(32, 36)], axis=1).reshape(4 * rows_out)
        line = total[0:1]
        refs[-1][...] = jnp.sqrt(line[:, 3:7] / (line[:, 7:8] * width)).reshape(4)

    return pl.pallas_call(
        kernel,
        name="finish_small",
        out_shape=outs,
        in_specs=[VMEM] * 2,
        out_specs=[VMEM] * len(outs),
        compiler_params=pltpu.CompilerParams(vmem_limit_bytes=ADD_LIMIT),
        cost_estimate=cost("add_step"),
    )(mine, theirs)


def finish(pairs, dims, moves):
    outs = [shape(value, f32) for value in dims]

    def kernel(*refs):
        core = lax.axis_index("rep")
        for pair, out, start, count, row_at, column in moves:
            mine, theirs = refs[2 * pair], refs[2 * pair + 1]
            target = refs[len(pairs) + out]
            at = slice(row_at, row_at + mine.shape[0])
            cols = slice(start, start + count)
            if column is None:
                target[at, :] = mine[:, cols].astype(f32) + theirs[:, cols].astype(f32)
                continue
            for ref, side in ((mine, core), (theirs, 1 - core)):
                target[at, pl.ds(pl.multiple_of(column + side * count, LANES), count)] = ref[:, cols].astype(f32)

    return pl.pallas_call(
        kernel,
        name="finish",
        out_shape=outs,
        in_specs=[VMEM] * len(pairs),
        out_specs=[VMEM] * len(outs),
        compiler_params=pltpu.CompilerParams(vmem_limit_bytes=ADD_LIMIT),
        cost_estimate=cost("add_step"),
    )(*pairs)


def per_device(*args):
    (
        long_target,
        short_target,
        long_memory,
        short_memory,
        long_cot,
        short_cot,
        long_target_len,
        short_target_len,
        long_memory_len,
        short_memory_len,
        self_inproj,
        self_qbias,
        self_vbias,
        self_outproj,
        self_obias,
        first_gain,
        first_shift,
        cross_qproj,
        cross_qbias,
        cross_kvproj,
        cross_vbias,
        cross_outproj,
        cross_obias,
        second_gain,
        second_shift,
        expand_weight,
        expand_bias,
        reduce_weight,
        reduce_bias,
        final_gain,
        final_shift,
    ) = args
    core = lax.axis_index("rep")
    devices = lax.axis_size("tok")
    group = devices // BLOCKS
    width = long_target.shape[2]
    hidden_width = expand_weight.shape[1]
    size = Sizes(long_target.shape[1], short_target.shape[1], width)
    n = size.own
    scaling = 1.0 / math.sqrt(HEAD_DIM)
    own = (long_target, short_target, long_memory, short_memory)
    other = tuple(swap(value) for value in own)
    f = run_forward(
        size,
        hidden_width,
        scaling,
        (long_target_len, short_target_len, long_memory_len, short_memory_len),
        own,
        other,
        (long_cot, short_cot),
        (self_inproj, self_outproj, cross_qproj, cross_kvproj, cross_outproj, expand_weight, reduce_weight),
        (
            self_qbias,
            self_vbias,
            self_obias,
            first_gain,
            first_shift,
            cross_qbias,
            cross_vbias,
            cross_obias,
            second_gain,
            second_shift,
            expand_bias,
            reduce_bias,
            final_gain,
            final_shift,
        ),
    )
    line = Line()
    ship1_other = swap(f["ship1"])
    ship2_other = swap(f["ship2"])
    ship3 = f["ship3"]
    ship3_other = swap(ship3)
    c = run_cross(
        size,
        scaling,
        f,
        ship3,
        f["third"],
        (expand_weight, cross_outproj, cross_qproj, self_outproj),
        (second_gain, first_gain),
    )
    line.record(c["low"])
    chalf_other = (swap(c["ship_half"]), swap(c["ship_self"]))
    cpart_other = [swap(value) for value in c["ship_part"]]
    (ffn_keep,) = line.wait(f["ffn_keep"])
    r = run_reduce_grad(size, group, f["ship2"], ship2_other, ffn_keep)
    c1 = Chunk(r["keep"], r["send"], ORDER_ZXY, group)
    line.record(r["keep"])
    (chalf_keep,) = line.wait(c["half_keep"])
    m = run_cross_grads(
        size,
        group,
        ship3,
        ship3_other,
        chalf_keep,
        chalf_other,
        c["part_keep"],
        cpart_other,
        (long_memory, short_memory, other[2], other[3]),
        cross_kvproj,
    )
    c3 = Chunk(m["keep"], m["send"], ORDER_YXZ, group)
    line.record(m["keep"])
    (inner_keep0,) = line.wait(f["inner_keep0"])
    e = run_expand_grad(size, group, f["ship1"], ship1_other, (inner_keep0, f["inner_keep1"]))
    c2 = Chunk(e["keep"], e["send"], ORDER_XZY, group)
    line.record(e["keep"])
    (dcontext,) = line.wait(c["dcontext"])
    b = run_self(size, scaling, f, ship3, dcontext)
    line.record(b["dq"])
    shalf_other = [swap(value) for value in b["ship_half"]]
    spart_other = [swap(value) for value in b["ship_part"]]
    c1.step(line, 0.0)
    (shalf_keep,) = line.wait(b["half_keep"])
    if group == 1:
        expand_rows = f["inner_sum"]
    else:
        expand_rows = f["inner_sum"].reshape(devices, 4, width // devices).transpose(1, 0, 2).reshape(4, width)
    t = run_self_grads(
        size,
        group,
        shalf_keep,
        shalf_other,
        b["part_keep"],
        spart_other,
        (long_target, short_target, other[0], other[1]),
        self_inproj,
        c["low"],
        b["dq"],
        {"sums0": f["sums"], "sums1": c["sums"], "sums2": b["sums"], "sums3": expand_rows},
    )
    c5 = Chunk(t["keep"], t["send"], ORDER_YXZ, group)
    line.record(t["keep"])
    c3.step(line, 0.0)
    c2.step(line, 0.0)
    c1.step(line, 12.0)
    memory_recv, target_recv = (swap(value) for value in line.wait(m["grad_send"], t["grad_send"]))
    for chunk in (c5, c3, c2):
        chunk.step(line)
    memory_grads, target_grads = add_tokens(
        size, *line.wait(m["grad_own"], memory_recv, t["grad_own"], target_recv)
    )
    line.record(target_grads[0])
    for chunk in (c1, c5, c3, c2, c1):
        chunk.step(line)
    reduce_mine = spread_blocks(c1.total, group, hidden_width // width)
    reduce_theirs = swap(reduce_mine)
    c5.step(line)
    c3.step(line, 0.0)
    cross_mine = spread(c3.total, group)
    cross_theirs = swap(cross_mine)
    c2.step(line, 0.0)
    expand_mine = spread(c2.total, group)
    expand_theirs = swap(expand_mine)
    c5.step(line, 4.0)
    self_mine = spread(c5.total, group)
    self_theirs = swap(self_mine)
    half = width // 2
    half_h = hidden_width // 2
    parts = hidden_width // width
    reduce_theirs, expand_theirs, cross_theirs = line.wait(reduce_theirs, expand_theirs, cross_theirs)
    rows_out = reduce_mine.shape[0]
    grad_reduce, grad_expand = finish(
        (reduce_mine, reduce_theirs, expand_mine, expand_theirs),
        ((parts * rows_out, width), (rows_out, hidden_width)),
        [(0, 0, at * half, half, at * rows_out, 0) for at in range(parts)] + [(1, 1, 0, half_h, 0, 0)],
    )
    grad_cross_kv, grad_cross_out, grad_cross_q, grad_self_out = finish(
        (cross_mine, cross_theirs),
        ((rows_out, 2 * width), (rows_out, width), (rows_out, width), (rows_out, width)),
        [
            (0, 0, 0, width, 0, 0),
            (0, 1, width, half, 0, 0),
            (0, 2, width + half, half, 0, 0),
            (0, 3, 2 * width, half, 0, 0),
        ],
    )
    grad_self_in, small = finish(
        (self_mine, self_theirs),
        ((rows_out, 3 * width), (rows_out, LANES)),
        [(0, 0, width, half, 0, 0), (0, 0, 0, width, 0, width), (0, 1, width + half, LANES, 0, None)],
    )
    if group == 1:
        *vectors, expand_bias_rows, statistics = finish_small(self_mine, self_theirs, width, width + half)
    else:
        small = small.T
        vectors = [small[at] for at in SMALL_ROWS]
        expand_bias_rows = small[32:36]
        statistics = jnp.sqrt(small[3:7, 0] / (small[7, 0] * width))
    grad_expand_bias = expand_bias_rows.reshape(-1)
    return (
        f["out_a"],
        f["out_b"],
        *target_grads,
        *memory_grads,
        grad_self_in,
        vectors[0],
        vectors[1],
        grad_self_out,
        vectors[2],
        vectors[3],
        vectors[4],
        grad_cross_q,
        vectors[5],
        grad_cross_kv,
        vectors[6],
        grad_cross_out,
        vectors[7],
        vectors[8],
        vectors[9],
        grad_expand,
        grad_expand_bias,
        grad_reduce,
        vectors[10],
        vectors[11],
        vectors[12],
        statistics,
    )


def solution(mesh):
    split = P("tok", "rep", None)
    in_specs = (split,) * 6 + (P("tok"),) * 4 + (P(),) * 21
    out_specs = (split,) * 6 + (
        P("tok", None),
        P("tok"),
        P("tok"),
        P("tok", None),
        P("tok"),
        P("tok"),
        P("tok"),
        P("tok", None),
        P("tok"),
        P("tok", None),
        P("tok"),
        P("tok", None),
        P("tok"),
        P("tok"),
        P("tok"),
        P("tok", None),
        P("tok"),
        P("tok", None),
        P("tok"),
        P("tok"),
        P("tok"),
        P(),
    )
    return jax.shard_map(per_device, mesh=mesh, in_specs=in_specs, out_specs=out_specs, check_vma=False)
```

```python
import math

import jax
import jax.numpy as jnp
from jax import lax
from jax.experimental import pallas as pl
from jax.experimental.pallas import tpu as pltpu
from jax.sharding import PartitionSpec as P

HEADS = 12
HEAD_DIM = 64
LANES = 128
EPS = 1e-05
MASKED = -1e30
LIMIT = 62 * 1024 * 1024
ADD_LIMIT = 24 * 1024 * 1024

f32 = jnp.float32
bf16 = jnp.bfloat16

ANY = pl.BlockSpec(memory_space=pl.ANY)
VMEM = pl.BlockSpec(memory_space=pltpu.VMEM)
SMEM = pl.BlockSpec(memory_space=pltpu.SMEM)


def dot(a, b):
    return lax.dot_general(a, b, (((1,), (0,)), ((), ())), preferred_element_type=f32)


def dot_nt(a, b):
    return lax.dot_general(a, b, (((1,), (1,)), ((), ())), preferred_element_type=f32)


def dot_tn(a, b):
    return lax.dot_general(a, b, (((0,), (0,)), ((), ())), preferred_element_type=f32)


def shape(dims, dtype):
    return jax.ShapeDtypeStruct(dims, dtype)


def whole(ref):
    return ref


def columns(start, count):
    return lambda ref: ref.at[:, pl.ds(start, count)]


def rows(start, count):
    return lambda ref: ref.at[pl.ds(start, count)]


def first(ref):
    return ref.at[0]


def load(array):
    return Load(array.shape, array.dtype, [(array, whole, 0)])


class Load:
    def __init__(self, dims, dtype, pieces):
        self.dims = dims
        self.dtype = dtype
        self.pieces = pieces


class Split:
    def __init__(self, dims, dtype, count):
        self.shape = dims
        self.dtype = jnp.dtype(dtype)
        self.count = count

    def parts(self):
        return [shape((self.shape[0] // self.count, *self.shape[1:]), self.dtype)] * self.count


def parts_of(value):
    return value.parts() if isinstance(value, Split) else [value]


class Stage:
    def __init__(self, sems):
        self.sems = sems
        self.count = 0
        self.refs = {}
        self.loads = {}
        self.targets = {}
        self.sent = []

    def start(self, source, target):
        copy = pltpu.make_async_copy(source, target, self.sems.at[self.count])
        self.count += 1
        copy.start()
        return copy

    def __getitem__(self, name):
        for copy in self.loads.pop(name, ()):
            copy.wait()
        return self.refs[name]

    def __setitem__(self, name, value):
        self.refs[name][...] = value
        self.put(name)

    def put(self, name):
        targets = self.targets.pop(name, ())
        for index, target in enumerate(targets):
            source = self.refs[name]
            if len(targets) > 1:
                source = source.at[pl.ds(index * target.shape[0], target.shape[0])]
            self.sent.append(self.start(source, target))

    def finish(self):
        for name in list(self.targets):
            self.put(name)
        for name in list(self.loads):
            self[name]
        for copy in self.sent:
            copy.wait()


TIMES = {
    "forward": 27,
    "expand_grad": 7,
    "reduce_grad": 8,
    "cross_back": 16,
    "self_back": 8,
    "cross_grads": 100,
    "self_grads": 9,
    "add_step": 20,
}
SCALE = 0.02


def cost(name, weight=1.0):
    return pl.CostEstimate(flops=int(TIMES[name] * weight * SCALE * 1.15e9), bytes_accessed=1024, transcendentals=0)


def staged(name, body, loads, direct, outs, scratch):
    arrays = [piece[0] for value in loads.values() for piece in value.pieces]
    arrays += [value for value, unused in direct.values()]
    specs = [ANY] * sum(len(value.pieces) for value in loads.values())
    specs += [space for unused, space in direct.values()]
    buffers = {key: pltpu.VMEM(value.dims, value.dtype) for key, value in loads.items()}
    buffers.update({key: pltpu.VMEM(value.shape, value.dtype) for key, value in outs.items()})
    buffers.update({key: pltpu.VMEM(value.shape, value.dtype) for key, value in scratch.items()})
    results = [part for value in outs.values() for part in parts_of(value)]
    copies = sum(len(value.pieces) for value in loads.values()) + len(results)

    def kernel(*refs):
        refs = list(refs)
        stage = Stage(refs[-1])
        sources = {key: [refs.pop(0) for unused in value.pieces] for key, value in loads.items()}
        for key in direct:
            stage.refs[key] = refs.pop(0)
        for key, value in outs.items():
            stage.targets[key] = [refs.pop(0) for unused in parts_of(value)]
        for key in buffers:
            stage.refs[key] = refs.pop(0)
        for key, value in loads.items():
            stage.loads[key] = []
            for ref, (unused, pick, start) in zip(sources[key], value.pieces):
                source = pick(ref)
                target = stage.refs[key]
                if source.shape != target.shape:
                    target = target.at[pl.ds(start, source.shape[0])]
                stage.loads[key].append(stage.start(source, target))
        body(stage)
        stage.finish()

    values = pl.pallas_call(
        kernel,
        name=name,
        out_shape=results,
        in_specs=specs,
        out_specs=[ANY] * len(results),
        scratch_shapes=[*buffers.values(), pltpu.SemaphoreType.DMA((copies,))],
        compiler_params=pltpu.CompilerParams(vmem_limit_bytes=LIMIT),
        cost_estimate=cost(name),
    )(*arrays)
    values = list(values)
    return {
        key: [values.pop(0) for unused in parts_of(value)] if isinstance(value, Split) else values.pop(0)
        for key, value in outs.items()
    }


def row(ref):
    return ref[...].astype(f32).reshape(1, ref.shape[0])


def lane_heads():
    lane = lax.broadcasted_iota(jnp.int32, (1, LANES), 1)
    return (lane < HEAD_DIM, lane >= HEAD_DIM)


def only(mask, value):
    return jnp.where(mask, value, jnp.zeros_like(value))


def both_heads(heads, value):
    return jnp.concatenate([only(heads[0], value), only(heads[1], value)], axis=0)


def rejoin(heads, value):
    rows = value.shape[0] // 2
    return jnp.where(heads[0], value[:rows], value[rows:])


class Sizes:
    def __init__(self, long_local, short_local, width):
        self.a = long_local
        self.b = short_local
        self.own = long_local + short_local
        self.full = 2 * self.own
        self.width = width
        self.pairs = width // LANES
        self.buckets = ((0, self.a, 0), (self.a, self.b, 2 * self.a))

    def own_pieces(self, long_part, short_part, other_long=None, other_short=None):
        pieces = [(long_part, first, 0), (short_part, first, self.a)]
        if other_long is not None:
            pieces += [(other_long, first, self.own), (other_short, first, self.own + self.a)]
        return pieces

    def full_pieces(self, long_part, short_part, other_long, other_short):
        return [
            (long_part, first, 0),
            (other_long, first, self.a),
            (short_part, first, 2 * self.a),
            (other_short, first, 2 * self.a + self.b),
        ]


def key_positions(rows, core):
    at = lax.broadcasted_iota(jnp.int32, (2 * rows, 1), 0)
    return jnp.where(at < rows, core * rows + at, (1 - core) * rows + at - rows)


def query_positions(rows, core):
    at = lax.broadcasted_iota(jnp.int32, (1, 2 * rows), 1)
    return core * rows + jnp.where(at < rows, at, at - rows)


def softmax_columns(scores):
    raised = jnp.exp(scores - jnp.max(scores, axis=0, keepdims=True))
    return (raised * (1.0 / jnp.sum(raised, axis=0, keepdims=True))).astype(bf16)


def attend(size, q, k, v, bias, probs, out, live):
    heads = lane_heads()
    for start, rows, kstart in size.buckets:
        which = 0 if start == 0 else 1
        weights = []
        for pair in range(size.pairs):
            lanes = slice(pair * LANES, (pair + 1) * LANES)
            queries = both_heads(heads, q[start : start + rows, lanes])
            scores = dot_nt(k[kstart : kstart + 2 * rows, lanes], queries) + bias[which][...]
            weights.append(softmax_columns(scores))
            if rows >= LANES:
                finish_pair(size, v, probs, out, live, which, pair, weights.pop(), heads)
        for pair, value in enumerate(weights):
            finish_pair(size, v, probs, out, live, which, pair, value, heads)


def finish_pair(size, v, probs, out, live, which, pair, weights, heads):
    start, rows, kstart = size.buckets[which]
    lanes = slice(pair * LANES, (pair + 1) * LANES)
    probs[which][pair] = weights
    values = v[kstart : kstart + 2 * rows, lanes]
    context = by_query(heads, weights, values)
    out[start : start + rows, lanes] = jnp.where(live[which], context, 0.0).astype(bf16)


def by_query(heads, across, keyed):
    rows = across.shape[1] // 2
    if rows < LANES:
        return rejoin(heads, dot_tn(across, keyed))
    feature = lax.broadcasted_iota(jnp.int32, (LANES, 1), 0)
    turned = dot(keyed.T, across)
    return jnp.where(feature < HEAD_DIM, turned[:, :rows], turned[:, rows:]).T


def head_sums(product):
    rows = product.shape[0]
    if rows < LANES:
        turned = jnp.concatenate([product, product], axis=0).T
        lane = lax.broadcasted_iota(jnp.int32, (1, LANES), 1)
        low = jnp.sum(turned[:HEAD_DIM], axis=0, keepdims=True)
        high = jnp.sum(turned[HEAD_DIM:], axis=0, keepdims=True)
        return jnp.where(lane < rows, low, high)
    turned = product.T
    low = jnp.sum(turned[:HEAD_DIM], axis=0, keepdims=True)
    high = jnp.sum(turned[HEAD_DIM:], axis=0, keepdims=True)
    return jnp.concatenate([low, high], axis=1)


def attend_back(size, q, k, v, probs, context, grad, dq, dk, dv, scaling):
    heads = lane_heads()
    for which, (start, rows, kstart) in enumerate(size.buckets):
        held = []

        def finish(pair, weights, grads, dscores):
            lanes = slice(pair * LANES, (pair + 1) * LANES)
            at = slice(start, start + rows)
            keys = slice(kstart, kstart + 2 * rows)
            dk[keys, lanes] = dot(dscores, both_heads(heads, q[at, lanes])).astype(bf16)
            dv[keys, lanes] = dot(weights, grads).astype(bf16)
            dq[at, lanes] = (by_query(heads, dscores, k[keys, lanes]) * scaling).astype(bf16)

        for pair in range(size.pairs):
            lanes = slice(pair * LANES, (pair + 1) * LANES)
            at = slice(start, start + rows)
            weights = probs[which][pair]
            grads = grad[at, lanes]
            centred = head_sums(grads.astype(f32) * context[at, lanes].astype(f32))
            grads = both_heads(heads, grads)
            dprobs = dot_nt(v[kstart : kstart + 2 * rows, lanes], grads)
            dscores = (weights.astype(f32) * (dprobs - centred)).astype(bf16)
            if rows >= LANES:
                finish(pair, weights, grads, dscores)
            else:
                held.append((pair, weights, grads, dscores))
        for item in held:
            finish(*item)


def norm_parts(tensor):
    centre = tensor - jnp.mean(tensor, axis=-1, keepdims=True)
    rstd = lax.rsqrt(jnp.mean(centre * centre, axis=-1, keepdims=True) + EPS)
    return centre * rstd, rstd


def norm_back(normed, rstd, gain, gradient):
    scaled = gradient * gain
    inner = scaled - jnp.mean(scaled, axis=-1, keepdims=True)
    inner = inner - normed * jnp.mean(scaled * normed, axis=-1, keepdims=True)
    return inner * rstd


def column_sum(tensor):
    return jnp.sum(tensor.astype(f32), axis=0, keepdims=True)


def live_column(rows, core, length):
    return core * rows + lax.broadcasted_iota(jnp.int32, (rows, 1), 0) < length


def forward_body(size, hidden_width, scaling, g):
    core = lax.axis_index("rep")
    a, b, own, width = size.a, size.b, size.own, size.width
    target_len = (g["target_len_a"][0], g["target_len_b"][0])
    memory_len = (g["memory_len_a"][0], g["memory_len_b"][0])
    live = (live_column(a, core, target_len[0]), live_column(b, core, target_len[1]))
    live_all = jnp.concatenate(live, axis=0)
    bias = (g["bias_a"], g["bias_b"])
    context, mixed, low1 = (columns_of(g["ship3"], at * width, width) for at in range(3))
    low2, inner_send = columns_of(g["ship1"], 0, width), columns_of(g["ship1"], width, hidden_width // 2)
    hidden, ffn_send = columns_of(g["ship2"], 0, hidden_width), columns_of(g["ship2"], hidden_width, width // 2)
    for which, rows in enumerate((a, b)):
        at = key_positions(rows, core)
        allowed = (at < target_len[which]) & (at <= query_positions(rows, core))
        bias[which][...] = jnp.where(allowed, 0.0, MASKED)
    xo = g["xo"]
    g["q"] = ((dot(xo[...], g["w_q"][...]) + row(g["qbias"])).astype(bf16) * scaling).astype(bf16)
    xf = g["xf"]
    g["k"] = dot(xf[...], g["w_k"][...]).astype(bf16)
    g["v"] = (dot(xf[...], g["w_v"][...]) + row(g["vbias"])).astype(bf16)
    attend(size, g["q"], g["k"], g["v"], bias, (g["ps_a"], g["ps_b"]), context, live)
    for name in ("ps_a", "ps_b"):
        g.put(name)
    mf, w_ckv = g["mf"], g["w_ckv"]
    g["ck"] = dot(mf[...], w_ckv[:, :width]).astype(bf16)
    g["cv"] = (dot(mf[...], w_ckv[:, width:]) + row(g["cvbias"])).astype(bf16)

    def squares(tensor):
        kept = jnp.where(live_all, tensor * tensor, 0.0)
        return jnp.sum(jnp.sum(kept, axis=0, keepdims=True), axis=1, keepdims=True)

    branch = g["branch"]
    self_branch = dot(context[...], g["w_out"][...]) + row(g["obias"])
    square_self = squares(self_branch)
    normed, rstd = norm_parts(xo[...].astype(f32) + self_branch)
    g["n1"] = normed
    g["r1"] = rstd
    after_self = normed * row(g["gain1"]) + row(g["shift1"])
    low1[...] = after_self.astype(bf16)
    branch[...] = after_self
    query = dot(low1[...], g["w_cq"][...]) + row(g["cqbias"])
    g["cq"] = (query.astype(bf16) * scaling).astype(bf16)
    for which, rows in enumerate((a, b)):
        allowed = key_positions(rows, core) < memory_len[which]
        bias[which][...] = jnp.broadcast_to(jnp.where(allowed, 0.0, MASKED), bias[which].shape)
    attend(size, g["cq"], g["ck"], g["cv"], bias, (g["pc_a"], g["pc_b"]), mixed, live)
    for name in ("pc_a", "pc_b", "ship3"):
        g.put(name)
    cross_branch = dot(mixed[...], g["w_cout"][...]) + row(g["cobias"])
    square_cross = squares(cross_branch)
    normed, rstd = norm_parts(branch[...] + cross_branch)
    g["n2"] = normed
    g["r2"] = rstd
    after_cross = normed * row(g["gain2"]) + row(g["shift2"])
    low2[...] = after_cross.astype(bf16)
    branch[...] = after_cross
    third, slope = g["third"], g["slope"]
    w_exp, w_red = g["w_exp"], g["w_red"]
    eb = row(g["ebias"])
    total = None
    for step in range(hidden_width // width):
        cols = slice(step * width, (step + 1) * width)
        act = dot(low2[...], w_exp[:, cols]) + eb[:, cols]
        phi = 0.5 * (1.0 + lax.erf(act * (1.0 / math.sqrt(2.0))))
        hidden[:, cols] = (act * phi).astype(bf16)
        density = jnp.exp(-0.5 * act * act) * (1.0 / math.sqrt(2.0 * math.pi))
        slope[:, cols] = (phi + act * density).astype(bf16)
        part = dot(hidden[:, cols], w_red[cols, :])
        if step == 0:
            third[...] = part
        else:
            third[...] += part
    ffn_branch = third[...] + row(g["rbias"])
    square_ffn = squares(ffn_branch)
    normed, rstd = norm_parts(branch[...] + ffn_branch)
    gain = row(g["gain3"])
    final = normed * gain + row(g["shift3"])
    square_final = squares(final)
    low = final.astype(bf16)
    g["out_a"] = low[:a][None]
    g["out_b"] = low[a:][None]
    gradient = jnp.where(live_all, g["cot"][...].astype(f32), 0.0)
    d_third = norm_back(normed, rstd, gain, gradient)
    g["third"] = d_third
    d_ffn = d_third.astype(bf16)
    dffn = g["dffn"]
    dffn[...] = d_ffn
    half = width // 2
    g["ffn_keep"] = dffn[:, half_of(core, half)]
    ffn_send[...] = dffn[:, half_of(1 - core, half)]
    g.put("ship2")
    sums = g["sums"]
    sums[0:1] = column_sum(gradient * normed)
    sums[1:2] = column_sum(gradient)
    sums[2:3] = column_sum(d_ffn)
    count = jnp.sum(jnp.where(live_all, 1.0, 0.0), axis=0, keepdims=True)
    for at, value in enumerate((square_final, square_self, square_cross, square_ffn, count)):
        sums[3 + at : 4 + at] = jnp.broadcast_to(value, (1, width))
    g.put("sums")
    half = hidden_width // 2
    for side in (1 - core, core):
        for at, start in enumerate(range(0, half, width)):
            cols = pl.ds(pl.multiple_of(side * half + start, LANES), width)
            grad = dot_nt(dffn[...], w_red[cols, :]) * slope[:, cols].astype(f32)
            low = grad.astype(bf16)
            g["inner_sum"][:, cols] = column_sum(low)
            if side is core:
                g["inner_keep%d" % at] = low
            else:
                inner_send[:, pl.ds(start, width)] = low
        g.put("ship1")


def columns_of(ref, start, count):
    return ref.at[:, pl.ds(start, count)]


def half_of(core, half):
    return pl.ds(pl.multiple_of(core * half, LANES), half)


def run_forward(size, hidden_width, scaling, lengths, own, other, cots, weights, vectors):
    a, b, n, t, w, h = size.a, size.b, size.own, size.full, size.width, hidden_width
    w_in, w_out, w_cq, w_ckv, w_cout, w_exp, w_red = weights
    loads = {
        "xo": Load((n, w), bf16, size.own_pieces(own[0], own[1])),
        "w_q": Load((w, w), bf16, [(w_in, columns(0, w), 0)]),
        "xf": Load((t, w), bf16, size.full_pieces(own[0], own[1], other[0], other[1])),
        "w_k": Load((w, w), bf16, [(w_in, columns(w, w), 0)]),
        "w_v": Load((w, w), bf16, [(w_in, columns(2 * w, w), 0)]),
        "mf": Load((t, w), bf16, size.full_pieces(own[2], own[3], other[2], other[3])),
        "w_ckv": load(w_ckv),
        "w_out": load(w_out),
        "w_cq": load(w_cq),
        "w_cout": load(w_cout),
        "w_exp": load(w_exp),
        "w_red": load(w_red),
        "cot": Load((n, w), bf16, size.own_pieces(cots[0], cots[1])),
    }
    names = ("qbias", "vbias", "obias", "gain1", "shift1", "cqbias", "cvbias", "cobias", "gain2", "shift2")
    names += ("ebias", "rbias", "gain3", "shift3")
    direct = dict(zip(("target_len_a", "target_len_b", "memory_len_a", "memory_len_b"), ((v, SMEM) for v in lengths)))
    direct.update(zip(names, ((v, VMEM) for v in vectors)))
    square = shape((n, w), bf16)
    keys = shape((t, w), bf16)
    outs = {
        "out_a": shape((1, a, w), bf16),
        "out_b": shape((1, b, w), bf16),
        "q": square,
        "k": keys,
        "v": keys,
        "cq": square,
        "ck": keys,
        "cv": keys,
        "ps_a": shape((size.pairs, 2 * a, 2 * a), bf16),
        "ps_b": shape((size.pairs, 2 * b, 2 * b), bf16),
        "pc_a": shape((size.pairs, 2 * a, 2 * a), bf16),
        "pc_b": shape((size.pairs, 2 * b, 2 * b), bf16),
        "ship1": shape((n, w + h // 2), bf16),
        "ship2": shape((n, h + w // 2), bf16),
        "ship3": shape((n, 3 * w), bf16),
        "n1": shape((n, w), f32),
        "r1": shape((n, 1), f32),
        "n2": shape((n, w), f32),
        "r2": shape((n, 1), f32),
        "third": shape((n, w), f32),
        "ffn_keep": shape((n, w // 2), bf16),
        "sums": shape((8, w), f32),
        "inner_keep0": square,
        "inner_keep1": square,
        "inner_sum": shape((1, h), f32),
    }
    scratch = {
        "bias_a": shape((2 * a, 2 * a), f32),
        "bias_b": shape((2 * b, 2 * b), f32),
        "branch": shape((n, w), f32),
        "slope": shape((n, h), bf16),
        "dffn": square,
    }
    return staged(
        "forward",
        lambda g: forward_body(size, hidden_width, scaling, g),
        loads,
        direct,
        outs,
        scratch,
    )


def split_partial(size, core, dk, dv, keep, send):
    a, b = size.a, size.b
    moves = ((0, a, a), (a, 0, a), (2 * a, 2 * a + b, b), (2 * a + b, 2 * a, b))
    for here, (stay, leave) in ((0, (dk, dv)), (1, (dv, dk))):

        @pl.when(core == here)
        def unused(stay=stay, leave=leave):
            keep[...] = stay[...]
            for target, source, rows in moves:
                send[pl.ds(target, rows)] = leave[pl.ds(source, rows)]


def through_norm(size, g, gradient, normed, rstd, gain, w_out, sums, back):
    normed = g[normed][...]
    d_sum = norm_back(normed, g[rstd][...], row(g[gain]), gradient)
    sums[0:1] = column_sum(gradient * normed)
    sums[1:2] = column_sum(gradient)
    low = d_sum.astype(bf16)
    sums[2:3] = column_sum(low)
    g["branch"][...] = low
    back[...] = dot_nt(low, g[w_out][...]).astype(bf16)
    return d_sum


def send_halves(core, value, keep, send, at, half):
    keep[:, at * half : (at + 1) * half] = value[:, half_of(core, half)]
    send[:, at * half : (at + 1) * half] = value[:, half_of(1 - core, half)]


def cross_body(size, scaling, parts, g):
    core = lax.axis_index("rep")
    half = size.width // 2
    keep = g["half_keep"]
    send, part_send = g["ship_half"], g["ship_part"]
    sums, sums2 = g["sums"].at[pl.ds(0, 8)], g["sums"].at[pl.ds(8, 8)]
    g["sums"][...] = jnp.zeros_like(g["sums"])
    gradient = g["third"][...]
    for index in range(parts):
        gradient = gradient + dot_nt(g["inner%d" % index][...], g["w_exp%d" % index][...])
    g["mid"][...] = through_norm(size, g, gradient, "n2", "r2", "gain2", "w_cout", sums, g["back"])
    send_halves(core, g["branch"], keep, send, 0, half)
    attend_back(
        size, g["cq"], g["ck"], g["cv"], (g["pc_a"], g["pc_b"]), g["mixed"], g["back"], g["dq"], g["dk"], g["dv"], scaling
    )
    send_halves(core, g["dq"], keep, send, 1, half)
    g.put("ship_half")
    split_partial(size, core, g["dk"], g["dv"], g["part_keep"], part_send)
    g.put("ship_part")
    g.put("part_keep")
    gradient = g["mid"][...] + dot_nt(g["dq"][...], g["w_cq"][...])
    g["low"] = through_norm(size, g, gradient, "n1", "r1", "gain1", "w_out", sums2, g["dcontext"])
    g.put("dcontext")
    keep[:, 2 * half :] = g["branch"][:, half_of(core, half)]
    g["ship_self"] = g["branch"][:, half_of(1 - core, half)]
    g.put("half_keep")
    sums[3:4] = column_sum(g["dq"][...])
    sums[4:5] = column_sum(g["dv"][...])


def run_cross(size, scaling, f, ship3, third, weights, gains):
    n, t, w = size.own, size.full, size.width
    w_exp, w_cout, w_cq, w_out = weights
    loads = {
        "third": load(third),
    }
    parts = w_exp.shape[1] // w

    def column_part(index):
        def pick(ref):
            core = lax.axis_index("rep")
            side = core if index < 2 else 1 - core
            return ref.at[:, pl.ds(pl.multiple_of((2 * side + index % 2) * w, LANES), w)]

        return Load((w, w), bf16, [(w_exp, pick, 0)])

    for index in range(parts):
        source = (f["inner_keep%d" % index], whole, 0) if index < 2 else (f["ship1"], columns((index - 1) * w, w), 0)
        loads["inner%d" % index] = Load((n, w), bf16, [source])
        loads["w_exp%d" % index] = column_part(index)
    loads |= {
        "n2": load(f["n2"]),
        "r2": load(f["r2"]),
        "w_cout": load(w_cout),
        "mixed": Load((n, w), bf16, [(ship3, columns(w, w), 0)]),
        "cv": load(f["cv"]),
        "pc_a": load(f["pc_a"]),
        "cq": load(f["cq"]),
        "ck": load(f["ck"]),
        "pc_b": load(f["pc_b"]),
        "w_cq": load(w_cq),
        "n1": load(f["n1"]),
        "r1": load(f["r1"]),
        "w_out": load(w_out),
    }
    square = shape((n, w), bf16)
    keys = shape((t, w), bf16)
    return staged(
        "cross_back",
        lambda g: cross_body(size, scaling, parts, g),
        loads,
        {"gain2": (gains[0], VMEM), "gain1": (gains[1], VMEM)},
        {
            "low": shape((n, w), f32),
            "dcontext": square,
            "half_keep": shape((n, 3 * (w // 2)), bf16),
            "ship_half": square,
            "ship_self": shape((n, w // 2), bf16),
            "part_keep": keys,
            "ship_part": Split((t, w), bf16, PIECES),
            "sums": shape((16, w), f32),
        },
        {"branch": square, "back": square, "dq": square, "dk": keys, "dv": keys, "mid": shape((n, w), f32)},
    )


def self_body(size, scaling, g):
    core = lax.axis_index("rep")
    half = size.width // 2
    send, part_send = g["ship_half"], g["ship_part"]
    sums = g["sums"]
    sums[...] = jnp.zeros_like(sums)
    attend_back(
        size, g["q"], g["k"], g["v"], (g["ps_a"], g["ps_b"]), g["context"], g["dcontext"], g["dq"], g["dk"], g["dv"], scaling
    )
    g.put("dq")
    split_partial(size, core, g["dk"], g["dv"], g["part_keep"], part_send)
    g.put("ship_part")
    send_halves(core, g["dq"], g["half_keep"], send, 0, half)
    g.put("ship_half")
    g.put("part_keep")
    g.put("half_keep")
    sums[0:1] = column_sum(g["dq"][...])
    sums[1:2] = column_sum(g["dv"][...])


def run_self(size, scaling, f, ship3, dcontext):
    n, t, w = size.own, size.full, size.width
    loads = {
        "dcontext": load(dcontext),
        "context": Load((n, w), bf16, [(ship3, columns(0, w), 0)]),
        "v": load(f["v"]),
        "ps_a": load(f["ps_a"]),
        "q": load(f["q"]),
        "k": load(f["k"]),
        "ps_b": load(f["ps_b"]),
    }
    square = shape((n, w), bf16)
    keys = shape((t, w), bf16)
    return staged(
        "self_back",
        lambda g: self_body(size, scaling, g),
        loads,
        {},
        {
            "dq": square,
            "half_keep": shape((n, w // 2), bf16),
            "ship_half": Split((n, w // 2), bf16, 1),
            "part_keep": keys,
            "ship_part": Split((t, w), bf16, PIECES),
            "sums": shape((8, w), f32),
        },
        {"dk": keys, "dv": keys},
    )


PIECES = 2
BLOCKS = 16
STAGES = 4
ORDER_XZY = (0, 2, 3, 1)
ORDER_YXZ = (1, 0, 2, 3)
ORDER_ZXY = (2, 3, 0, 1)


class Scatter:
    def __init__(self, order, me, keep, send, rows):
        self.order = order
        self.me = me
        self.keep = keep
        self.send = send
        self.rows = rows

    def store(self, block, value, start, count):
        distance = self.me ^ block
        place = 0
        for stage, bit in enumerate(self.order):
            place = place + (((distance >> bit) & 1) << (STAGES - 1 - stage))
        low = place < BLOCKS // 2
        at = pl.multiple_of(jnp.where(low, place, place - BLOCKS // 2) * self.rows, 16)
        rows = pl.ds(at, self.rows)
        cols = slice(start, start + count)

        @pl.when(low)
        def unused():
            self.keep[rows, cols] = value.astype(bf16)

        @pl.when(jnp.logical_not(low))
        def unused_too():
            self.send[rows, cols] = value.astype(bf16)

    def store_all(self, product, start):
        for block in range(BLOCKS):
            self.store(block, product[block * self.rows : (block + 1) * self.rows], start, product.shape[1])


def my_block(group):
    return lax.axis_index("tok") // group


def chunk_outs(size, columns, names):
    rows = size.width // 2
    return {name: shape((rows, columns), bf16) for name in names}


def expand_body(size, group, g):
    scatter = Scatter(ORDER_XZY, my_block(group), g["keep"], g["send"], size.width // BLOCKS)
    for at in range(2):
        scatter.store_all(dot_tn(g["low"][...], g["d%d" % at][...]), at * size.width)
    g.put("send")


def run_expand_grad(size, group, ship, ship_other, keeps):
    n, t, w = size.own, size.full, size.width
    loads = {"low": Load((t, w), bf16, [(ship, columns(0, w), 0), (ship_other, columns(0, w), n)])}
    for at, keep in enumerate(keeps):
        loads["d%d" % at] = Load((t, w), bf16, [(keep, whole, 0), (ship_other, columns(w + at * w, w), n)])
    return staged(
        "expand_grad",
        lambda g: expand_body(size, group, g),
        loads,
        {},
        chunk_outs(size, 2 * w, ("keep", "send")),
        {},
    )


def reduce_chunk(group, index):
    return (my_block(group) >> 2) ^ (1, 3, 0, 2)[index]


def reduce_body(size, group, g):
    count = size.width // BLOCKS
    half = size.width // 2
    parts = BLOCKS // 4
    mine = my_block(group) & 3
    for index in range(4):
        target = g["send"] if index < 2 else g["keep"]
        product = dot_tn(g["hidden%d" % index][...], g["d"][...])
        for block in range(4):
            distance = mine ^ block
            place = (index % 2) * 4 + ((distance & 1) << 1) + (distance >> 1)
            at = pl.ds(pl.multiple_of(place * count, 16), count)
            for part in range(parts):
                start = (block * parts + part) * count
                target[at, part * half : (part + 1) * half] = product[start : start + count].astype(bf16)
        if index % 2 == 1:
            g.put("send" if index < 2 else "keep")


def run_reduce_grad(size, group, ship, ship_other, keep):
    n, t, w = size.own, size.full, size.width
    half = keep.shape[1]
    h = ship.shape[1] - half
    quarter = h // 4

    def chunk(index):
        def pick(ref):
            return ref.at[:, pl.ds(pl.multiple_of(reduce_chunk(group, index) * quarter, LANES), quarter)]

        return Load((t, quarter), bf16, [(ship, pick, 0), (ship_other, pick, n)])

    loads = {"d": Load((t, half), bf16, [(keep, whole, 0), (ship_other, columns(h, half), n)])}
    loads.update({"hidden%d" % index: chunk(index) for index in range(4)})
    return staged(
        "reduce_grad",
        lambda g: reduce_body(size, group, g),
        loads,
        {},
        chunk_outs(size, h // 2, ("send", "keep")),
        {},
    )


def projection_share(size, g, scatter):
    a, b = size.a, size.b
    total = g["total"]
    total[...] = (g["part_keep"][...].astype(f32) + g["part_recv"][...].astype(f32)).astype(bf16)
    scatter.store_all(dot_tn(g["source"][...], total[...]), 0)
    g.put("send")
    share = dot_nt(total[...], g["weight"][...])
    g["grad_send"][pl.ds(0, a)] = share[a : 2 * a].astype(bf16)
    g["grad_send"][pl.ds(a, b)] = share[2 * a + b :].astype(bf16)
    g["grad_own"][pl.ds(0, a)] = share[:a]
    g["grad_own"][pl.ds(a, b)] = share[2 * a : 2 * a + b]


def cross_grad_body(size, group, g):
    width = size.width
    half = width // 2
    scatter = Scatter(ORDER_YXZ, my_block(group), g["keep"], g["send"], width // BLOCKS)
    for at, name in enumerate(("mixed", "low1")):
        cols = slice(at * half, (at + 1) * half)
        scatter.store_all(dot_tn(g[name][...], g["halves"][:, cols]), width + at * half)
    scatter.store_all(dot_tn(g["context"][...], g["halves_self"][...]), 2 * width)
    projection_share(size, g, scatter)
    g.put("keep")
    g.put("grad_send")


def stacked(arrays, start):
    return [(array, whole, start + index * array.shape[0]) for index, array in enumerate(arrays)]


def my_columns(weight, width):
    skip = weight.shape[1] - 2 * width

    def pick(ref):
        return ref.at[:, pl.ds(pl.multiple_of(skip + lax.axis_index("rep") * width, LANES), width)]

    return Load((width, width), bf16, [(weight, pick, 0)])


def run_cross_grads(size, group, ship3, ship3_other, half_keep, half_recv, part_keep, part_recv, sources, weight):
    n, t, w = size.own, size.full, size.width

    def both(at):
        return Load((t, w), bf16, [(ship3, columns(at * w, w), 0), (ship3_other, columns(at * w, w), n)])

    half = w // 2
    outs = chunk_outs(size, w + 3 * half, ("keep", "send"))
    outs["grad_own"] = shape((n, w), f32)
    outs["grad_send"] = shape((n, w), bf16)
    return staged(
        "cross_grads",
        lambda g: cross_grad_body(size, group, g),
        {
            "mixed": both(1),
            "halves": Load((t, 2 * half), bf16, [(half_keep, columns(0, 2 * half), 0), (half_recv[0], whole, n)]),
            "low1": both(2),
            "context": both(0),
            "halves_self": Load((t, half), bf16, [(half_keep, columns(2 * half, half), 0), (half_recv[1], whole, n)]),
            "part_keep": load(part_keep),
            "part_recv": Load((t, w), bf16, stacked(part_recv, 0)),
            "source": Load((t, w), bf16, size.full_pieces(*sources)),
            "weight": my_columns(weight, w),
        },
        {},
        outs,
        {"total": shape((t, w), bf16)},
    )


def regroup(value, width, count):
    parts = value.shape[1] // width
    lane = lax.broadcasted_iota(jnp.int32, (1, width), 1)
    rows_out = [jnp.zeros((1, width), f32)] * parts
    for step in range(parts):
        piece = value[:, step * width : (step + 1) * width]
        for at in range(width // count):
            device, part = divmod(step * (width // count) + at, parts)
            moved = pltpu.roll(piece, ((device - at) * count) % width, 1)
            mine = (lane >= device * count) & (lane < (device + 1) * count)
            rows_out[part] = jnp.where(mine, moved, rows_out[part])
    return jnp.concatenate(rows_out, axis=0)


def self_grad_body(size, group, sums, g):
    width = size.width
    half = width // 2
    count = width // BLOCKS
    scatter = Scatter(ORDER_YXZ, my_block(group), g["keep"], g["send"], count)
    held = g["rows"]
    held[...] = jnp.zeros_like(held)
    at = 0
    for name in sums:
        value = g[name][...]
        if value.shape[1] > width:
            value = regroup(value, width, count)
        held[pl.ds(at, value.shape[0])] = value
        at += value.shape[0]
    scatter.store_all(jnp.transpose(held[...]), width + half)
    scatter.store_all(dot_tn(g["lhs"][...], g["halves"][...]), width)
    projection_share(size, g, scatter)
    g.put("keep")
    g.put("grad_send")
    g["grad_own"][...] += g["low"][...] + dot_nt(g["dq"][...], g["w_q"][...])


def run_self_grads(size, group, half_keep, half_recv, part_keep, part_recv, sources, weight, low, dq, sums):
    n, t, w = size.own, size.full, size.width
    half = w // 2
    loads = {key: load(value) for key, value in sums.items()}
    loads.update(
        part_keep=load(part_keep),
        part_recv=Load((t, w), bf16, stacked(part_recv, 0)),
        source=Load((t, w), bf16, size.full_pieces(*sources)),
        weight=my_columns(weight, w),
        lhs=Load((t, w), bf16, size.own_pieces(*sources)),
        halves=Load((t, half), bf16, [(half_keep, whole, 0), *stacked(half_recv, n)]),
        dq=load(dq),
        w_q=Load((w, w), bf16, [(weight, columns(0, w), 0)]),
        low=load(low),
    )
    outs = chunk_outs(size, w + half + LANES, ("keep", "send"))
    outs["grad_own"] = shape((n, w), f32)
    outs["grad_send"] = shape((n, w), bf16)
    return staged(
        "self_grads",
        lambda g: self_grad_body(size, group, tuple(sums), g),
        loads,
        {},
        outs,
        {"total": shape((t, w), bf16), "rows": shape((LANES, w), f32)},
    )


def swap(value):
    return lax.ppermute(value, "rep", [(0, 1), (1, 0)])


class Line:
    def __init__(self):
        self.last = None

    def wait(self, *values):
        if self.last is None:
            return values
        return lax.optimization_barrier((*values, self.last))[:-1]

    def record(self, value):
        self.last = value


def add_step(pairs, weight=1.0):
    rows = pairs[0][0].shape[0] // 2
    columns = sum(keep.shape[1] for keep, unused in pairs)

    def kernel(*refs):
        keep_out, send_out = refs[-2:]
        at = 0
        for index in range(len(pairs)):
            keep, received = refs[2 * index], refs[2 * index + 1]
            cols = slice(at, at + keep.shape[1])
            at += keep.shape[1]
            total = (keep[...].astype(f32) + received[...].astype(f32)).astype(bf16)
            keep_out[:, cols] = total[:rows]
            send_out[:, cols] = total[rows:]

    flat = [value for pair in pairs for value in pair]
    return pl.pallas_call(
        kernel,
        name="add_step",
        out_shape=[shape((rows, columns), bf16)] * 2,
        in_specs=[VMEM] * len(flat),
        out_specs=[VMEM] * 2,
        compiler_params=pltpu.CompilerParams(vmem_limit_bytes=ADD_LIMIT),
        cost_estimate=cost("add_step", weight),
    )(*flat)


def add_last(keep, received, weight=1.0):
    def kernel(keep, received, out):
        out[...] = (keep[...].astype(f32) + received[...].astype(f32)).astype(bf16)

    return pl.pallas_call(
        kernel,
        name="add_last",
        out_shape=shape(keep.shape, bf16),
        in_specs=[VMEM] * 2,
        out_specs=VMEM,
        compiler_params=pltpu.CompilerParams(vmem_limit_bytes=ADD_LIMIT),
        cost_estimate=cost("add_step", weight),
    )(keep, received)


class Chunk:
    def __init__(self, keep, send, order, group, stage=0):
        self.keep = keep
        self.order = order
        self.group = group
        self.stage = stage
        self.begin(send)

    def begin(self, send):
        devices = lax.axis_size("tok")
        bit = self.group << self.order[self.stage]
        self.received = lax.ppermute(send, "tok", [(i, i ^ bit) for i in range(devices)])

    def launch(self, line):
        (send,) = line.wait(self.send)
        self.begin(send)

    def step(self, line, weight=1.0):
        self.absorb(line, weight)
        if self.stage < STAGES:
            self.begin(self.send)

    def absorb(self, line, weight=1.0):
        keep, received = line.wait(self.keep, self.received)
        self.stage += 1
        if self.stage == STAGES:
            self.total = add_last(keep, received, weight)
            line.record(self.total)
            return
        self.keep, self.send = add_step([(keep, received)], weight)
        line.record(self.keep)


def spread(total, group):
    if group == 1:
        return total
    devices = lax.axis_size("tok")
    sets = [[start + i for i in range(group)] for start in range(0, devices, group)]
    total = lax.psum_scatter(total.astype(f32), "tok", scatter_dimension=0, tiled=True, axis_index_groups=sets)
    return total.astype(bf16)


def spread_blocks(total, group, parts):
    if group == 1:
        return total
    wide = total.shape[1] // parts
    rows_in = jnp.concatenate([total[:, at * wide : (at + 1) * wide] for at in range(parts)], axis=0)
    rows_in = spread(rows_in, group)
    count = rows_in.shape[0] // parts
    return jnp.concatenate([rows_in[at * count : (at + 1) * count] for at in range(parts)], axis=1)


def merge(line, *chunks):
    values = line.wait(*[value for chunk in chunks for value in (chunk.keep, chunk.received)])
    keep, send = add_step(list(zip(values[::2], values[1::2])))
    line.record(keep)
    return Chunk(keep, send, chunks[0].order, chunks[0].group, chunks[0].stage + 1)


def add_tokens(size, *values):
    a, b, w = size.a, size.b, size.width

    def kernel(*refs):
        for at in range(2):
            own, received = refs[2 * at : 2 * at + 2]
            long_out, short_out = refs[4 + 2 * at : 6 + 2 * at]
            long_out[0] = (own[:a] + received[:a].astype(f32)).astype(bf16)
            short_out[0] = (own[a:] + received[a:].astype(f32)).astype(bf16)

    outs = pl.pallas_call(
        kernel,
        name="add_tokens",
        out_shape=[shape((1, a, w), bf16), shape((1, b, w), bf16)] * 2,
        in_specs=[VMEM] * 4,
        out_specs=[VMEM] * 4,
        compiler_params=pltpu.CompilerParams(vmem_limit_bytes=ADD_LIMIT),
        cost_estimate=cost("add_step", 0.0),
    )(*values)
    return outs[:2], outs[2:]


SMALL_ROWS = (24, 25, 18, 16, 17, 11, 12, 10, 8, 9, 2, 0, 1)


def finish_small(mine, theirs, width, start):
    rows_out = mine.shape[0]
    outs = [shape((rows_out,), f32)] * len(SMALL_ROWS) + [shape((4 * rows_out,), f32), shape((4,), f32)]

    def kernel(mine, theirs, *refs):
        cols = slice(start, start + LANES)
        total = mine[:, cols].astype(f32) + theirs[:, cols].astype(f32)
        turned = total.T
        for ref, at in zip(refs, SMALL_ROWS):
            ref[...] = turned[at : at + 1].reshape(rows_out)
        refs[-2][...] = jnp.concatenate([turned[at : at + 1] for at in range(32, 36)], axis=1).reshape(4 * rows_out)
        line = total[0:1]
        refs[-1][...] = jnp.sqrt(line[:, 3:7] / (line[:, 7:8] * width)).reshape(4)

    return pl.pallas_call(
        kernel,
        name="finish_small",
        out_shape=outs,
        in_specs=[VMEM] * 2,
        out_specs=[VMEM] * len(outs),
        compiler_params=pltpu.CompilerParams(vmem_limit_bytes=ADD_LIMIT),
        cost_estimate=cost("add_step"),
    )(mine, theirs)


def finish(pairs, dims, moves):
    outs = [shape(value, f32) for value in dims]

    def kernel(*refs):
        core = lax.axis_index("rep")
        for pair, out, start, count, row_at, column in moves:
            mine, theirs = refs[2 * pair], refs[2 * pair + 1]
            target = refs[len(pairs) + out]
            at = slice(row_at, row_at + mine.shape[0])
            cols = slice(start, start + count)
            if column is None:
                target[at, :] = mine[:, cols].astype(f32) + theirs[:, cols].astype(f32)
                continue
            for ref, side in ((mine, core), (theirs, 1 - core)):
                target[at, pl.ds(pl.multiple_of(column + side * count, LANES), count)] = ref[:, cols].astype(f32)

    return pl.pallas_call(
        kernel,
        name="finish",
        out_shape=outs,
        in_specs=[VMEM] * len(pairs),
        out_specs=[VMEM] * len(outs),
        compiler_params=pltpu.CompilerParams(vmem_limit_bytes=ADD_LIMIT),
        cost_estimate=cost("add_step"),
    )(*pairs)


def per_device(*args):
    (
        long_target,
        short_target,
        long_memory,
        short_memory,
        long_cot,
        short_cot,
        long_target_len,
        short_target_len,
        long_memory_len,
        short_memory_len,
        self_inproj,
        self_qbias,
        self_vbias,
        self_outproj,
        self_obias,
        first_gain,
        first_shift,
        cross_qproj,
        cross_qbias,
        cross_kvproj,
        cross_vbias,
        cross_outproj,
        cross_obias,
        second_gain,
        second_shift,
        expand_weight,
        expand_bias,
        reduce_weight,
        reduce_bias,
        final_gain,
        final_shift,
    ) = args
    core = lax.axis_index("rep")
    devices = lax.axis_size("tok")
    group = devices // BLOCKS
    width = long_target.shape[2]
    hidden_width = expand_weight.shape[1]
    size = Sizes(long_target.shape[1], short_target.shape[1], width)
    n = size.own
    scaling = 1.0 / math.sqrt(HEAD_DIM)
    own = (long_target, short_target, long_memory, short_memory)
    other = tuple(swap(value) for value in own)
    f = run_forward(
        size,
        hidden_width,
        scaling,
        (long_target_len, short_target_len, long_memory_len, short_memory_len),
        own,
        other,
        (long_cot, short_cot),
        (self_inproj, self_outproj, cross_qproj, cross_kvproj, cross_outproj, expand_weight, reduce_weight),
        (
            self_qbias,
            self_vbias,
            self_obias,
            first_gain,
            first_shift,
            cross_qbias,
            cross_vbias,
            cross_obias,
            second_gain,
            second_shift,
            expand_bias,
            reduce_bias,
            final_gain,
            final_shift,
        ),
    )
    line = Line()
    ship1_other = swap(f["ship1"])
    ship2_other = swap(f["ship2"])
    ship3 = f["ship3"]
    ship3_other = swap(ship3)
    c = run_cross(
        size,
        scaling,
        f,
        ship3,
        f["third"],
        (expand_weight, cross_outproj, cross_qproj, self_outproj),
        (second_gain, first_gain),
    )
    line.record(c["low"])
    chalf_other = (swap(c["ship_half"]), swap(c["ship_self"]))
    cpart_other = [swap(value) for value in c["ship_part"]]
    (ffn_keep,) = line.wait(f["ffn_keep"])
    r = run_reduce_grad(size, group, f["ship2"], ship2_other, ffn_keep)
    c1 = Chunk(r["keep"], r["send"], ORDER_ZXY, group)
    line.record(r["keep"])
    (chalf_keep,) = line.wait(c["half_keep"])
    m = run_cross_grads(
        size,
        group,
        ship3,
        ship3_other,
        chalf_keep,
        chalf_other,
        c["part_keep"],
        cpart_other,
        (long_memory, short_memory, other[2], other[3]),
        cross_kvproj,
    )
    c3 = Chunk(m["keep"], m["send"], ORDER_YXZ, group)
    line.record(m["keep"])
    (inner_keep0,) = line.wait(f["inner_keep0"])
    e = run_expand_grad(size, group, f["ship1"], ship1_other, (inner_keep0, f["inner_keep1"]))
    c2 = Chunk(e["keep"], e["send"], ORDER_XZY, group)
    line.record(e["keep"])
    (dcontext,) = line.wait(c["dcontext"])
    b = run_self(size, scaling, f, ship3, dcontext)
    line.record(b["dq"])
    shalf_other = [swap(value) for value in b["ship_half"]]
    spart_other = [swap(value) for value in b["ship_part"]]
    c1.step(line, 0.0)
    (shalf_keep,) = line.wait(b["half_keep"])
    if group == 1:
        expand_rows = f["inner_sum"]
    else:
        expand_rows = f["inner_sum"].reshape(devices, 4, width // devices).transpose(1, 0, 2).reshape(4, width)
    t = run_self_grads(
        size,
        group,
        shalf_keep,
        shalf_other,
        b["part_keep"],
        spart_other,
        (long_target, short_target, other[0], other[1]),
        self_inproj,
        c["low"],
        b["dq"],
        {"sums0": f["sums"], "sums1": c["sums"], "sums2": b["sums"], "sums3": expand_rows},
    )
    c5 = Chunk(t["keep"], t["send"], ORDER_YXZ, group)
    line.record(t["keep"])
    c3.step(line, 0.0)
    c2.step(line, 0.0)
    c1.step(line, 12.0)
    memory_recv, target_recv = (swap(value) for value in line.wait(m["grad_send"], t["grad_send"]))
    for chunk in (c5, c3, c2):
        chunk.step(line)
    memory_grads, target_grads = add_tokens(
        size, *line.wait(m["grad_own"], memory_recv, t["grad_own"], target_recv)
    )
    line.record(target_grads[0])
    for chunk in (c1, c5, c3, c2, c1):
        chunk.step(line)
    reduce_mine = spread_blocks(c1.total, group, hidden_width // width)
    reduce_theirs = swap(reduce_mine)
    c5.step(line)
    c3.step(line, 0.5)
    cross_mine = spread(c3.total, group)
    cross_theirs = swap(cross_mine)
    c2.step(line, 0.5)
    expand_mine = spread(c2.total, group)
    expand_theirs = swap(expand_mine)
    c5.step(line, 4.0)
    self_mine = spread(c5.total, group)
    self_theirs = swap(self_mine)
    half = width // 2
    half_h = hidden_width // 2
    parts = hidden_width // width
    reduce_theirs, expand_theirs, cross_theirs = line.wait(reduce_theirs, expand_theirs, cross_theirs)
    rows_out = reduce_mine.shape[0]
    grad_reduce, grad_expand = finish(
        (reduce_mine, reduce_theirs, expand_mine, expand_theirs),
        ((parts * rows_out, width), (rows_out, hidden_width)),
        [(0, 0, at * half, half, at * rows_out, 0) for at in range(parts)] + [(1, 1, 0, half_h, 0, 0)],
    )
    grad_cross_kv, grad_cross_out, grad_cross_q, grad_self_out = finish(
        (cross_mine, cross_theirs),
        ((rows_out, 2 * width), (rows_out, width), (rows_out, width), (rows_out, width)),
        [
            (0, 0, 0, width, 0, 0),
            (0, 1, width, half, 0, 0),
            (0, 2, width + half, half, 0, 0),
            (0, 3, 2 * width, half, 0, 0),
        ],
    )
    grad_self_in, small = finish(
        (self_mine, self_theirs),
        ((rows_out, 3 * width), (rows_out, LANES)),
        [(0, 0, width, half, 0, 0), (0, 0, 0, width, 0, width), (0, 1, width + half, LANES, 0, None)],
    )
    if group == 1:
        *vectors, expand_bias_rows, statistics = finish_small(self_mine, self_theirs, width, width + half)
    else:
        small = small.T
        vectors = [small[at] for at in SMALL_ROWS]
        expand_bias_rows = small[32:36]
        statistics = jnp.sqrt(small[3:7, 0] / (small[7, 0] * width))
    grad_expand_bias = expand_bias_rows.reshape(-1)
    return (
        f["out_a"],
        f["out_b"],
        *target_grads,
        *memory_grads,
        grad_self_in,
        vectors[0],
        vectors[1],
        grad_self_out,
        vectors[2],
        vectors[3],
        vectors[4],
        grad_cross_q,
        vectors[5],
        grad_cross_kv,
        vectors[6],
        grad_cross_out,
        vectors[7],
        vectors[8],
        vectors[9],
        grad_expand,
        grad_expand_bias,
        grad_reduce,
        vectors[10],
        vectors[11],
        vectors[12],
        statistics,
    )


def solution(mesh):
    split = P("tok", "rep", None)
    in_specs = (split,) * 6 + (P("tok"),) * 4 + (P(),) * 21
    out_specs = (split,) * 6 + (
        P("tok", None),
        P("tok"),
        P("tok"),
        P("tok", None),
        P("tok"),
        P("tok"),
        P("tok"),
        P("tok", None),
        P("tok"),
        P("tok", None),
        P("tok"),
        P("tok", None),
        P("tok"),
        P("tok"),
        P("tok"),
        P("tok", None),
        P("tok"),
        P("tok", None),
        P("tok"),
        P("tok"),
        P("tok"),
        P(),
    )
    return jax.shard_map(per_device, mesh=mesh, in_specs=in_specs, out_specs=out_specs, check_vma=False)
```

```python
import math

import jax
import jax.numpy as jnp
from jax import lax
from jax.experimental import pallas as pl
from jax.experimental.pallas import tpu as pltpu
from jax.sharding import PartitionSpec as P

HEADS = 12
HEAD_DIM = 64
LANES = 128
EPS = 1e-05
MASKED = -1e30
LIMIT = 62 * 1024 * 1024
ADD_LIMIT = 24 * 1024 * 1024

f32 = jnp.float32
bf16 = jnp.bfloat16

ANY = pl.BlockSpec(memory_space=pl.ANY)
VMEM = pl.BlockSpec(memory_space=pltpu.VMEM)
SMEM = pl.BlockSpec(memory_space=pltpu.SMEM)


def dot(a, b):
    return lax.dot_general(a, b, (((1,), (0,)), ((), ())), preferred_element_type=f32)


def dot_nt(a, b):
    return lax.dot_general(a, b, (((1,), (1,)), ((), ())), preferred_element_type=f32)


def dot_tn(a, b):
    return lax.dot_general(a, b, (((0,), (0,)), ((), ())), preferred_element_type=f32)


def shape(dims, dtype):
    return jax.ShapeDtypeStruct(dims, dtype)


def whole(ref):
    return ref


def columns(start, count):
    return lambda ref: ref.at[:, pl.ds(start, count)]


def rows(start, count):
    return lambda ref: ref.at[pl.ds(start, count)]


def first(ref):
    return ref.at[0]


def load(array):
    return Load(array.shape, array.dtype, [(array, whole, 0)])


class Load:
    def __init__(self, dims, dtype, pieces):
        self.dims = dims
        self.dtype = dtype
        self.pieces = pieces


class Split:
    def __init__(self, dims, dtype, count):
        self.shape = dims
        self.dtype = jnp.dtype(dtype)
        self.count = count

    def parts(self):
        return [shape((self.shape[0] // self.count, *self.shape[1:]), self.dtype)] * self.count


def parts_of(value):
    return value.parts() if isinstance(value, Split) else [value]


class Stage:
    def __init__(self, sems):
        self.sems = sems
        self.count = 0
        self.refs = {}
        self.loads = {}
        self.targets = {}
        self.sent = []

    def start(self, source, target):
        copy = pltpu.make_async_copy(source, target, self.sems.at[self.count])
        self.count += 1
        copy.start()
        return copy

    def __getitem__(self, name):
        for copy in self.loads.pop(name, ()):
            copy.wait()
        return self.refs[name]

    def __setitem__(self, name, value):
        self.refs[name][...] = value
        self.put(name)

    def put(self, name):
        targets = self.targets.pop(name, ())
        for index, target in enumerate(targets):
            source = self.refs[name]
            if len(targets) > 1:
                source = source.at[pl.ds(index * target.shape[0], target.shape[0])]
            self.sent.append(self.start(source, target))

    def finish(self):
        for name in list(self.targets):
            self.put(name)
        for name in list(self.loads):
            self[name]
        for copy in self.sent:
            copy.wait()


TIMES = {
    "forward": 27,
    "expand_grad": 7,
    "reduce_grad": 8,
    "cross_back": 16,
    "self_back": 8,
    "cross_grads": 100,
    "self_grads": 9,
    "add_step": 20,
}
SCALE = 0.02


def cost(name, weight=1.0):
    return pl.CostEstimate(flops=int(TIMES[name] * weight * SCALE * 1.15e9), bytes_accessed=1024, transcendentals=0)


def staged(name, body, loads, direct, outs, scratch):
    arrays = [piece[0] for value in loads.values() for piece in value.pieces]
    arrays += [value for value, unused in direct.values()]
    specs = [ANY] * sum(len(value.pieces) for value in loads.values())
    specs += [space for unused, space in direct.values()]
    buffers = {key: pltpu.VMEM(value.dims, value.dtype) for key, value in loads.items()}
    buffers.update({key: pltpu.VMEM(value.shape, value.dtype) for key, value in outs.items()})
    buffers.update({key: pltpu.VMEM(value.shape, value.dtype) for key, value in scratch.items()})
    results = [part for value in outs.values() for part in parts_of(value)]
    copies = sum(len(value.pieces) for value in loads.values()) + len(results)

    def kernel(*refs):
        refs = list(refs)
        stage = Stage(refs[-1])
        sources = {key: [refs.pop(0) for unused in value.pieces] for key, value in loads.items()}
        for key in direct:
            stage.refs[key] = refs.pop(0)
        for key, value in outs.items():
            stage.targets[key] = [refs.pop(0) for unused in parts_of(value)]
        for key in buffers:
            stage.refs[key] = refs.pop(0)
        for key, value in loads.items():
            stage.loads[key] = []
            for ref, (unused, pick, start) in zip(sources[key], value.pieces):
                source = pick(ref)
                target = stage.refs[key]
                if source.shape != target.shape:
                    target = target.at[pl.ds(start, source.shape[0])]
                stage.loads[key].append(stage.start(source, target))
        body(stage)
        stage.finish()

    values = pl.pallas_call(
        kernel,
        name=name,
        out_shape=results,
        in_specs=specs,
        out_specs=[ANY] * len(results),
        scratch_shapes=[*buffers.values(), pltpu.SemaphoreType.DMA((copies,))],
        compiler_params=pltpu.CompilerParams(vmem_limit_bytes=LIMIT),
        cost_estimate=cost(name),
    )(*arrays)
    values = list(values)
    return {
        key: [values.pop(0) for unused in parts_of(value)] if isinstance(value, Split) else values.pop(0)
        for key, value in outs.items()
    }


def row(ref):
    return ref[...].astype(f32).reshape(1, ref.shape[0])


def lane_heads():
    lane = lax.broadcasted_iota(jnp.int32, (1, LANES), 1)
    return (lane < HEAD_DIM, lane >= HEAD_DIM)


def only(mask, value):
    return jnp.where(mask, value, jnp.zeros_like(value))


def both_heads(heads, value):
    return jnp.concatenate([only(heads[0], value), only(heads[1], value)], axis=0)


def rejoin(heads, value):
    rows = value.shape[0] // 2
    return jnp.where(heads[0], value[:rows], value[rows:])


class Sizes:
    def __init__(self, long_local, short_local, width):
        self.a = long_local
        self.b = short_local
        self.own = long_local + short_local
        self.full = 2 * self.own
        self.width = width
        self.pairs = width // LANES
        self.buckets = ((0, self.a, 0), (self.a, self.b, 2 * self.a))

    def own_pieces(self, long_part, short_part, other_long=None, other_short=None):
        pieces = [(long_part, first, 0), (short_part, first, self.a)]
        if other_long is not None:
            pieces += [(other_long, first, self.own), (other_short, first, self.own + self.a)]
        return pieces

    def full_pieces(self, long_part, short_part, other_long, other_short):
        return [
            (long_part, first, 0),
            (other_long, first, self.a),
            (short_part, first, 2 * self.a),
            (other_short, first, 2 * self.a + self.b),
        ]


def key_positions(rows, core):
    at = lax.broadcasted_iota(jnp.int32, (2 * rows, 1), 0)
    return jnp.where(at < rows, core * rows + at, (1 - core) * rows + at - rows)


def query_positions(rows, core):
    at = lax.broadcasted_iota(jnp.int32, (1, 2 * rows), 1)
    return core * rows + jnp.where(at < rows, at, at - rows)


def softmax_columns(scores):
    raised = jnp.exp(scores - jnp.max(scores, axis=0, keepdims=True))
    return (raised * (1.0 / jnp.sum(raised, axis=0, keepdims=True))).astype(bf16)


def attend(size, q, k, v, bias, probs, out, live):
    heads = lane_heads()
    for start, rows, kstart in size.buckets:
        which = 0 if start == 0 else 1
        weights = []
        for pair in range(size.pairs):
            lanes = slice(pair * LANES, (pair + 1) * LANES)
            queries = both_heads(heads, q[start : start + rows, lanes])
            scores = dot_nt(k[kstart : kstart + 2 * rows, lanes], queries) + bias[which][...]
            weights.append(softmax_columns(scores))
            if rows >= LANES:
                finish_pair(size, v, probs, out, live, which, pair, weights.pop(), heads)
        for pair, value in enumerate(weights):
            finish_pair(size, v, probs, out, live, which, pair, value, heads)


def finish_pair(size, v, probs, out, live, which, pair, weights, heads):
    start, rows, kstart = size.buckets[which]
    lanes = slice(pair * LANES, (pair + 1) * LANES)
    probs[which][pair] = weights
    values = v[kstart : kstart + 2 * rows, lanes]
    context = by_query(heads, weights, values)
    out[start : start + rows, lanes] = jnp.where(live[which], context, 0.0).astype(bf16)


def by_query(heads, across, keyed):
    rows = across.shape[1] // 2
    if rows < LANES:
        return rejoin(heads, dot_tn(across, keyed))
    feature = lax.broadcasted_iota(jnp.int32, (LANES, 1), 0)
    turned = dot(keyed.T, across)
    return jnp.where(feature < HEAD_DIM, turned[:, :rows], turned[:, rows:]).T


def head_sums(product):
    rows = product.shape[0]
    if rows < LANES:
        turned = jnp.concatenate([product, product], axis=0).T
        lane = lax.broadcasted_iota(jnp.int32, (1, LANES), 1)
        low = jnp.sum(turned[:HEAD_DIM], axis=0, keepdims=True)
        high = jnp.sum(turned[HEAD_DIM:], axis=0, keepdims=True)
        return jnp.where(lane < rows, low, high)
    turned = product.T
    low = jnp.sum(turned[:HEAD_DIM], axis=0, keepdims=True)
    high = jnp.sum(turned[HEAD_DIM:], axis=0, keepdims=True)
    return jnp.concatenate([low, high], axis=1)


def attend_back(size, q, k, v, probs, context, grad, dq, dk, dv, scaling):
    heads = lane_heads()
    for which, (start, rows, kstart) in enumerate(size.buckets):
        held = []

        def finish(pair, weights, grads, dscores):
            lanes = slice(pair * LANES, (pair + 1) * LANES)
            at = slice(start, start + rows)
            keys = slice(kstart, kstart + 2 * rows)
            dk[keys, lanes] = dot(dscores, both_heads(heads, q[at, lanes])).astype(bf16)
            dv[keys, lanes] = dot(weights, grads).astype(bf16)
            dq[at, lanes] = (by_query(heads, dscores, k[keys, lanes]) * scaling).astype(bf16)

        for pair in range(size.pairs):
            lanes = slice(pair * LANES, (pair + 1) * LANES)
            at = slice(start, start + rows)
            weights = probs[which][pair]
            grads = grad[at, lanes]
            centred = head_sums(grads.astype(f32) * context[at, lanes].astype(f32))
            grads = both_heads(heads, grads)
            dprobs = dot_nt(v[kstart : kstart + 2 * rows, lanes], grads)
            dscores = (weights.astype(f32) * (dprobs - centred)).astype(bf16)
            if rows >= LANES:
                finish(pair, weights, grads, dscores)
            else:
                held.append((pair, weights, grads, dscores))
        for item in held:
            finish(*item)


def norm_parts(tensor):
    centre = tensor - jnp.mean(tensor, axis=-1, keepdims=True)
    rstd = lax.rsqrt(jnp.mean(centre * centre, axis=-1, keepdims=True) + EPS)
    return centre * rstd, rstd


def norm_back(normed, rstd, gain, gradient):
    scaled = gradient * gain
    inner = scaled - jnp.mean(scaled, axis=-1, keepdims=True)
    inner = inner - normed * jnp.mean(scaled * normed, axis=-1, keepdims=True)
    return inner * rstd


def column_sum(tensor):
    return jnp.sum(tensor.astype(f32), axis=0, keepdims=True)


def live_column(rows, core, length):
    return core * rows + lax.broadcasted_iota(jnp.int32, (rows, 1), 0) < length


def forward_body(size, hidden_width, scaling, g):
    core = lax.axis_index("rep")
    a, b, own, width = size.a, size.b, size.own, size.width
    target_len = (g["target_len_a"][0], g["target_len_b"][0])
    memory_len = (g["memory_len_a"][0], g["memory_len_b"][0])
    live = (live_column(a, core, target_len[0]), live_column(b, core, target_len[1]))
    live_all = jnp.concatenate(live, axis=0)
    bias = (g["bias_a"], g["bias_b"])
    context, mixed, low1 = (columns_of(g["ship3"], at * width, width) for at in range(3))
    low2, inner_send = columns_of(g["ship1"], 0, width), columns_of(g["ship1"], width, hidden_width // 2)
    hidden, ffn_send = columns_of(g["ship2"], 0, hidden_width), columns_of(g["ship2"], hidden_width, width // 2)
    for which, rows in enumerate((a, b)):
        at = key_positions(rows, core)
        allowed = (at < target_len[which]) & (at <= query_positions(rows, core))
        bias[which][...] = jnp.where(allowed, 0.0, MASKED)
    xo = g["xo"]
    g["q"] = ((dot(xo[...], g["w_q"][...]) + row(g["qbias"])).astype(bf16) * scaling).astype(bf16)
    xf = g["xf"]
    g["k"] = dot(xf[...], g["w_k"][...]).astype(bf16)
    g["v"] = (dot(xf[...], g["w_v"][...]) + row(g["vbias"])).astype(bf16)
    attend(size, g["q"], g["k"], g["v"], bias, (g["ps_a"], g["ps_b"]), context, live)
    for name in ("ps_a", "ps_b"):
        g.put(name)
    mf, w_ckv = g["mf"], g["w_ckv"]
    g["ck"] = dot(mf[...], w_ckv[:, :width]).astype(bf16)
    g["cv"] = (dot(mf[...], w_ckv[:, width:]) + row(g["cvbias"])).astype(bf16)

    def squares(tensor):
        kept = jnp.where(live_all, tensor * tensor, 0.0)
        return jnp.sum(jnp.sum(kept, axis=0, keepdims=True), axis=1, keepdims=True)

    branch = g["branch"]
    self_branch = dot(context[...], g["w_out"][...]) + row(g["obias"])
    square_self = squares(self_branch)
    normed, rstd = norm_parts(xo[...].astype(f32) + self_branch)
    g["n1"] = normed
    g["r1"] = rstd
    after_self = normed * row(g["gain1"]) + row(g["shift1"])
    low1[...] = after_self.astype(bf16)
    branch[...] = after_self
    query = dot(low1[...], g["w_cq"][...]) + row(g["cqbias"])
    g["cq"] = (query.astype(bf16) * scaling).astype(bf16)
    for which, rows in enumerate((a, b)):
        allowed = key_positions(rows, core) < memory_len[which]
        bias[which][:, :LANES] = jnp.broadcast_to(jnp.where(allowed, 0.0, MASKED), (2 * rows, LANES))
    bias = tuple(ref.at[:, pl.ds(0, 1)] for ref in bias)
    attend(size, g["cq"], g["ck"], g["cv"], bias, (g["pc_a"], g["pc_b"]), mixed, live)
    for name in ("pc_a", "pc_b", "ship3"):
        g.put(name)
    cross_branch = dot(mixed[...], g["w_cout"][...]) + row(g["cobias"])
    square_cross = squares(cross_branch)
    normed, rstd = norm_parts(branch[...] + cross_branch)
    g["n2"] = normed
    g["r2"] = rstd
    after_cross = normed * row(g["gain2"]) + row(g["shift2"])
    low2[...] = after_cross.astype(bf16)
    branch[...] = after_cross
    third, slope = g["third"], g["slope"]
    w_exp, w_red = g["w_exp"], g["w_red"]
    eb = row(g["ebias"])
    total = None
    for step in range(hidden_width // width):
        cols = slice(step * width, (step + 1) * width)
        act = dot(low2[...], w_exp[:, cols]) + eb[:, cols]
        phi = 0.5 * (1.0 + lax.erf(act * (1.0 / math.sqrt(2.0))))
        hidden[:, cols] = (act * phi).astype(bf16)
        density = jnp.exp(-0.5 * act * act) * (1.0 / math.sqrt(2.0 * math.pi))
        slope[:, cols] = (phi + act * density).astype(bf16)
        part = dot(hidden[:, cols], w_red[cols, :])
        if step == 0:
            third[...] = part
        else:
            third[...] += part
    ffn_branch = third[...] + row(g["rbias"])
    square_ffn = squares(ffn_branch)
    normed, rstd = norm_parts(branch[...] + ffn_branch)
    gain = row(g["gain3"])
    final = normed * gain + row(g["shift3"])
    square_final = squares(final)
    low = final.astype(bf16)
    g["out_a"] = low[:a][None]
    g["out_b"] = low[a:][None]
    gradient = jnp.where(live_all, g["cot"][...].astype(f32), 0.0)
    d_third = norm_back(normed, rstd, gain, gradient)
    g["third"] = d_third
    d_ffn = d_third.astype(bf16)
    dffn = g["dffn"]
    dffn[...] = d_ffn
    half = width // 2
    g["ffn_keep"] = dffn[:, half_of(core, half)]
    ffn_send[...] = dffn[:, half_of(1 - core, half)]
    g.put("ship2")
    sums = g["sums"]
    sums[0:1] = column_sum(gradient * normed)
    sums[1:2] = column_sum(gradient)
    sums[2:3] = column_sum(d_ffn)
    count = jnp.sum(jnp.where(live_all, 1.0, 0.0), axis=0, keepdims=True)
    for at, value in enumerate((square_final, square_self, square_cross, square_ffn, count)):
        sums[3 + at : 4 + at] = jnp.broadcast_to(value, (1, width))
    g.put("sums")
    half = hidden_width // 2
    for side in (1 - core, core):
        for at, start in enumerate(range(0, half, width)):
            cols = pl.ds(pl.multiple_of(side * half + start, LANES), width)
            grad = dot_nt(dffn[...], w_red[cols, :]) * slope[:, cols].astype(f32)
            low = grad.astype(bf16)
            g["inner_sum"][:, cols] = column_sum(low)
            if side is core:
                g["inner_keep%d" % at] = low
            else:
                inner_send[:, pl.ds(start, width)] = low
        g.put("ship1")


def columns_of(ref, start, count):
    return ref.at[:, pl.ds(start, count)]


def half_of(core, half):
    return pl.ds(pl.multiple_of(core * half, LANES), half)


def run_forward(size, hidden_width, scaling, lengths, own, other, cots, weights, vectors):
    a, b, n, t, w, h = size.a, size.b, size.own, size.full, size.width, hidden_width
    w_in, w_out, w_cq, w_ckv, w_cout, w_exp, w_red = weights
    loads = {
        "xo": Load((n, w), bf16, size.own_pieces(own[0], own[1])),
        "w_q": Load((w, w), bf16, [(w_in, columns(0, w), 0)]),
        "xf": Load((t, w), bf16, size.full_pieces(own[0], own[1], other[0], other[1])),
        "w_k": Load((w, w), bf16, [(w_in, columns(w, w), 0)]),
        "w_v": Load((w, w), bf16, [(w_in, columns(2 * w, w), 0)]),
        "mf": Load((t, w), bf16, size.full_pieces(own[2], own[3], other[2], other[3])),
        "w_ckv": load(w_ckv),
        "w_out": load(w_out),
        "w_cq": load(w_cq),
        "w_cout": load(w_cout),
        "w_exp": load(w_exp),
        "w_red": load(w_red),
        "cot": Load((n, w), bf16, size.own_pieces(cots[0], cots[1])),
    }
    names = ("qbias", "vbias", "obias", "gain1", "shift1", "cqbias", "cvbias", "cobias", "gain2", "shift2")
    names += ("ebias", "rbias", "gain3", "shift3")
    direct = dict(zip(("target_len_a", "target_len_b", "memory_len_a", "memory_len_b"), ((v, SMEM) for v in lengths)))
    direct.update(zip(names, ((v, VMEM) for v in vectors)))
    square = shape((n, w), bf16)
    keys = shape((t, w), bf16)
    outs = {
        "out_a": shape((1, a, w), bf16),
        "out_b": shape((1, b, w), bf16),
        "q": square,
        "k": keys,
        "v": keys,
        "cq": square,
        "ck": keys,
        "cv": keys,
        "ps_a": shape((size.pairs, 2 * a, 2 * a), bf16),
        "ps_b": shape((size.pairs, 2 * b, 2 * b), bf16),
        "pc_a": shape((size.pairs, 2 * a, 2 * a), bf16),
        "pc_b": shape((size.pairs, 2 * b, 2 * b), bf16),
        "ship1": shape((n, w + h // 2), bf16),
        "ship2": shape((n, h + w // 2), bf16),
        "ship3": shape((n, 3 * w), bf16),
        "n1": shape((n, w), f32),
        "r1": shape((n, 1), f32),
        "n2": shape((n, w), f32),
        "r2": shape((n, 1), f32),
        "third": shape((n, w), f32),
        "ffn_keep": shape((n, w // 2), bf16),
        "sums": shape((8, w), f32),
        "inner_keep0": square,
        "inner_keep1": square,
        "inner_sum": shape((1, h), f32),
    }
    scratch = {
        "bias_a": shape((2 * a, 2 * a), f32),
        "bias_b": shape((2 * b, 2 * b), f32),
        "branch": shape((n, w), f32),
        "slope": shape((n, h), bf16),
        "dffn": square,
    }
    return staged(
        "forward",
        lambda g: forward_body(size, hidden_width, scaling, g),
        loads,
        direct,
        outs,
        scratch,
    )


def split_partial(size, core, dk, dv, keep, send):
    a, b = size.a, size.b
    moves = ((0, a, a), (a, 0, a), (2 * a, 2 * a + b, b), (2 * a + b, 2 * a, b))
    for here, (stay, leave) in ((0, (dk, dv)), (1, (dv, dk))):

        @pl.when(core == here)
        def unused(stay=stay, leave=leave):
            keep[...] = stay[...]
            for target, source, rows in moves:
                send[pl.ds(target, rows)] = leave[pl.ds(source, rows)]


def through_norm(size, g, gradient, normed, rstd, gain, w_out, sums, back):
    normed = g[normed][...]
    d_sum = norm_back(normed, g[rstd][...], row(g[gain]), gradient)
    sums[0:1] = column_sum(gradient * normed)
    sums[1:2] = column_sum(gradient)
    low = d_sum.astype(bf16)
    sums[2:3] = column_sum(low)
    g["branch"][...] = low
    back[...] = dot_nt(low, g[w_out][...]).astype(bf16)
    return d_sum


def send_halves(core, value, keep, send, at, half):
    keep[:, at * half : (at + 1) * half] = value[:, half_of(core, half)]
    send[:, at * half : (at + 1) * half] = value[:, half_of(1 - core, half)]


def cross_body(size, scaling, parts, g):
    core = lax.axis_index("rep")
    half = size.width // 2
    keep = g["half_keep"]
    send, part_send = g["ship_half"], g["ship_part"]
    sums, sums2 = g["sums"].at[pl.ds(0, 8)], g["sums"].at[pl.ds(8, 8)]
    g["sums"][...] = jnp.zeros_like(g["sums"])
    gradient = g["third"][...]
    for index in range(parts):
        gradient = gradient + dot_nt(g["inner%d" % index][...], g["w_exp%d" % index][...])
    g["mid"][...] = through_norm(size, g, gradient, "n2", "r2", "gain2", "w_cout", sums, g["back"])
    send_halves(core, g["branch"], keep, send, 0, half)
    attend_back(
        size, g["cq"], g["ck"], g["cv"], (g["pc_a"], g["pc_b"]), g["mixed"], g["back"], g["dq"], g["dk"], g["dv"], scaling
    )
    send_halves(core, g["dq"], keep, send, 1, half)
    g.put("ship_half")
    split_partial(size, core, g["dk"], g["dv"], g["part_keep"], part_send)
    g.put("ship_part")
    g.put("part_keep")
    gradient = g["mid"][...] + dot_nt(g["dq"][...], g["w_cq"][...])
    g["low"] = through_norm(size, g, gradient, "n1", "r1", "gain1", "w_out", sums2, g["dcontext"])
    g.put("dcontext")
    keep[:, 2 * half :] = g["branch"][:, half_of(core, half)]
    g["ship_self"] = g["branch"][:, half_of(1 - core, half)]
    g.put("half_keep")
    sums[3:4] = column_sum(g["dq"][...])
    sums[4:5] = column_sum(g["dv"][...])


def run_cross(size, scaling, f, ship3, third, weights, gains):
    n, t, w = size.own, size.full, size.width
    w_exp, w_cout, w_cq, w_out = weights
    loads = {
        "third": load(third),
    }
    parts = w_exp.shape[1] // w

    def column_part(index):
        def pick(ref):
            core = lax.axis_index("rep")
            side = core if index < 2 else 1 - core
            return ref.at[:, pl.ds(pl.multiple_of((2 * side + index % 2) * w, LANES), w)]

        return Load((w, w), bf16, [(w_exp, pick, 0)])

    for index in range(parts):
        source = (f["inner_keep%d" % index], whole, 0) if index < 2 else (f["ship1"], columns((index - 1) * w, w), 0)
        loads["inner%d" % index] = Load((n, w), bf16, [source])
        loads["w_exp%d" % index] = column_part(index)
    loads |= {
        "n2": load(f["n2"]),
        "r2": load(f["r2"]),
        "w_cout": load(w_cout),
        "mixed": Load((n, w), bf16, [(ship3, columns(w, w), 0)]),
        "cv": load(f["cv"]),
        "pc_a": load(f["pc_a"]),
        "cq": load(f["cq"]),
        "ck": load(f["ck"]),
        "pc_b": load(f["pc_b"]),
        "w_cq": load(w_cq),
        "n1": load(f["n1"]),
        "r1": load(f["r1"]),
        "w_out": load(w_out),
    }
    square = shape((n, w), bf16)
    keys = shape((t, w), bf16)
    return staged(
        "cross_back",
        lambda g: cross_body(size, scaling, parts, g),
        loads,
        {"gain2": (gains[0], VMEM), "gain1": (gains[1], VMEM)},
        {
            "low": shape((n, w), f32),
            "dcontext": square,
            "half_keep": shape((n, 3 * (w // 2)), bf16),
            "ship_half": square,
            "ship_self": shape((n, w // 2), bf16),
            "part_keep": keys,
            "ship_part": Split((t, w), bf16, PIECES),
            "sums": shape((16, w), f32),
        },
        {"branch": square, "back": square, "dq": square, "dk": keys, "dv": keys, "mid": shape((n, w), f32)},
    )


def self_body(size, scaling, g):
    core = lax.axis_index("rep")
    half = size.width // 2
    send, part_send = g["ship_half"], g["ship_part"]
    sums = g["sums"]
    sums[...] = jnp.zeros_like(sums)
    attend_back(
        size, g["q"], g["k"], g["v"], (g["ps_a"], g["ps_b"]), g["context"], g["dcontext"], g["dq"], g["dk"], g["dv"], scaling
    )
    g.put("dq")
    split_partial(size, core, g["dk"], g["dv"], g["part_keep"], part_send)
    g.put("ship_part")
    send_halves(core, g["dq"], g["half_keep"], send, 0, half)
    g.put("ship_half")
    g.put("part_keep")
    g.put("half_keep")
    sums[0:1] = column_sum(g["dq"][...])
    sums[1:2] = column_sum(g["dv"][...])


def run_self(size, scaling, f, ship3, dcontext):
    n, t, w = size.own, size.full, size.width
    loads = {
        "dcontext": load(dcontext),
        "context": Load((n, w), bf16, [(ship3, columns(0, w), 0)]),
        "v": load(f["v"]),
        "ps_a": load(f["ps_a"]),
        "q": load(f["q"]),
        "k": load(f["k"]),
        "ps_b": load(f["ps_b"]),
    }
    square = shape((n, w), bf16)
    keys = shape((t, w), bf16)
    return staged(
        "self_back",
        lambda g: self_body(size, scaling, g),
        loads,
        {},
        {
            "dq": square,
            "half_keep": shape((n, w // 2), bf16),
            "ship_half": Split((n, w // 2), bf16, 1),
            "part_keep": keys,
            "ship_part": Split((t, w), bf16, PIECES),
            "sums": shape((8, w), f32),
        },
        {"dk": keys, "dv": keys},
    )


PIECES = 2
BLOCKS = 16
STAGES = 4
ORDER_XZY = (0, 2, 3, 1)
ORDER_YXZ = (1, 0, 2, 3)
ORDER_ZXY = (2, 3, 0, 1)


class Scatter:
    def __init__(self, order, me, keep, send, rows):
        self.order = order
        self.me = me
        self.keep = keep
        self.send = send
        self.rows = rows

    def store(self, block, value, start, count):
        distance = self.me ^ block
        place = 0
        for stage, bit in enumerate(self.order):
            place = place + (((distance >> bit) & 1) << (STAGES - 1 - stage))
        low = place < BLOCKS // 2
        at = pl.multiple_of(jnp.where(low, place, place - BLOCKS // 2) * self.rows, 16)
        rows = pl.ds(at, self.rows)
        cols = slice(start, start + count)

        @pl.when(low)
        def unused():
            self.keep[rows, cols] = value.astype(bf16)

        @pl.when(jnp.logical_not(low))
        def unused_too():
            self.send[rows, cols] = value.astype(bf16)

    def store_all(self, product, start):
        for block in range(BLOCKS):
            self.store(block, product[block * self.rows : (block + 1) * self.rows], start, product.shape[1])


def my_block(group):
    return lax.axis_index("tok") // group


def chunk_outs(size, columns, names):
    rows = size.width // 2
    return {name: shape((rows, columns), bf16) for name in names}


def expand_body(size, group, g):
    scatter = Scatter(ORDER_XZY, my_block(group), g["keep"], g["send"], size.width // BLOCKS)
    for at in range(2):
        scatter.store_all(dot_tn(g["low"][...], g["d%d" % at][...]), at * size.width)
    g.put("send")


def run_expand_grad(size, group, ship, ship_other, keeps):
    n, t, w = size.own, size.full, size.width
    loads = {"low": Load((t, w), bf16, [(ship, columns(0, w), 0), (ship_other, columns(0, w), n)])}
    for at, keep in enumerate(keeps):
        loads["d%d" % at] = Load((t, w), bf16, [(keep, whole, 0), (ship_other, columns(w + at * w, w), n)])
    return staged(
        "expand_grad",
        lambda g: expand_body(size, group, g),
        loads,
        {},
        chunk_outs(size, 2 * w, ("keep", "send")),
        {},
    )


def reduce_chunk(group, index):
    return (my_block(group) >> 2) ^ (1, 3, 0, 2)[index]


def reduce_body(size, group, g):
    count = size.width // BLOCKS
    half = size.width // 2
    parts = BLOCKS // 4
    mine = my_block(group) & 3
    for index in range(4):
        target = g["send"] if index < 2 else g["keep"]
        product = dot_tn(g["hidden%d" % index][...], g["d"][...])
        for block in range(4):
            distance = mine ^ block
            place = (index % 2) * 4 + ((distance & 1) << 1) + (distance >> 1)
            at = pl.ds(pl.multiple_of(place * count, 16), count)
            for part in range(parts):
                start = (block * parts + part) * count
                target[at, part * half : (part + 1) * half] = product[start : start + count].astype(bf16)
        if index % 2 == 1:
            g.put("send" if index < 2 else "keep")


def run_reduce_grad(size, group, ship, ship_other, keep):
    n, t, w = size.own, size.full, size.width
    half = keep.shape[1]
    h = ship.shape[1] - half
    quarter = h // 4

    def chunk(index):
        def pick(ref):
            return ref.at[:, pl.ds(pl.multiple_of(reduce_chunk(group, index) * quarter, LANES), quarter)]

        return Load((t, quarter), bf16, [(ship, pick, 0), (ship_other, pick, n)])

    loads = {"d": Load((t, half), bf16, [(keep, whole, 0), (ship_other, columns(h, half), n)])}
    loads.update({"hidden%d" % index: chunk(index) for index in range(4)})
    return staged(
        "reduce_grad",
        lambda g: reduce_body(size, group, g),
        loads,
        {},
        chunk_outs(size, h // 2, ("send", "keep")),
        {},
    )


def projection_share(size, g, scatter):
    a, b = size.a, size.b
    total = g["total"]
    total[...] = (g["part_keep"][...].astype(f32) + g["part_recv"][...].astype(f32)).astype(bf16)
    scatter.store_all(dot_tn(g["source"][...], total[...]), 0)
    g.put("send")
    share = dot_nt(total[...], g["weight"][...])
    g["grad_send"][pl.ds(0, a)] = share[a : 2 * a].astype(bf16)
    g["grad_send"][pl.ds(a, b)] = share[2 * a + b :].astype(bf16)
    g["grad_own"][pl.ds(0, a)] = share[:a]
    g["grad_own"][pl.ds(a, b)] = share[2 * a : 2 * a + b]


def cross_grad_body(size, group, g):
    width = size.width
    half = width // 2
    scatter = Scatter(ORDER_YXZ, my_block(group), g["keep"], g["send"], width // BLOCKS)
    for at, name in enumerate(("mixed", "low1")):
        cols = slice(at * half, (at + 1) * half)
        scatter.store_all(dot_tn(g[name][...], g["halves"][:, cols]), width + at * half)
    scatter.store_all(dot_tn(g["context"][...], g["halves_self"][...]), 2 * width)
    projection_share(size, g, scatter)
    g.put("keep")
    g.put("grad_send")


def stacked(arrays, start):
    return [(array, whole, start + index * array.shape[0]) for index, array in enumerate(arrays)]


def my_columns(weight, width):
    skip = weight.shape[1] - 2 * width

    def pick(ref):
        return ref.at[:, pl.ds(pl.multiple_of(skip + lax.axis_index("rep") * width, LANES), width)]

    return Load((width, width), bf16, [(weight, pick, 0)])


def run_cross_grads(size, group, ship3, ship3_other, half_keep, half_recv, part_keep, part_recv, sources, weight):
    n, t, w = size.own, size.full, size.width

    def both(at):
        return Load((t, w), bf16, [(ship3, columns(at * w, w), 0), (ship3_other, columns(at * w, w), n)])

    half = w // 2
    outs = chunk_outs(size, w + 3 * half, ("keep", "send"))
    outs["grad_own"] = shape((n, w), f32)
    outs["grad_send"] = shape((n, w), bf16)
    return staged(
        "cross_grads",
        lambda g: cross_grad_body(size, group, g),
        {
            "mixed": both(1),
            "halves": Load((t, 2 * half), bf16, [(half_keep, columns(0, 2 * half), 0), (half_recv[0], whole, n)]),
            "low1": both(2),
            "context": both(0),
            "halves_self": Load((t, half), bf16, [(half_keep, columns(2 * half, half), 0), (half_recv[1], whole, n)]),
            "part_keep": load(part_keep),
            "part_recv": Load((t, w), bf16, stacked(part_recv, 0)),
            "source": Load((t, w), bf16, size.full_pieces(*sources)),
            "weight": my_columns(weight, w),
        },
        {},
        outs,
        {"total": shape((t, w), bf16)},
    )


def regroup(value, width, count):
    parts = value.shape[1] // width
    lane = lax.broadcasted_iota(jnp.int32, (1, width), 1)
    rows_out = [jnp.zeros((1, width), f32)] * parts
    for step in range(parts):
        piece = value[:, step * width : (step + 1) * width]
        for at in range(width // count):
            device, part = divmod(step * (width // count) + at, parts)
            moved = pltpu.roll(piece, ((device - at) * count) % width, 1)
            mine = (lane >= device * count) & (lane < (device + 1) * count)
            rows_out[part] = jnp.where(mine, moved, rows_out[part])
    return jnp.concatenate(rows_out, axis=0)


def self_grad_body(size, group, sums, g):
    width = size.width
    half = width // 2
    count = width // BLOCKS
    scatter = Scatter(ORDER_YXZ, my_block(group), g["keep"], g["send"], count)
    held = g["rows"]
    held[...] = jnp.zeros_like(held)
    at = 0
    for name in sums:
        value = g[name][...]
        if value.shape[1] > width:
            value = regroup(value, width, count)
        held[pl.ds(at, value.shape[0])] = value
        at += value.shape[0]
    scatter.store_all(jnp.transpose(held[...]), width + half)
    scatter.store_all(dot_tn(g["lhs"][...], g["halves"][...]), width)
    projection_share(size, g, scatter)
    g.put("keep")
    g.put("grad_send")
    g["grad_own"][...] += g["low"][...] + dot_nt(g["dq"][...], g["w_q"][...])


def run_self_grads(size, group, half_keep, half_recv, part_keep, part_recv, sources, weight, low, dq, sums):
    n, t, w = size.own, size.full, size.width
    half = w // 2
    loads = {key: load(value) for key, value in sums.items()}
    loads.update(
        part_keep=load(part_keep),
        part_recv=Load((t, w), bf16, stacked(part_recv, 0)),
        source=Load((t, w), bf16, size.full_pieces(*sources)),
        weight=my_columns(weight, w),
        lhs=Load((t, w), bf16, size.own_pieces(*sources)),
        halves=Load((t, half), bf16, [(half_keep, whole, 0), *stacked(half_recv, n)]),
        dq=load(dq),
        w_q=Load((w, w), bf16, [(weight, columns(0, w), 0)]),
        low=load(low),
    )
    outs = chunk_outs(size, w + half + LANES, ("keep", "send"))
    outs["grad_own"] = shape((n, w), f32)
    outs["grad_send"] = shape((n, w), bf16)
    return staged(
        "self_grads",
        lambda g: self_grad_body(size, group, tuple(sums), g),
        loads,
        {},
        outs,
        {"total": shape((t, w), bf16), "rows": shape((LANES, w), f32)},
    )


def swap(value):
    return lax.ppermute(value, "rep", [(0, 1), (1, 0)])


class Line:
    def __init__(self):
        self.last = None

    def wait(self, *values):
        if self.last is None:
            return values
        return lax.optimization_barrier((*values, self.last))[:-1]

    def record(self, value):
        self.last = value


def add_step(pairs, weight=1.0):
    rows = pairs[0][0].shape[0] // 2
    columns = sum(keep.shape[1] for keep, unused in pairs)

    def kernel(*refs):
        keep_out, send_out = refs[-2:]
        at = 0
        for index in range(len(pairs)):
            keep, received = refs[2 * index], refs[2 * index + 1]
            cols = slice(at, at + keep.shape[1])
            at += keep.shape[1]
            total = (keep[...].astype(f32) + received[...].astype(f32)).astype(bf16)
            keep_out[:, cols] = total[:rows]
            send_out[:, cols] = total[rows:]

    flat = [value for pair in pairs for value in pair]
    return pl.pallas_call(
        kernel,
        name="add_step",
        out_shape=[shape((rows, columns), bf16)] * 2,
        in_specs=[VMEM] * len(flat),
        out_specs=[VMEM] * 2,
        compiler_params=pltpu.CompilerParams(vmem_limit_bytes=ADD_LIMIT),
        cost_estimate=cost("add_step", weight),
    )(*flat)


def add_last(keep, received, weight=1.0):
    def kernel(keep, received, out):
        out[...] = (keep[...].astype(f32) + received[...].astype(f32)).astype(bf16)

    return pl.pallas_call(
        kernel,
        name="add_last",
        out_shape=shape(keep.shape, bf16),
        in_specs=[VMEM] * 2,
        out_specs=VMEM,
        compiler_params=pltpu.CompilerParams(vmem_limit_bytes=ADD_LIMIT),
        cost_estimate=cost("add_step", weight),
    )(keep, received)


class Chunk:
    def __init__(self, keep, send, order, group, stage=0):
        self.keep = keep
        self.order = order
        self.group = group
        self.stage = stage
        self.begin(send)

    def begin(self, send):
        devices = lax.axis_size("tok")
        bit = self.group << self.order[self.stage]
        self.received = lax.ppermute(send, "tok", [(i, i ^ bit) for i in range(devices)])

    def launch(self, line):
        (send,) = line.wait(self.send)
        self.begin(send)

    def step(self, line, weight=1.0):
        self.absorb(line, weight)
        if self.stage < STAGES:
            self.begin(self.send)

    def absorb(self, line, weight=1.0):
        keep, received = line.wait(self.keep, self.received)
        self.stage += 1
        if self.stage == STAGES:
            self.total = add_last(keep, received, weight)
            line.record(self.total)
            return
        self.keep, self.send = add_step([(keep, received)], weight)
        line.record(self.keep)


def spread(total, group):
    if group == 1:
        return total
    devices = lax.axis_size("tok")
    sets = [[start + i for i in range(group)] for start in range(0, devices, group)]
    total = lax.psum_scatter(total.astype(f32), "tok", scatter_dimension=0, tiled=True, axis_index_groups=sets)
    return total.astype(bf16)


def spread_blocks(total, group, parts):
    if group == 1:
        return total
    wide = total.shape[1] // parts
    rows_in = jnp.concatenate([total[:, at * wide : (at + 1) * wide] for at in range(parts)], axis=0)
    rows_in = spread(rows_in, group)
    count = rows_in.shape[0] // parts
    return jnp.concatenate([rows_in[at * count : (at + 1) * count] for at in range(parts)], axis=1)


def merge(line, *chunks):
    values = line.wait(*[value for chunk in chunks for value in (chunk.keep, chunk.received)])
    keep, send = add_step(list(zip(values[::2], values[1::2])))
    line.record(keep)
    return Chunk(keep, send, chunks[0].order, chunks[0].group, chunks[0].stage + 1)


def add_tokens(size, *values):
    a, b, w = size.a, size.b, size.width

    def kernel(*refs):
        for at in range(2):
            own, received = refs[2 * at : 2 * at + 2]
            long_out, short_out = refs[4 + 2 * at : 6 + 2 * at]
            long_out[0] = (own[:a] + received[:a].astype(f32)).astype(bf16)
            short_out[0] = (own[a:] + received[a:].astype(f32)).astype(bf16)

    outs = pl.pallas_call(
        kernel,
        name="add_tokens",
        out_shape=[shape((1, a, w), bf16), shape((1, b, w), bf16)] * 2,
        in_specs=[VMEM] * 4,
        out_specs=[VMEM] * 4,
        compiler_params=pltpu.CompilerParams(vmem_limit_bytes=ADD_LIMIT),
        cost_estimate=cost("add_step", 0.0),
    )(*values)
    return outs[:2], outs[2:]


SMALL_ROWS = (24, 25, 18, 16, 17, 11, 12, 10, 8, 9, 2, 0, 1)


def finish_small(mine, theirs, width, start):
    rows_out = mine.shape[0]
    outs = [shape((rows_out,), f32)] * len(SMALL_ROWS) + [shape((4 * rows_out,), f32), shape((4,), f32)]

    def kernel(mine, theirs, *refs):
        cols = slice(start, start + LANES)
        total = mine[:, cols].astype(f32) + theirs[:, cols].astype(f32)
        turned = total.T
        for ref, at in zip(refs, SMALL_ROWS):
            ref[...] = turned[at : at + 1].reshape(rows_out)
        refs[-2][...] = jnp.concatenate([turned[at : at + 1] for at in range(32, 36)], axis=1).reshape(4 * rows_out)
        line = total[0:1]
        refs[-1][...] = jnp.sqrt(line[:, 3:7] / (line[:, 7:8] * width)).reshape(4)

    return pl.pallas_call(
        kernel,
        name="finish_small",
        out_shape=outs,
        in_specs=[VMEM] * 2,
        out_specs=[VMEM] * len(outs),
        compiler_params=pltpu.CompilerParams(vmem_limit_bytes=ADD_LIMIT),
        cost_estimate=cost("add_step"),
    )(mine, theirs)


def finish(pairs, dims, moves):
    outs = [shape(value, f32) for value in dims]

    def kernel(*refs):
        core = lax.axis_index("rep")
        for pair, out, start, count, row_at, column in moves:
            mine, theirs = refs[2 * pair], refs[2 * pair + 1]
            target = refs[len(pairs) + out]
            at = slice(row_at, row_at + mine.shape[0])
            cols = slice(start, start + count)
            if column is None:
                target[at, :] = mine[:, cols].astype(f32) + theirs[:, cols].astype(f32)
                continue
            for ref, side in ((mine, core), (theirs, 1 - core)):
                target[at, pl.ds(pl.multiple_of(column + side * count, LANES), count)] = ref[:, cols].astype(f32)

    return pl.pallas_call(
        kernel,
        name="finish",
        out_shape=outs,
        in_specs=[VMEM] * len(pairs),
        out_specs=[VMEM] * len(outs),
        compiler_params=pltpu.CompilerParams(vmem_limit_bytes=ADD_LIMIT),
        cost_estimate=cost("add_step"),
    )(*pairs)


def per_device(*args):
    (
        long_target,
        short_target,
        long_memory,
        short_memory,
        long_cot,
        short_cot,
        long_target_len,
        short_target_len,
        long_memory_len,
        short_memory_len,
        self_inproj,
        self_qbias,
        self_vbias,
        self_outproj,
        self_obias,
        first_gain,
        first_shift,
        cross_qproj,
        cross_qbias,
        cross_kvproj,
        cross_vbias,
        cross_outproj,
        cross_obias,
        second_gain,
        second_shift,
        expand_weight,
        expand_bias,
        reduce_weight,
        reduce_bias,
        final_gain,
        final_shift,
    ) = args
    core = lax.axis_index("rep")
    devices = lax.axis_size("tok")
    group = devices // BLOCKS
    width = long_target.shape[2]
    hidden_width = expand_weight.shape[1]
    size = Sizes(long_target.shape[1], short_target.shape[1], width)
    n = size.own
    scaling = 1.0 / math.sqrt(HEAD_DIM)
    own = (long_target, short_target, long_memory, short_memory)
    other = tuple(swap(value) for value in own)
    f = run_forward(
        size,
        hidden_width,
        scaling,
        (long_target_len, short_target_len, long_memory_len, short_memory_len),
        own,
        other,
        (long_cot, short_cot),
        (self_inproj, self_outproj, cross_qproj, cross_kvproj, cross_outproj, expand_weight, reduce_weight),
        (
            self_qbias,
            self_vbias,
            self_obias,
            first_gain,
            first_shift,
            cross_qbias,
            cross_vbias,
            cross_obias,
            second_gain,
            second_shift,
            expand_bias,
            reduce_bias,
            final_gain,
            final_shift,
        ),
    )
    line = Line()
    ship1_other = swap(f["ship1"])
    ship2_other = swap(f["ship2"])
    ship3 = f["ship3"]
    ship3_other = swap(ship3)
    c = run_cross(
        size,
        scaling,
        f,
        ship3,
        f["third"],
        (expand_weight, cross_outproj, cross_qproj, self_outproj),
        (second_gain, first_gain),
    )
    line.record(c["low"])
    chalf_other = (swap(c["ship_half"]), swap(c["ship_self"]))
    cpart_other = [swap(value) for value in c["ship_part"]]
    (ffn_keep,) = line.wait(f["ffn_keep"])
    r = run_reduce_grad(size, group, f["ship2"], ship2_other, ffn_keep)
    c1 = Chunk(r["keep"], r["send"], ORDER_ZXY, group)
    line.record(r["keep"])
    (chalf_keep,) = line.wait(c["half_keep"])
    m = run_cross_grads(
        size,
        group,
        ship3,
        ship3_other,
        chalf_keep,
        chalf_other,
        c["part_keep"],
        cpart_other,
        (long_memory, short_memory, other[2], other[3]),
        cross_kvproj,
    )
    c3 = Chunk(m["keep"], m["send"], ORDER_YXZ, group)
    line.record(m["keep"])
    (inner_keep0,) = line.wait(f["inner_keep0"])
    e = run_expand_grad(size, group, f["ship1"], ship1_other, (inner_keep0, f["inner_keep1"]))
    c2 = Chunk(e["keep"], e["send"], ORDER_XZY, group)
    line.record(e["keep"])
    (dcontext,) = line.wait(c["dcontext"])
    b = run_self(size, scaling, f, ship3, dcontext)
    line.record(b["dq"])
    shalf_other = [swap(value) for value in b["ship_half"]]
    spart_other = [swap(value) for value in b["ship_part"]]
    c1.step(line, 0.0)
    (shalf_keep,) = line.wait(b["half_keep"])
    if group == 1:
        expand_rows = f["inner_sum"]
    else:
        expand_rows = f["inner_sum"].reshape(devices, 4, width // devices).transpose(1, 0, 2).reshape(4, width)
    t = run_self_grads(
        size,
        group,
        shalf_keep,
        shalf_other,
        b["part_keep"],
        spart_other,
        (long_target, short_target, other[0], other[1]),
        self_inproj,
        c["low"],
        b["dq"],
        {"sums0": f["sums"], "sums1": c["sums"], "sums2": b["sums"], "sums3": expand_rows},
    )
    c5 = Chunk(t["keep"], t["send"], ORDER_YXZ, group)
    line.record(t["keep"])
    c3.step(line, 0.0)
    c2.step(line, 0.0)
    c1.step(line, 12.0)
    memory_recv, target_recv = (swap(value) for value in line.wait(m["grad_send"], t["grad_send"]))
    for chunk in (c5, c3, c2):
        chunk.step(line)
    memory_grads, target_grads = add_tokens(
        size, *line.wait(m["grad_own"], memory_recv, t["grad_own"], target_recv)
    )
    line.record(target_grads[0])
    for chunk in (c1, c5, c3, c2, c1):
        chunk.step(line)
    reduce_mine = spread_blocks(c1.total, group, hidden_width // width)
    reduce_theirs = swap(reduce_mine)
    c5.step(line)
    c3.step(line, 0.5)
    cross_mine = spread(c3.total, group)
    cross_theirs = swap(cross_mine)
    c2.step(line, 0.5)
    expand_mine = spread(c2.total, group)
    expand_theirs = swap(expand_mine)
    c5.step(line, 4.0)
    self_mine = spread(c5.total, group)
    self_theirs = swap(self_mine)
    half = width // 2
    half_h = hidden_width // 2
    parts = hidden_width // width
    reduce_theirs, expand_theirs, cross_theirs = line.wait(reduce_theirs, expand_theirs, cross_theirs)
    rows_out = reduce_mine.shape[0]
    grad_reduce, grad_expand = finish(
        (reduce_mine, reduce_theirs, expand_mine, expand_theirs),
        ((parts * rows_out, width), (rows_out, hidden_width)),
        [(0, 0, at * half, half, at * rows_out, 0) for at in range(parts)] + [(1, 1, 0, half_h, 0, 0)],
    )
    grad_cross_kv, grad_cross_out, grad_cross_q, grad_self_out = finish(
        (cross_mine, cross_theirs),
        ((rows_out, 2 * width), (rows_out, width), (rows_out, width), (rows_out, width)),
        [
            (0, 0, 0, width, 0, 0),
            (0, 1, width, half, 0, 0),
            (0, 2, width + half, half, 0, 0),
            (0, 3, 2 * width, half, 0, 0),
        ],
    )
    grad_self_in, small = finish(
        (self_mine, self_theirs),
        ((rows_out, 3 * width), (rows_out, LANES)),
        [(0, 0, width, half, 0, 0), (0, 0, 0, width, 0, width), (0, 1, width + half, LANES, 0, None)],
    )
    if group == 1:
        *vectors, expand_bias_rows, statistics = finish_small(self_mine, self_theirs, width, width + half)
    else:
        small = small.T
        vectors = [small[at] for at in SMALL_ROWS]
        expand_bias_rows = small[32:36]
        statistics = jnp.sqrt(small[3:7, 0] / (small[7, 0] * width))
    grad_expand_bias = expand_bias_rows.reshape(-1)
    return (
        f["out_a"],
        f["out_b"],
        *target_grads,
        *memory_grads,
        grad_self_in,
        vectors[0],
        vectors[1],
        grad_self_out,
        vectors[2],
        vectors[3],
        vectors[4],
        grad_cross_q,
        vectors[5],
        grad_cross_kv,
        vectors[6],
        grad_cross_out,
        vectors[7],
        vectors[8],
        vectors[9],
        grad_expand,
        grad_expand_bias,
        grad_reduce,
        vectors[10],
        vectors[11],
        vectors[12],
        statistics,
    )


def solution(mesh):
    split = P("tok", "rep", None)
    in_specs = (split,) * 6 + (P("tok"),) * 4 + (P(),) * 21
    out_specs = (split,) * 6 + (
        P("tok", None),
        P("tok"),
        P("tok"),
        P("tok", None),
        P("tok"),
        P("tok"),
        P("tok"),
        P("tok", None),
        P("tok"),
        P("tok", None),
        P("tok"),
        P("tok", None),
        P("tok"),
        P("tok"),
        P("tok"),
        P("tok", None),
        P("tok"),
        P("tok", None),
        P("tok"),
        P("tok"),
        P("tok"),
        P(),
    )
    return jax.shard_map(per_device, mesh=mesh, in_specs=in_specs, out_specs=out_specs, check_vma=False)
```
